32 devices in a mesh: grp: 2 (over y), trade: 4 (over z), date: 2 (over x), path: 2 (over core).
Axes of the slice: x: 2, y: 2, z: 4, core: 2. Of those that a mesh axis runs over, the one named last changes fastest.
Arguments:
- driver_increments: float32 [16, 256, 128], P(('grp', 'date'), 'path'), parts along dimension 0, may hold values from -4 to 4
- persistence_ratio: float32 [16, 128], P(('grp', 'date')), parts along dimension 0, may hold values from 0 to 1, as said below
- deal_sensitivity: bfloat16 [128, 65536], P(None, ('grp', 'trade')), parts along dimension 1, may hold values from -0.5 to 0.5
- signed_notional: float32 [65536], P(('grp', 'trade')), parts along dimension 0, may hold values from -0.4 to 0.4
- batch_obligor: int32 [512], P(('grp', 'trade')), parts along dimension 0, may hold values from 0 to 127, as said below
- collateral_ceiling: float32 [256], P(('grp', 'trade')), parts along dimension 0, may hold values from -1 to 1
- default_discount_mass: float32 [16, 128], P(('grp', 'date'), 'trade'), parts along dimension 0, may hold values from 0.1 to 1
Outputs:
- exposure_profile: float32 [16, 128], P(('grp', 'date'), 'trade'), parts along dimension 0
- shock_gradient: float32 [16, 256, 128], P(('grp', 'date'), 'path'), parts along dimension 0
The draws below stay inside these ranges and needn't reach their ends.
There are 2 independent parts, one for each index of `grp`. The reference program is written for one: setup_inputs(seed, part) draws one part's arguments, and reference() takes and returns one part's arrays. A program takes and returns all parts, laid end to end along the dimension named above; each array names one. Nothing has to cross between parts.
Inputs may be any that keep to these rules, and one draw needn't show every extreme that they name: `persistence_ratio`: strictly between 0 and 1. `batch_obligor`: counterparty c belongs to trade shard c // 32. Of the 64 trade blocks of one trade shard, at most 32 have counterparties on any one trade shard, and in every trade shard some counterparty shard receives exactly 32 of them.
All inputs are finite; a program needn't handle non-finite values.
Results may differ from the reference program's by a relative error of at most 0.0019.
Values sent between devices are 32-bit elements; how exact they have to be, the bound alone decides.
No kernel may reach another device: no remote copies, remote signals or barrier semaphores. Data moves between devices by JAX's collectives and lax.ppermute only.
A program may use at most 64 MiB of HBM per device.

```python
import math
import jax
import jax.numpy as jnp
from jax import lax

STATE_DRIVERS = 128
CP_DEV = 32
TB_DEV = 64
CAP = 32
EXPOSURE_DATES = 8
PATHS = 256
DEAL_COUNT = 32768
CPTY = 128
TRADE_BLOCKS = 256


def draw_persistence_ratio(key, part):
    base_start = jax.random.fold_in(key, 11)
    hazard_key, roughness_key, dates_key, spike_key = jax.random.split(base_start, 4)
    lower = math.log(0.2 / EXPOSURE_DATES)
    upper = math.log(1.5)
    rate_factor = jnp.exp(jax.random.uniform(hazard_key, (STATE_DRIVERS,), jnp.float32, lower, upper))
    roughness = jax.random.uniform(roughness_key, (EXPOSURE_DATES, STATE_DRIVERS), jnp.float32, 0.6, 1.4)
    retained_flag = jnp.exp(-rate_factor[None, :] * roughness)
    spike_dates = jax.random.randint(dates_key, (2,), 0, EXPOSURE_DATES)
    spike_flag = jnp.any(jnp.arange(EXPOSURE_DATES)[:, None] == spike_dates[None, :], axis=1)
    spike_loss = jax.random.uniform(spike_key, (EXPOSURE_DATES, STATE_DRIVERS), jnp.float32, 0.5, 0.8)
    return jnp.where(spike_flag[:, None], retained_flag * spike_loss, retained_flag).astype(jnp.float32)


def draw_batch_obligor(key, part):
    shard_total = TRADE_BLOCKS // TB_DEV
    slot_total = shard_total * CAP

    def draw_shard(shard_index):
        shard_key = jax.random.fold_in(jax.random.fold_in(key, 23), shard_index)
        key_rank, key_full, key_local, key_order = jax.random.split(shard_key, 4)
        ranking = jax.random.permutation(key_rank, slot_total).astype(jnp.int32)
        full_shard = jax.random.randint(key_full, (), 0, shard_total)
        slot_owner = jnp.arange(slot_total, dtype=jnp.int32) // CAP
        scoring = jnp.where(slot_owner == full_shard, ranking - slot_total, ranking)
        chosen = jnp.argsort(scoring)[:TB_DEV].astype(jnp.int32)
        chosen = chosen[jax.random.permutation(key_order, TB_DEV)]
        local_pick = jax.random.randint(key_local, (TB_DEV,), 0, CP_DEV)
        return chosen // CAP * CP_DEV + local_pick
    return jax.vmap(draw_shard)(jnp.arange(shard_total)).reshape(-1).astype(jnp.int32)


def level_of(key, dims, cuts, low, top_value):
    factor_of, own = 1.0, jax.random.fold_in(key, 6)
    for position, shards_of in cuts:
        draws = jnp.exp(jax.random.uniform(jax.random.fold_in(own, position), (shards_of,), jnp.float32, low / len(cuts), top_value / len(cuts)))
        factor_of = factor_of * jnp.repeat(draws, dims[position] // shards_of).reshape([-1 if axis == position else 1 for axis in range(len(dims))])
    return factor_of


def centred(stream_key, extent, deviation, bound, cuts=(), kind=jnp.bfloat16):
    gain = level_of(stream_key, extent, cuts, -0.22, 0.18) if cuts else 1.0
    array = jax.random.normal(stream_key, extent, jnp.float32) * deviation * gain
    return jnp.minimum(jnp.maximum(array, -bound), bound).astype(kind)


def setup_inputs(seed: int = 0, part: int = 0) -> dict:
    streams_of = jax.random.split(jax.random.key(seed), 8)
    part_keys = jax.random.split(jax.random.fold_in(streams_of[7], part), 8)
    return {
        "driver_increments": centred(part_keys[0], (EXPOSURE_DATES, PATHS, STATE_DRIVERS), 0.5, 4.0, ((0, 2), (1, 2)), jnp.float32),
        "persistence_ratio": draw_persistence_ratio(jax.random.fold_in(jax.random.fold_in(streams_of[7], part), 71), part),
        "deal_sensitivity": centred(part_keys[2], (STATE_DRIVERS, DEAL_COUNT), STATE_DRIVERS ** -0.5, 0.5, ((1, 4),)),
        "signed_notional": centred(part_keys[3], (DEAL_COUNT,), 0.0625, 0.4, ((0, 4),), jnp.float32),
        "batch_obligor": draw_batch_obligor(jax.random.fold_in(jax.random.fold_in(streams_of[7], part), 71), part),
        "collateral_ceiling": jnp.clip(jax.random.uniform(part_keys[5], (CPTY,), jnp.float32, -1.0, 1.0) * level_of(part_keys[5], (CPTY,), ((0, 4),), -0.4, 0.0), -1.0, 1.0),
        "default_discount_mass": jnp.clip(jnp.exp(math.log(1.0) - 2.3025851 * jax.random.uniform(part_keys[6], (EXPOSURE_DATES, CPTY), jnp.float32) ** level_of(part_keys[6], (EXPOSURE_DATES, CPTY), ((0, 2), (1, 4)), -0.2, 0.2)), 0.1, 1.0),
    }


block_width = 128
cluster_extent = 512
highest = lax.Precision.HIGHEST


def reference(driver_increments, persistence_ratio, deal_sensitivity, signed_notional, batch_obligor, collateral_ceiling, default_discount_mass):
    def advance(state_now, inputs):
        retain, shock_now = inputs
        state_now = retain[None, :] * state_now + shock_now
        return state_now, state_now

    _, states = lax.scan(advance, jnp.zeros((PATHS, STATE_DRIVERS), jnp.float32), (persistence_ratio, driver_increments))
    row_count = EXPOSURE_DATES * PATHS
    state_bf = states.reshape(row_count, STATE_DRIVERS).astype(jnp.bfloat16)
    cluster_ordinal = DEAL_COUNT // cluster_extent
    per_group = cluster_extent // block_width
    sensitivity_clusters = deal_sensitivity.reshape(STATE_DRIVERS, cluster_ordinal, cluster_extent).transpose(1, 0, 2)
    size_groups = signed_notional.reshape(cluster_ordinal, cluster_extent)

    def value_group(inputs):
        sensitivity_portion, size_part = inputs
        linear = jnp.dot(state_bf, sensitivity_portion, preferred_element_type=jnp.float32)
        trade_value = jax.nn.softplus(linear) * size_part[None, :]
        return trade_value.reshape(row_count, per_group, block_width).sum(axis=2)

    block_sums = lax.map(value_group, (sensitivity_clusters, size_groups))
    block_sums = block_sums.transpose(1, 0, 2).reshape(row_count, TRADE_BLOCKS)
    ownership = (batch_obligor[:, None] == jnp.arange(CPTY, dtype=jnp.int32)[None, :]).astype(jnp.float32)
    netted = jnp.dot(block_sums, ownership, precision=highest)
    shifted = netted - collateral_ceiling[None, :]
    exposure = jax.nn.softplus(shifted).reshape(EXPOSURE_DATES, PATHS, CPTY)
    exposure_profile = jnp.sum(exposure, axis=1) / PATHS
    net_adjoint = (default_discount_mass[:, None, :] * jax.nn.sigmoid(shifted).reshape(EXPOSURE_DATES, PATHS, CPTY)).reshape(row_count, CPTY)
    block_adjoint = jnp.dot(net_adjoint, ownership.T, precision=highest)
    adjoint_groups = block_adjoint.reshape(row_count, cluster_ordinal, per_group).transpose(1, 0, 2)

    def pull_group(running, inputs):
        sensitivity_portion, size_part, upstream = inputs
        linear = jnp.dot(state_bf, sensitivity_portion, preferred_element_type=jnp.float32)
        slope_term = jax.nn.sigmoid(linear) * size_part[None, :]
        value_adjoint = (upstream[:, :, None] * slope_term.reshape(row_count, per_group, block_width)).reshape(row_count, cluster_extent).astype(jnp.bfloat16)
        product = lax.dot_general(value_adjoint, sensitivity_portion, (((1,), (1,)), ((), ())), preferred_element_type=jnp.float32)
        return running + product, None

    direct, _ = lax.scan(pull_group, jnp.zeros((row_count, STATE_DRIVERS), jnp.float32), (sensitivity_clusters, size_groups, adjoint_groups))
    direct = direct.reshape(EXPOSURE_DATES, PATHS, STATE_DRIVERS)

    def retreat(message, inputs):
        retain, source = inputs
        adjoint = source + message
        return retain[None, :] * adjoint, adjoint

    _, shock_gradient = lax.scan(retreat, jnp.zeros((PATHS, STATE_DRIVERS), jnp.float32), (persistence_ratio, direct), reverse=True)
    return exposure_profile, shock_gradient
```

```python
import functools

import jax
import jax.numpy as jnp
from jax import lax
from jax.experimental import pallas as pl
from jax.experimental.pallas import tpu as pltpu
from jax.sharding import PartitionSpec as P

block_width = 128
highest = lax.Precision.HIGHEST
f32 = jnp.float32
bf16 = jnp.bfloat16


def swap(value, axes, sizes, flips):
    count = 1
    for size in sizes:
        count *= size
    pairs = []
    for flat in range(count):
        rest, target, scale = flat, 0, 1
        for size, flip in zip(reversed(sizes), reversed(flips)):
            target += ((rest % size) ^ flip) * scale
            rest //= size
            scale *= size
        pairs.append((flat, target))
    return lax.ppermute(value, axes, pairs)


def entering(value, axis, combine, identity, reverse):
    length, index = (lax.axis_size(axis), lax.axis_index(axis))
    everything = jax.tree.map(lambda part: lax.all_gather(part, axis), value)
    before = jax.tree.map(
        lambda part, zero: jnp.broadcast_to(jnp.asarray(zero, part.dtype), part.shape),
        value,
        identity,
    )
    for k in range(length):
        at = length - 1 - k if reverse else k
        reached = at > index if reverse else at < index
        new = combine(before, jax.tree.map(lambda part: part[at], everything))
        before = jax.tree.map(lambda a, b: jnp.where(reached, a, b), new, before)
    return before


def compose(earlier, later):
    return (later[0] * earlier[0], later[0] * earlier[1] + later[1])


def softplus(v):
    return jnp.maximum(v, jnp.log(1.0 + jnp.exp(jnp.minimum(v, 80.0))))


def value_kernel(blocks, x_ref, rho_ref, arriving_ref, first_ref, d_ref, n_ref, sums_ref, state_ref):
    dates, paths, _ = x_ref.shape

    @pl.when(pl.program_id(0) == 0)
    def _():
        carried = arriving_ref[...] * first_ref[0:1, :]
        for t in range(dates):
            carried = rho_ref[t : t + 1, :] * carried + x_ref[t]
            state_ref[:, t * paths : (t + 1) * paths] = carried.T.astype(bf16)

    size_t = n_ref[...].T
    linear = jnp.dot(d_ref[...].T, state_ref[...], preferred_element_type=f32)
    for b in range(blocks):
        value = softplus(linear[b * block_width : (b + 1) * block_width]) * size_t[:, b : b + 1]
        sums_ref[b : b + 1, :] = jnp.sum(value, axis=0, keepdims=True)


def value_pass(x, rho, arriving, keep, d, n):
    dates, paths, factors = x.shape
    rows, trades = dates * paths, d.shape[1]
    step = min(2048, trades)
    blocks = step // block_width
    whole = lambda *shape: pl.BlockSpec(shape, lambda i: (0,) * len(shape))
    return pl.pallas_call(
        functools.partial(value_kernel, blocks),
        grid=(trades // step,),
        in_specs=[
            whole(dates, paths, factors),
            whole(dates, factors),
            whole(paths, factors),
            whole(8, factors),
            pl.BlockSpec((factors, step), lambda i: (0, i)),
            pl.BlockSpec((blocks, block_width), lambda i: (i, 0)),
        ],
        out_specs=[pl.BlockSpec((blocks, rows), lambda i: (i, 0)), whole(factors, rows)],
        out_shape=[
            jax.ShapeDtypeStruct((trades // block_width, rows), f32),
            jax.ShapeDtypeStruct((factors, rows), bf16),
        ],
        compiler_params=pltpu.CompilerParams(vmem_limit_bytes=50 << 20),
        cost_estimate=pl.CostEstimate(
            flops=2 * rows * trades * factors, bytes_accessed=2 * trades * factors, transcendentals=2 * rows * trades
        ),
        name="value_pass",
    )(x, rho, arriving, keep, d, n)


def split_dot(selector, value):
    selector = selector.astype(bf16)
    high = value.astype(bf16)
    rest = value - high.astype(f32)
    middle = rest.astype(bf16)
    low = (rest - middle.astype(f32)).astype(bf16)
    dot = functools.partial(jnp.dot, selector, preferred_element_type=f32)
    return dot(low) + dot(middle) + dot(high)


def net_stage(shards, cpty_dev, dates, me, sums, small, upstream_ref, exposure_ref):
    blocks, rows = sums[0].shape
    paths = rows // dates
    cpties = shards * cpty_dev
    shift = cpty_dev.bit_length() - 1
    netted = None
    own = None
    columns = []
    for k in range(shards):
        tall = small[k][...].T
        columns.append(tall)

        def label(owner):
            owner = owner.astype(jnp.int32)
            return (((owner >> shift) ^ me) << shift) + (owner & (cpty_dev - 1))

        row = label(small[k][dates + 1 : dates + 2, :blocks])
        pick = lax.broadcasted_iota(jnp.int32, (cpties, blocks), 0) == row
        part = split_dot(jnp.where(pick, 1.0, 0.0), sums[k][...])
        netted = part if netted is None else netted + part
        if k == 0:
            column = label(tall[:blocks, dates + 1 : dates + 2])
            own = jnp.where(lax.broadcasted_iota(jnp.int32, (blocks, cpties), 1) == column, 1.0, 0.0)
    adjoint = []
    for k in range(shards):
        shifted = netted[k * cpty_dev : (k + 1) * cpty_dev] - columns[k][:cpty_dev, dates : dates + 1]
        slope = 0.5 * jnp.tanh(0.5 * shifted) + 0.5
        adjoint.append(
            jnp.concatenate(
                [
                    slope[:, t * paths : (t + 1) * paths] * columns[k][:cpty_dev, t : t + 1]
                    for t in range(dates)
                ],
                axis=1,
            )
        )
        if k == 0:
            exposed = softplus(shifted)
            lane = lax.broadcasted_iota(jnp.int32, (cpty_dev, 128), 1)
            table = jnp.zeros((cpty_dev, 128), f32)
            for t in range(dates):
                total = jnp.sum(exposed[:, t * paths : (t + 1) * paths], axis=1, keepdims=True)
                table = jnp.where(lane == t, total, table)
            exposure_ref[...] = table.T[:dates]
    upstream_ref[...] = split_dot(own, jnp.concatenate(adjoint, axis=0))


def pull_step(blocks, upstream, half_ref, d_ref, n_ref, total_ref):
    size_t = 0.5 * n_ref[...].T
    linear = jnp.dot(d_ref[...].T, half_ref[...], preferred_element_type=f32)
    parts = []
    for b in range(blocks):
        slope = jnp.tanh(linear[b * block_width : (b + 1) * block_width])
        size = size_t[:, b : b + 1]
        parts.append(((slope * size + size) * upstream[b : b + 1, :]).astype(bf16))
    total_ref[...] += jnp.dot(d_ref[...], jnp.concatenate(parts, axis=0), preferred_element_type=f32)


def pull_net_kernel(shards, cpty_dev, dates, blocks, me_ref, state_ref, rho_ref, d_ref, n_ref, *refs):
    sums, refs = refs[:shards], refs[shards:]
    small, refs = refs[:shards], refs[shards:]
    exposure_ref, refs = refs[0], refs[1:]
    chain, refs = refs[:shards], refs[shards:]
    message, refs = refs[:shards], refs[shards:]
    upstream_ref, half_ref, total_ref, chained_ref, message_ref = refs
    rows = state_ref.shape[1]
    paths = rows // dates
    i = pl.program_id(0)
    me = me_ref[0]

    @pl.when(i == 0)
    def _():
        half_ref[...] = state_ref[...] * 0.5
        total_ref[...] = jnp.zeros_like(total_ref)
        net_stage(shards, cpty_dev, dates, me, sums, small, upstream_ref, exposure_ref)

    upstream = upstream_ref[pl.ds(pl.multiple_of(i * blocks, blocks), blocks), :]
    pull_step(blocks, upstream, half_ref, d_ref, n_ref, total_ref)

    @pl.when(i == pl.num_programs(0) - 1)
    def _():
        carried = jnp.zeros((paths, rho_ref.shape[1]), f32)
        for t in reversed(range(dates)):
            adjoint = total_ref[:, t * paths : (t + 1) * paths].T + carried
            chained_ref[t] = adjoint
            carried = rho_ref[t : t + 1, :] * adjoint
        message_ref[...] = carried
        piece = paths // shards
        for k in range(shards):
            at = pl.ds(pl.multiple_of((me ^ k) * piece, piece), piece)
            chain[k][...] = chained_ref[:, at, :]
            message[k][...] = message_ref[at, :]


def pull_net_pass(shards, dates, cpty_dev, me, state, rho, d, n, sums, small):
    factors, rows = state.shape
    trades = d.shape[1]
    paths = rows // dates
    piece = paths // shards
    step = min(2048, trades)
    blocks = step // block_width
    whole = lambda *shape: pl.BlockSpec(shape, lambda i, s: (0,) * len(shape))
    out = pl.pallas_call(
        functools.partial(pull_net_kernel, shards, cpty_dev, dates, blocks),
        grid_spec=pltpu.PrefetchScalarGridSpec(
            num_scalar_prefetch=1,
            grid=(trades // step,),
            in_specs=[
                whole(factors, rows),
                whole(dates, factors),
                pl.BlockSpec((factors, step), lambda i, s: (0, i)),
                pl.BlockSpec((blocks, block_width), lambda i, s: (i, 0)),
            ]
            + [whole(*part.shape) for part in sums]
            + [whole(*part.shape) for part in small],
            out_specs=[whole(dates, cpty_dev)]
            + [whole(dates, piece, factors)] * shards
            + [whole(piece, factors)] * shards,
            scratch_shapes=[
                pltpu.VMEM(sums[0].shape, f32),
                pltpu.VMEM((factors, rows), bf16),
                pltpu.VMEM((factors, rows), f32),
                pltpu.VMEM((dates, paths, factors), f32),
                pltpu.VMEM((paths, factors), f32),
            ],
        ),
        out_shape=[jax.ShapeDtypeStruct((dates, cpty_dev), f32)]
        + [jax.ShapeDtypeStruct((dates, piece, factors), f32)] * shards
        + [jax.ShapeDtypeStruct((piece, factors), f32)] * shards,
        compiler_params=pltpu.CompilerParams(vmem_limit_bytes=50 << 20),
        cost_estimate=pl.CostEstimate(
            flops=4 * rows * trades * factors, bytes_accessed=2 * trades * factors, transcendentals=rows * trades
        ),
        name="pull_net_pass",
    )(me, state, rho, d, n, *sums, *small)
    return out[0], out[1 : 1 + shards], out[1 + shards :]


def pull_kernel(blocks, state_ref, d_ref, n_ref, upstream_ref, direct_ref, half_ref, total_ref):
    dates, paths, _ = direct_ref.shape

    @pl.when(pl.program_id(0) == 0)
    def _():
        half_ref[...] = state_ref[...] * 0.5
        total_ref[...] = jnp.zeros_like(total_ref)

    pull_step(blocks, upstream_ref[...], half_ref, d_ref, n_ref, total_ref)

    @pl.when(pl.program_id(0) == pl.num_programs(0) - 1)
    def _():
        for t in range(dates):
            direct_ref[t] = total_ref[:, t * paths : (t + 1) * paths].T


def pull_pass(dates, state, d, n, upstream):
    factors, rows = state.shape
    trades = d.shape[1]
    paths = rows // dates
    step = min(2048, trades)
    blocks = step // block_width
    whole = lambda *shape: pl.BlockSpec(shape, lambda i: (0,) * len(shape))
    return pl.pallas_call(
        functools.partial(pull_kernel, blocks),
        grid=(trades // step,),
        in_specs=[
            whole(factors, rows),
            pl.BlockSpec((factors, step), lambda i: (0, i)),
            pl.BlockSpec((blocks, block_width), lambda i: (i, 0)),
            pl.BlockSpec((blocks, rows), lambda i: (i, 0)),
        ],
        out_specs=whole(dates, paths, factors),
        out_shape=jax.ShapeDtypeStruct((dates, paths, factors), f32),
        scratch_shapes=[pltpu.VMEM((factors, rows), bf16), pltpu.VMEM((factors, rows), f32)],
        compiler_params=pltpu.CompilerParams(vmem_limit_bytes=50 << 20),
        name="pull_pass",
    )(state, d, n, upstream)


def place_kernel(shards, me_ref, *refs):
    pieces, out_ref = refs[:shards], refs[shards]
    size = pieces[0].shape[1]
    for k in range(shards):
        at = pl.ds(pl.multiple_of((me_ref[0] ^ k) * size, size), size)
        out_ref[:, at, :] = pieces[k][...]


def place(me, pieces):
    shards = len(pieces)
    dates, size, factors = pieces[0].shape
    whole = lambda *shape: pl.BlockSpec(shape, lambda i, s: (0,) * len(shape))
    return pl.pallas_call(
        functools.partial(place_kernel, shards),
        grid_spec=pltpu.PrefetchScalarGridSpec(
            num_scalar_prefetch=1,
            grid=(1,),
            in_specs=[whole(dates, size, factors)] * shards,
            out_specs=whole(dates, shards * size, factors),
        ),
        out_shape=jax.ShapeDtypeStruct((dates, shards * size, factors), f32),
        name="place",
    )(me, *pieces)


def local_chain(x, rho):
    carried = x[0]
    gain = rho[0]
    for t in range(1, x.shape[0]):
        carried = rho[t][None, :] * carried + x[t]
        gain = rho[t] * gain
    return gain, carried


def near(x, rho, d, size, obligor, ceiling, mass):
    dates, paths, factors = x.shape
    shards = lax.axis_size("trade")
    cpty_dev = ceiling.shape[0]
    n = size.reshape(-1, block_width)
    blocks = n.shape[0]
    me = lax.axis_index("trade").astype(jnp.int32)[None]
    later = lax.axis_index("date") > 0
    _, carried = local_chain(x, rho)
    arriving = swap(carried, ("date",), (2,), (1,))
    keep = jnp.broadcast_to(jnp.where(later, 1.0, 0.0).astype(f32), (8, factors))

    wide = lambda part: jnp.pad(part, ((0, 0), (0, 128 - part.shape[1])))
    facts = jnp.concatenate([wide(mass), wide(ceiling[None, :]), wide(obligor.astype(f32)[None, :])], axis=0)
    facts = jnp.pad(facts, ((0, 8 - facts.shape[0]), (0, 0)))
    small = [facts] + [swap(facts, ("trade",), (shards,), (k,)) for k in range(1, shards)]

    sums, state = value_pass(x, rho, arriving, keep, d, n)
    sums = [sums] + [swap(sums, ("trade",), (shards,), (k,)) for k in range(1, shards)]
    exposure, chain, message = pull_net_pass(shards, dates, cpty_dev, me, state, rho, d, n, sums, small)
    total_paths = paths * lax.axis_size("path")
    exposure_profile = (exposure + swap(exposure, ("path",), (2,), (1,))) / total_paths

    chain = [chain[0]] + [swap(chain[k], ("trade",), (shards,), (k,)) for k in range(1, shards)]
    message = [swap(message[k], ("trade", "date"), (shards, 2), (k, 1)) for k in range(shards)]
    total = functools.reduce(jnp.add, chain)
    reached = jnp.where(later, 0.0, functools.reduce(jnp.add, message))
    rows = []
    for t in reversed(range(dates)):
        rows.append(total[t] + reached)
        reached = rho[t][None, :] * reached
    own = jnp.stack(rows[::-1])
    pieces = [own] + [swap(own, ("trade",), (shards,), (k,)) for k in range(1, shards)]
    return exposure_profile, place(me, pieces)


def far(x, rho, d, size, obligor, ceiling, mass):
    dates, paths, factors = x.shape
    rows = dates * paths
    cpty_dev = ceiling.shape[0]
    n = size.reshape(-1, block_width)
    value = local_chain(x, rho)
    identity = (jnp.ones_like(value[0]), jnp.zeros_like(value[1]))
    _, arriving = entering(value, "date", compose, identity, False)
    sums, state = value_pass(x, rho, arriving, jnp.ones((8, factors), f32), d, n)
    cpties = cpty_dev * lax.axis_size("trade")
    ownership = (obligor[:, None] == jnp.arange(cpties, dtype=jnp.int32)[None, :]).astype(f32)
    partial = lax.dot_general(ownership, sums, (((0,), (0,)), ((), ())), precision=highest)
    netted = lax.psum_scatter(partial, "trade", scatter_dimension=0, tiled=True)
    shifted = (netted - ceiling[:, None]).reshape(cpty_dev, dates, paths)
    exposure = jnp.sum(jax.nn.softplus(shifted), axis=2).T
    exposure_profile = lax.psum(exposure, "path") / (paths * lax.axis_size("path"))
    adjoint = (mass.T[:, :, None] * jax.nn.sigmoid(shifted)).reshape(cpty_dev, rows)
    gathered = lax.all_gather(adjoint, "trade", axis=0, tiled=True)
    upstream = jnp.dot(ownership, gathered, precision=highest)
    direct = lax.psum(pull_pass(dates, state, d, n, upstream), "trade")

    gain = jnp.ones((factors,), f32)
    message = jnp.zeros((paths, factors), f32)
    for t in reversed(range(dates)):
        message = rho[t][None, :] * (direct[t] + message)
        gain = rho[t] * gain
    _, message = entering((gain, message), "date", compose, identity, True)
    adjoints = []
    for t in reversed(range(dates)):
        adjoint = direct[t] + message
        adjoints.append(adjoint)
        message = rho[t][None, :] * adjoint
    return exposure_profile, jnp.stack(adjoints[::-1])


def solution(mesh):
    close = mesh.shape["date"] == 2 and mesh.shape["trade"] == 4 and mesh.shape["path"] == 2
    return jax.shard_map(
        near if close else far,
        mesh=mesh,
        in_specs=(
            P(("grp", "date"), "path", None),
            P(("grp", "date"), None),
            P(None, ("grp", "trade")),
            P(("grp", "trade")),
            P(("grp", "trade")),
            P(("grp", "trade")),
            P(("grp", "date"), "trade"),
        ),
        out_specs=(P(("grp", "date"), "trade"), P(("grp", "date"), "path", None)),
        check_vma=False,
    )
```

```python
import functools

import jax
import jax.numpy as jnp
from jax import lax
from jax.experimental import pallas as pl
from jax.experimental.pallas import tpu as pltpu
from jax.sharding import PartitionSpec as P

block_width = 128
highest = lax.Precision.HIGHEST
f32 = jnp.float32
bf16 = jnp.bfloat16


def swap(value, axes, sizes, flips):
    count = 1
    for size in sizes:
        count *= size
    pairs = []
    for flat in range(count):
        rest, target, scale = flat, 0, 1
        for size, flip in zip(reversed(sizes), reversed(flips)):
            target += ((rest % size) ^ flip) * scale
            rest //= size
            scale *= size
        pairs.append((flat, target))
    return lax.ppermute(value, axes, pairs)


def entering(value, axis, combine, identity, reverse):
    length, index = (lax.axis_size(axis), lax.axis_index(axis))
    everything = jax.tree.map(lambda part: lax.all_gather(part, axis), value)
    before = jax.tree.map(
        lambda part, zero: jnp.broadcast_to(jnp.asarray(zero, part.dtype), part.shape),
        value,
        identity,
    )
    for k in range(length):
        at = length - 1 - k if reverse else k
        reached = at > index if reverse else at < index
        new = combine(before, jax.tree.map(lambda part: part[at], everything))
        before = jax.tree.map(lambda a, b: jnp.where(reached, a, b), new, before)
    return before


def compose(earlier, later):
    return (later[0] * earlier[0], later[0] * earlier[1] + later[1])


def softplus(v):
    return jnp.maximum(v, jnp.log(1.0 + jnp.exp(jnp.minimum(v, 80.0))))


def chain_kernel(x_ref, rho_ref, carried_ref):
    carried = x_ref[0]
    for t in range(1, x_ref.shape[0]):
        carried = rho_ref[t : t + 1, :] * carried + x_ref[t]
    carried_ref[...] = carried


def chain_pass(x, rho):
    return pl.pallas_call(
        chain_kernel, out_shape=jax.ShapeDtypeStruct(x.shape[1:], f32), name="chain_pass"
    )(x, rho)


def prepare_kernel(d_ref, n_ref, x_ref, rho_ref, turned_ref, size_ref, x_out_ref, rho_out_ref):
    turned_ref[...] = d_ref[...].T

    @pl.when(pl.program_id(0) == 0)
    def _():
        size_ref[...] = n_ref[...]
        x_out_ref[...] = x_ref[...]
        rho_out_ref[...] = rho_ref[...]


def prepare_pass(d, n, x, rho):
    factors, trades = d.shape
    step = min(2048, trades)
    whole = lambda *shape: pl.BlockSpec(shape, lambda i: (0,) * len(shape))
    return pl.pallas_call(
        prepare_kernel,
        grid=(trades // step,),
        in_specs=[pl.BlockSpec((factors, step), lambda i: (0, i)), whole(*n.shape), whole(*x.shape), whole(*rho.shape)],
        out_specs=[pl.BlockSpec((step, factors), lambda i: (i, 0)), whole(*n.shape), whole(*x.shape), whole(*rho.shape)],
        out_shape=[
            jax.ShapeDtypeStruct((trades, factors), bf16),
            jax.ShapeDtypeStruct(n.shape, f32),
            jax.ShapeDtypeStruct(x.shape, f32),
            jax.ShapeDtypeStruct(rho.shape, f32),
        ],
        compiler_params=pltpu.CompilerParams(vmem_limit_bytes=8 << 20),
        cost_estimate=pl.CostEstimate(flops=0, bytes_accessed=4 * trades * factors, transcendentals=0),
        name="prepare_pass",
    )(d, n, x, rho)


def value_kernel(step, x_ref, rho_ref, arriving_ref, keep_ref, facts_ref, turned_ref, n_ref, sums_ref, state_ref):
    dates, paths, _ = x_ref.shape
    trades = turned_ref.shape[0]
    blocks = step // block_width
    carried = arriving_ref[...] * keep_ref[0].astype(f32)
    for t in range(dates):
        carried = rho_ref[t : t + 1, :] * carried + x_ref[t]
        state_ref[:, t * paths : (t + 1) * paths] = carried.T.astype(bf16)
    total = trades // block_width
    sums_ref[total : total + 8, :128] = facts_ref[...]

    @pl.loop(0, trades // step)
    def _(c):
        size_t = n_ref[pl.ds(pl.multiple_of(c * blocks, blocks), blocks), :].T
        turned = turned_ref[pl.ds(pl.multiple_of(c * step, step), step), :]
        linear = jnp.dot(turned, state_ref[...], preferred_element_type=f32)
        lines = []
        for b in range(blocks):
            value = softplus(linear[b * block_width : (b + 1) * block_width]) * size_t[:, b : b + 1]
            lines.append(jnp.sum(value, axis=0, keepdims=True))
        sums_ref[pl.ds(pl.multiple_of(c * blocks, blocks), blocks), :] = jnp.concatenate(lines, axis=0)


def value_pass(x, rho, arriving, keep, facts, turned, n):
    dates, paths, factors = x.shape
    rows, trades = dates * paths, turned.shape[0]
    vmem = pl.BlockSpec(memory_space=pltpu.VMEM)
    return pl.pallas_call(
        functools.partial(value_kernel, min(2048, trades)),
        in_specs=[vmem, vmem, vmem, pl.BlockSpec(memory_space=pltpu.SMEM), vmem, vmem, vmem],
        out_specs=[vmem, vmem],
        out_shape=[
            jax.ShapeDtypeStruct((trades // block_width + 8, rows), f32),
            jax.ShapeDtypeStruct((factors, rows), bf16),
        ],
        compiler_params=pltpu.CompilerParams(vmem_limit_bytes=32 << 20),
        cost_estimate=pl.CostEstimate(
            flops=2 * rows * trades * factors, bytes_accessed=2 * trades * factors, transcendentals=2 * rows * trades
        ),
        name="value_pass",
    )(x, rho, arriving, keep, facts, turned, n)


def split_dot(selector, value):
    selector = selector.astype(bf16)
    high = value.astype(bf16)
    rest = value - high.astype(f32)
    middle = rest.astype(bf16)
    low = (rest - middle.astype(f32)).astype(bf16)
    dot = functools.partial(jnp.dot, selector, preferred_element_type=f32)
    return dot(low) + dot(middle) + dot(high)


def net_stage(shards, cpty_dev, dates, me, sums, upstream_ref, exposure_ref):
    blocks, rows = sums[0].shape
    blocks -= 8
    small = [part.at[blocks : blocks + 8, :128] for part in sums]
    paths = rows // dates
    cpties = shards * cpty_dev
    shift = cpty_dev.bit_length() - 1
    netted = None
    own = None
    columns = []
    for k in range(shards):
        tall = small[k][...].T
        columns.append(tall)

        def label(owner):
            owner = owner.astype(jnp.int32)
            return (((owner >> shift) ^ me) << shift) + (owner & (cpty_dev - 1))

        row = label(small[k][dates + 1 : dates + 2, :blocks])
        pick = lax.broadcasted_iota(jnp.int32, (cpties, blocks), 0) == row
        part = split_dot(jnp.where(pick, 1.0, 0.0), sums[k][:blocks])
        netted = part if netted is None else netted + part
        if k == 0:
            column = label(tall[:blocks, dates + 1 : dates + 2])
            own = jnp.where(lax.broadcasted_iota(jnp.int32, (blocks, cpties), 1) == column, 1.0, 0.0)
    adjoint = []
    for k in range(shards):
        shifted = netted[k * cpty_dev : (k + 1) * cpty_dev] - columns[k][:cpty_dev, dates : dates + 1]
        slope = 0.5 * jnp.tanh(0.5 * shifted) + 0.5
        adjoint.append(
            jnp.concatenate(
                [
                    slope[:, t * paths : (t + 1) * paths] * columns[k][:cpty_dev, t : t + 1]
                    for t in range(dates)
                ],
                axis=1,
            )
        )
        if k == 0:
            exposed = softplus(shifted)
            lane = lax.broadcasted_iota(jnp.int32, (cpty_dev, 128), 1)
            table = jnp.zeros((cpty_dev, 128), f32)
            for t in range(dates):
                total = jnp.sum(exposed[:, t * paths : (t + 1) * paths], axis=1, keepdims=True)
                table = jnp.where(lane == t, total, table)
            exposure_ref[...] = table.T[:dates]
    upstream_ref[...] = split_dot(own, jnp.concatenate(adjoint, axis=0))


def pull_step(blocks, upstream, half_ref, d_ref, n_ref, total_ref):
    size_t = 0.5 * n_ref[...].T
    linear = jnp.dot(d_ref[...].T, half_ref[...], preferred_element_type=f32)
    parts = []
    for b in range(blocks):
        slope = jnp.tanh(linear[b * block_width : (b + 1) * block_width])
        size = size_t[:, b : b + 1]
        parts.append(((slope * size + size) * upstream[b : b + 1, :]).astype(bf16))
    total_ref[...] += jnp.dot(d_ref[...], jnp.concatenate(parts, axis=0), preferred_element_type=f32)


def pull_net_kernel(shards, cpty_dev, dates, blocks, me_ref, state_ref, rho_ref, d_ref, n_ref, *refs):
    sums, refs = refs[:shards], refs[shards:]
    exposure_ref, refs = refs[0], refs[1:]
    chain, refs = refs[:shards], refs[shards:]
    upstream_ref, half_ref, total_ref, chained_ref = refs
    rows = state_ref.shape[1]
    paths = rows // dates
    i = pl.program_id(0)
    me = me_ref[0]

    @pl.when(i == 0)
    def _():
        half_ref[...] = state_ref[...] * 0.5
        total_ref[...] = jnp.zeros_like(total_ref)
        net_stage(shards, cpty_dev, dates, me, sums, upstream_ref, exposure_ref)

    upstream = upstream_ref[pl.ds(pl.multiple_of(i * blocks, blocks), blocks), :]
    pull_step(blocks, upstream, half_ref, d_ref, n_ref, total_ref)

    @pl.when(i == pl.num_programs(0) - 1)
    def _():
        carried = jnp.zeros((paths, rho_ref.shape[1]), f32)
        for t in reversed(range(dates)):
            adjoint = total_ref[:, t * paths : (t + 1) * paths].T + carried
            chained_ref[t] = adjoint
            carried = rho_ref[t : t + 1, :] * adjoint
        piece = paths // shards
        for k in range(shards):
            at = pl.ds(pl.multiple_of((me ^ k) * piece, piece), piece)
            chain[k][...] = chained_ref[:, at, :]


def pull_net_pass(shards, dates, cpty_dev, me, state, rho, d, n, sums):
    factors, rows = state.shape
    trades = d.shape[1]
    paths = rows // dates
    piece = paths // shards
    step = min(2048, trades)
    blocks = step // block_width
    whole = lambda *shape: pl.BlockSpec(shape, lambda i, s: (0,) * len(shape))
    out = pl.pallas_call(
        functools.partial(pull_net_kernel, shards, cpty_dev, dates, blocks),
        grid_spec=pltpu.PrefetchScalarGridSpec(
            num_scalar_prefetch=1,
            grid=(trades // step,),
            in_specs=[
                whole(factors, rows),
                whole(dates, factors),
                pl.BlockSpec((factors, step), lambda i, s: (0, i)),
                pl.BlockSpec((blocks, block_width), lambda i, s: (i, 0)),
            ]
            + [whole(*part.shape) for part in sums],
            out_specs=[whole(dates, cpty_dev)] + [whole(dates, piece, factors)] * shards,
            scratch_shapes=[
                pltpu.VMEM((trades // block_width, rows), f32),
                pltpu.VMEM((factors, rows), bf16),
                pltpu.VMEM((factors, rows), f32),
                pltpu.VMEM((dates, paths, factors), f32),
            ],
        ),
        out_shape=[jax.ShapeDtypeStruct((dates, cpty_dev), f32)]
        + [jax.ShapeDtypeStruct((dates, piece, factors), f32)] * shards,
        compiler_params=pltpu.CompilerParams(vmem_limit_bytes=32 << 20),
        cost_estimate=pl.CostEstimate(
            flops=4 * rows * trades * factors, bytes_accessed=2 * trades * factors, transcendentals=rows * trades
        ),
        name="pull_net_pass",
    )(me, state, rho, d, n, *sums)
    return out[0], out[1:]


def pull_kernel(blocks, state_ref, d_ref, n_ref, upstream_ref, direct_ref, half_ref, total_ref):
    dates, paths, _ = direct_ref.shape

    @pl.when(pl.program_id(0) == 0)
    def _():
        half_ref[...] = state_ref[...] * 0.5
        total_ref[...] = jnp.zeros_like(total_ref)

    pull_step(blocks, upstream_ref[...], half_ref, d_ref, n_ref, total_ref)

    @pl.when(pl.program_id(0) == pl.num_programs(0) - 1)
    def _():
        for t in range(dates):
            direct_ref[t] = total_ref[:, t * paths : (t + 1) * paths].T


def pull_pass(dates, state, d, n, upstream):
    factors, rows = state.shape
    trades = d.shape[1]
    paths = rows // dates
    step = min(2048, trades)
    blocks = step // block_width
    whole = lambda *shape: pl.BlockSpec(shape, lambda i: (0,) * len(shape))
    return pl.pallas_call(
        functools.partial(pull_kernel, blocks),
        grid=(trades // step,),
        in_specs=[
            whole(factors, rows),
            pl.BlockSpec((factors, step), lambda i: (0, i)),
            pl.BlockSpec((blocks, block_width), lambda i: (i, 0)),
            pl.BlockSpec((blocks, rows), lambda i: (i, 0)),
        ],
        out_specs=whole(dates, paths, factors),
        out_shape=jax.ShapeDtypeStruct((dates, paths, factors), f32),
        scratch_shapes=[pltpu.VMEM((factors, rows), bf16), pltpu.VMEM((factors, rows), f32)],
        compiler_params=pltpu.CompilerParams(vmem_limit_bytes=50 << 20),
        name="pull_pass",
    )(state, d, n, upstream)


def place_kernel(shards, me_ref, *refs):
    pieces, out_ref = refs[:shards], refs[shards]
    size = pieces[0].shape[1]
    for k in range(shards):
        at = pl.ds(pl.multiple_of((me_ref[0] ^ k) * size, size), size)
        out_ref[:, at, :] = pieces[k][...]


def place(me, pieces):
    shards = len(pieces)
    dates, size, factors = pieces[0].shape
    whole = lambda *shape: pl.BlockSpec(shape, lambda i, s: (0,) * len(shape))
    return pl.pallas_call(
        functools.partial(place_kernel, shards),
        grid_spec=pltpu.PrefetchScalarGridSpec(
            num_scalar_prefetch=1,
            grid=(1,),
            in_specs=[whole(dates, size, factors)] * shards,
            out_specs=whole(dates, shards * size, factors),
        ),
        out_shape=jax.ShapeDtypeStruct((dates, shards * size, factors), f32),
        compiler_params=pltpu.CompilerParams(vmem_limit_bytes=4 << 20),
        name="place",
    )(me, *pieces)


def local_chain(x, rho):
    carried = x[0]
    gain = rho[0]
    for t in range(1, x.shape[0]):
        carried = rho[t][None, :] * carried + x[t]
        gain = rho[t] * gain
    return gain, carried


def near(x, rho, d, size, obligor, ceiling, mass):
    dates, paths, factors = x.shape
    shards = lax.axis_size("trade")
    cpty_dev = ceiling.shape[0]
    n = size.reshape(-1, block_width)
    me = lax.axis_index("trade").astype(jnp.int32)[None]
    date = lax.axis_index("date").astype(jnp.int32)
    over = lambda value, k: swap(value, ("trade",), (shards,), (k,))

    arriving = swap(chain_pass(x, rho), ("date",), (2,), (1,))
    turned, n_near, x_near, rho_near = prepare_pass(d, n, x, rho)
    wide = lambda part: jnp.pad(part, ((0, 0), (0, 128 - part.shape[1])))
    facts = jnp.concatenate([wide(mass), wide(ceiling[None, :]), wide(obligor.astype(f32)[None, :])], axis=0)
    facts = jnp.pad(facts, ((0, 8 - facts.shape[0]), (0, 0)))
    sums, state = value_pass(x_near, rho_near, arriving, date[None], facts, turned, n_near)

    sums = [sums] + [over(sums, k) for k in range(1, shards)]
    exposure, chain = pull_net_pass(shards, dates, cpty_dev, me, state, rho, d, n, sums)
    total = functools.reduce(jnp.add, [chain[0]] + [over(chain[k], k) for k in range(1, shards)])

    message = swap(rho[0][None, :] * total[0], ("date",), (2,), (1,))
    weights = [jnp.where(date > 0, 0.0, jnp.ones((factors,), f32))]
    for t in reversed(range(1, dates)):
        weights.append(rho[t] * weights[-1])
    own = total + jnp.stack(weights[::-1])[:, None, :] * message[None]
    own, exposure = lax.optimization_barrier((own, exposure))
    pieces = [own] + [over(own, k) for k in range(1, shards)]
    exposure_profile = (exposure + swap(exposure, ("path",), (2,), (1,))) / (paths * lax.axis_size("path"))
    return exposure_profile, place(me, pieces)


def far(x, rho, d, size, obligor, ceiling, mass):
    dates, paths, factors = x.shape
    rows = dates * paths
    cpty_dev = ceiling.shape[0]
    n = size.reshape(-1, block_width)
    value = local_chain(x, rho)
    identity = (jnp.ones_like(value[0]), jnp.zeros_like(value[1]))
    _, arriving = entering(value, "date", compose, identity, False)
    turned, n_near, x_near, rho_near = prepare_pass(d, n, x, rho)
    keep = jnp.ones((1,), jnp.int32)
    sums, state = value_pass(x_near, rho_near, arriving, keep, jnp.zeros((8, 128), f32), turned, n_near)
    sums = sums[: n.shape[0]]
    cpties = cpty_dev * lax.axis_size("trade")
    ownership = (obligor[:, None] == jnp.arange(cpties, dtype=jnp.int32)[None, :]).astype(f32)
    partial = lax.dot_general(ownership, sums, (((0,), (0,)), ((), ())), precision=highest)
    netted = lax.psum_scatter(partial, "trade", scatter_dimension=0, tiled=True)
    shifted = (netted - ceiling[:, None]).reshape(cpty_dev, dates, paths)
    exposure = jnp.sum(jax.nn.softplus(shifted), axis=2).T
    exposure_profile = lax.psum(exposure, "path") / (paths * lax.axis_size("path"))
    adjoint = (mass.T[:, :, None] * jax.nn.sigmoid(shifted)).reshape(cpty_dev, rows)
    gathered = lax.all_gather(adjoint, "trade", axis=0, tiled=True)
    upstream = jnp.dot(ownership, gathered, precision=highest)
    direct = lax.psum(pull_pass(dates, state, d, n, upstream), "trade")

    gain = jnp.ones((factors,), f32)
    message = jnp.zeros((paths, factors), f32)
    for t in reversed(range(dates)):
        message = rho[t][None, :] * (direct[t] + message)
        gain = rho[t] * gain
    _, message = entering((gain, message), "date", compose, identity, True)
    adjoints = []
    for t in reversed(range(dates)):
        adjoint = direct[t] + message
        adjoints.append(adjoint)
        message = rho[t][None, :] * adjoint
    return exposure_profile, jnp.stack(adjoints[::-1])


def solution(mesh):
    close = mesh.shape["date"] == 2 and mesh.shape["trade"] == 4 and mesh.shape["path"] == 2
    return jax.shard_map(
        near if close else far,
        mesh=mesh,
        in_specs=(
            P(("grp", "date"), "path", None),
            P(("grp", "date"), None),
            P(None, ("grp", "trade")),
            P(("grp", "trade")),
            P(("grp", "trade")),
            P(("grp", "trade")),
            P(("grp", "date"), "trade"),
        ),
        out_specs=(P(("grp", "date"), "trade"), P(("grp", "date"), "path", None)),
        check_vma=False,
    )
```

```python
import functools

import jax
import jax.numpy as jnp
from jax import lax
from jax.experimental import pallas as pl
from jax.experimental.pallas import tpu as pltpu
from jax.sharding import PartitionSpec as P

block_width = 128
highest = lax.Precision.HIGHEST
f32 = jnp.float32
bf16 = jnp.bfloat16


def swap(value, axes, sizes, flips):
    count = 1
    for size in sizes:
        count *= size
    pairs = []
    for flat in range(count):
        rest, target, scale = flat, 0, 1
        for size, flip in zip(reversed(sizes), reversed(flips)):
            target += ((rest % size) ^ flip) * scale
            rest //= size
            scale *= size
        pairs.append((flat, target))
    return lax.ppermute(value, axes, pairs)


def entering(value, axis, combine, identity, reverse):
    length, index = (lax.axis_size(axis), lax.axis_index(axis))
    everything = jax.tree.map(lambda part: lax.all_gather(part, axis), value)
    before = jax.tree.map(
        lambda part, zero: jnp.broadcast_to(jnp.asarray(zero, part.dtype), part.shape),
        value,
        identity,
    )
    for k in range(length):
        at = length - 1 - k if reverse else k
        reached = at > index if reverse else at < index
        new = combine(before, jax.tree.map(lambda part: part[at], everything))
        before = jax.tree.map(lambda a, b: jnp.where(reached, a, b), new, before)
    return before


def compose(earlier, later):
    return (later[0] * earlier[0], later[0] * earlier[1] + later[1])


def softplus(v):
    return jnp.maximum(v, jnp.log(1.0 + jnp.exp(jnp.minimum(v, 80.0))))


def far_copy(*parts):
    return [pltpu.with_memory_space_constraint(part, pltpu.HBM) for part in parts]


def chain_kernel(x_hbm, rho_hbm, carried_ref, x_ref, rho_ref, sems):
    dates = x_ref.shape[0]
    copies = [pltpu.make_async_copy(x_hbm.at[t], x_ref.at[t], sems.at[t]) for t in range(dates)]
    copies.append(pltpu.make_async_copy(rho_hbm, rho_ref, sems.at[dates]))
    for copy in copies:
        copy.start()
    copies[dates].wait()
    copies[0].wait()
    carried = x_ref[0]
    for t in range(1, dates):
        copies[t].wait()
        carried = rho_ref[t : t + 1, :] * carried + x_ref[t]
    carried_ref[...] = carried


def chain_pass(x, rho):
    return pl.pallas_call(
        chain_kernel,
        in_specs=[pl.BlockSpec(memory_space=pltpu.HBM)] * 2,
        out_specs=[pl.BlockSpec(memory_space=pltpu.VMEM)] * 3,
        out_shape=[
            jax.ShapeDtypeStruct(x.shape[1:], f32),
            jax.ShapeDtypeStruct(x.shape, f32),
            jax.ShapeDtypeStruct(rho.shape, f32),
        ],
        scratch_shapes=[pltpu.SemaphoreType.DMA((x.shape[0] + 1,))],
        compiler_params=pltpu.CompilerParams(vmem_limit_bytes=4 << 20),
        name="chain_pass",
    )(*far_copy(x, rho))


def prepare_kernel(step, d_hbm, n_hbm, mass_hbm, ceiling_hbm, obligor_hbm, *refs):
    turned_ref, n_ref, facts_ref, d_ref, mass_ref, ceiling_ref, obligor_ref, sems = refs
    pieces = d_ref.shape[1] // step
    copies = []
    for c in range(pieces):
        part = pl.ds(c * step, step)
        copies.append(pltpu.make_async_copy(d_hbm.at[:, part], d_ref.at[:, part], sems.at[c]))
    small = ((n_hbm, n_ref), (mass_hbm, mass_ref), (ceiling_hbm, ceiling_ref), (obligor_hbm, obligor_ref))
    for k, (source, target) in enumerate(small):
        copies.append(pltpu.make_async_copy(source, target, sems.at[pieces + k]))
    for copy in copies:
        copy.start()
    for c in range(pieces):
        copies[c].wait()
        turned_ref[c * step : (c + 1) * step, :] = d_ref[:, c * step : (c + 1) * step].T
    for copy in copies[pieces:]:
        copy.wait()
    dates, cpties = mass_ref.shape
    facts_ref[...] = jnp.zeros_like(facts_ref)
    facts_ref[:dates, :cpties] = mass_ref[...]
    facts_ref[dates : dates + 1, :cpties] = ceiling_ref[...]
    facts_ref[dates + 1 : dates + 2, : obligor_ref.shape[1]] = obligor_ref[...].astype(f32)


def prepare_pass(d, n, mass, ceiling, obligor):
    factors, trades = d.shape
    step = min(2048, trades)
    hbm = pl.BlockSpec(memory_space=pltpu.HBM)
    vmem = pl.BlockSpec(memory_space=pltpu.VMEM)
    ceiling, obligor = ceiling[None, :], obligor[None, :]
    return pl.pallas_call(
        functools.partial(prepare_kernel, step),
        in_specs=[hbm] * 5,
        out_specs=[vmem] * 3,
        out_shape=[
            jax.ShapeDtypeStruct((trades, factors), bf16),
            jax.ShapeDtypeStruct(n.shape, f32),
            jax.ShapeDtypeStruct((8, 128), f32),
        ],
        scratch_shapes=[
            pltpu.VMEM(d.shape, bf16),
            pltpu.VMEM(mass.shape, f32),
            pltpu.VMEM(ceiling.shape, f32),
            pltpu.VMEM(obligor.shape, jnp.int32),
            pltpu.SemaphoreType.DMA((trades // step + 4,)),
        ],
        compiler_params=pltpu.CompilerParams(vmem_limit_bytes=8 << 20),
        cost_estimate=pl.CostEstimate(flops=0, bytes_accessed=4 * trades * factors, transcendentals=0),
        name="prepare_pass",
    )(*far_copy(d, n, mass, ceiling, obligor))


def state_stage(x_ref, rho_ref, arriving_ref, keep_ref, state_refs):
    dates, paths, _ = x_ref.shape
    columns = [(ref, at) for ref in state_refs[::-1] for at in range(0, ref.shape[1], paths)]
    carried = arriving_ref[...] * keep_ref[0].astype(f32)
    for t, (ref, at) in enumerate(columns):
        carried = rho_ref[t : t + 1, :] * carried + x_ref[t]
        ref[:, at : at + paths] = carried.T.astype(bf16)


def sum_stage(step, state_ref, turned_ref, n_ref, sums_ref):
    blocks = step // block_width

    @pl.loop(0, turned_ref.shape[0] // step)
    def _(c):
        size_t = n_ref[pl.ds(pl.multiple_of(c * blocks, blocks), blocks), :].T
        turned = turned_ref[pl.ds(pl.multiple_of(c * step, step), step), :]
        linear = jnp.dot(turned, state_ref[...], preferred_element_type=f32)
        lines = []
        for b in range(blocks):
            value = softplus(linear[b * block_width : (b + 1) * block_width]) * size_t[:, b : b + 1]
            lines.append(jnp.sum(value, axis=0, keepdims=True))
        sums_ref[pl.ds(pl.multiple_of(c * blocks, blocks), blocks), :] = jnp.concatenate(lines, axis=0)


def first_value_kernel(step, x_ref, rho_ref, arriving_ref, keep_ref, facts_ref, turned_ref, n_ref, sums_ref, *state_refs):
    state_stage(x_ref, rho_ref, arriving_ref, keep_ref, state_refs)
    total = n_ref.shape[0]
    sums_ref[total:, :128] = facts_ref[...]
    sum_stage(step, state_refs[0], turned_ref, n_ref, sums_ref)


def value_cost(rows, trades, factors):
    return pl.CostEstimate(
        flops=2 * rows * trades * factors, bytes_accessed=2 * trades * factors, transcendentals=2 * rows * trades
    )


def first_value_pass(groups, x, rho, arriving, keep, facts, turned, n):
    dates, paths, factors = x.shape
    trades = turned.shape[0]
    rows = dates // groups * paths
    vmem = pl.BlockSpec(memory_space=pltpu.VMEM)
    out = pl.pallas_call(
        functools.partial(first_value_kernel, min(2048, trades)),
        in_specs=[vmem, vmem, vmem, pl.BlockSpec(memory_space=pltpu.SMEM), vmem, vmem, vmem],
        out_specs=[vmem] * (1 + groups),
        out_shape=[jax.ShapeDtypeStruct((n.shape[0] + 8, rows), f32)]
        + [jax.ShapeDtypeStruct((factors, rows), bf16)] * groups,
        compiler_params=pltpu.CompilerParams(vmem_limit_bytes=24 << 20),
        cost_estimate=value_cost(rows, trades, factors),
        name="first_value_pass",
    )(x, rho, arriving, keep, facts, turned, n)
    return out[0], out[1:]


def value_pass(state, turned, n):
    factors, rows = state.shape
    trades = turned.shape[0]
    vmem = pl.BlockSpec(memory_space=pltpu.VMEM)
    return pl.pallas_call(
        functools.partial(sum_stage, min(2048, trades)),
        in_specs=[vmem] * 3,
        out_specs=vmem,
        out_shape=jax.ShapeDtypeStruct((n.shape[0], rows), f32),
        compiler_params=pltpu.CompilerParams(vmem_limit_bytes=24 << 20),
        cost_estimate=value_cost(rows, trades, factors),
        name="value_pass",
    )(state, turned, n)


def split_dot(selector, value):
    selector = selector.astype(bf16)
    high = value.astype(bf16)
    rest = value - high.astype(f32)
    middle = rest.astype(bf16)
    low = (rest - middle.astype(f32)).astype(bf16)
    dot = functools.partial(jnp.dot, selector, preferred_element_type=f32)
    return dot(low) + dot(middle) + dot(high)


def net_stage(cpty_dev, dates, first, me, sums, facts, upstream_ref):
    shards = len(sums)
    blocks, rows = upstream_ref.shape
    count = rows // 128
    cpties = shards * cpty_dev
    shift = cpty_dev.bit_length() - 1

    def label(owner):
        owner = owner.astype(jnp.int32)
        return (((owner >> shift) ^ me) << shift) + (owner & (cpty_dev - 1))

    columns = [facts[k].T for k in range(shards)]
    netted = None
    for k in range(shards):
        row = label(facts[k][dates + 1 : dates + 2, :blocks])
        pick = lax.broadcasted_iota(jnp.int32, (cpties, blocks), 0) == row
        part = split_dot(jnp.where(pick, 1.0, 0.0), sums[k][:blocks])
        netted = part if netted is None else netted + part
    column = label(columns[0][:blocks, dates + 1 : dates + 2])
    own = jnp.where(lax.broadcasted_iota(jnp.int32, (blocks, cpties), 1) == column, 1.0, 0.0)
    adjoint, totals = [], []
    for k in range(shards):
        shifted = netted[k * cpty_dev : (k + 1) * cpty_dev] - columns[k][:cpty_dev, dates : dates + 1]
        slope = 0.5 * jnp.tanh(0.5 * shifted) + 0.5
        parts = []
        for t in range(count):
            mass = columns[k][:cpty_dev, first + t : first + t + 1]
            parts.append(slope[:, t * 128 : (t + 1) * 128] * mass)
        adjoint.append(jnp.concatenate(parts, axis=1))
        if k == 0:
            exposed = softplus(shifted)
            for t in range(count):
                totals.append(jnp.sum(exposed[:, t * 128 : (t + 1) * 128], axis=1, keepdims=True))
    upstream_ref[...] = split_dot(own, jnp.concatenate(adjoint, axis=0))
    return totals


def pull_stage(step, state_ref, turned_ref, d_ref, n_ref, upstream_ref, half_ref, total_ref):
    blocks = step // block_width
    half_ref[...] = state_ref[...] * 0.5
    total_ref[...] = jnp.zeros_like(total_ref)

    @pl.loop(0, d_ref.shape[1] // step)
    def _(c):
        lines = pl.ds(pl.multiple_of(c * blocks, blocks), blocks)
        trades = pl.ds(pl.multiple_of(c * step, step), step)
        size_t = 0.5 * n_ref[lines, :].T
        upstream = upstream_ref[lines, :]
        linear = jnp.dot(turned_ref[trades, :], half_ref[...], preferred_element_type=f32)
        parts = []
        for b in range(blocks):
            slope = jnp.tanh(linear[b * block_width : (b + 1) * block_width])
            size = size_t[:, b : b + 1]
            parts.append(((slope * size + size) * upstream[b : b + 1, :]).astype(bf16))
        total_ref[...] += jnp.dot(d_ref[:, trades], jnp.concatenate(parts, axis=0), preferred_element_type=f32)


def write_table(table_ref, totals, first):
    lane = lax.broadcasted_iota(jnp.int32, (totals[0].shape[0], 128), 1)
    table = jnp.zeros(lane.shape, f32)
    for t, total in enumerate(totals):
        table = jnp.where(lane == t, total, table)
    table_ref[first : first + len(totals), :] = table.T[: len(totals)]


def late_pull_kernel(step, shards, cpty_dev, dates, first, me_ref, state_ref, turned_ref, d_ref, n_ref, *refs):
    sums, refs = refs[:shards], refs[shards:]
    exposure_ref, facts_ref, direct_ref, upstream_ref, half_ref, total_ref = refs
    blocks = n_ref.shape[0]
    facts = [part[blocks : blocks + 8, :128] for part in sums]
    for k in range(shards):
        facts_ref[8 * k : 8 * (k + 1), :] = facts[k]
    totals = net_stage(cpty_dev, dates, first, me_ref[0], sums, facts, upstream_ref)
    write_table(exposure_ref, totals, 0)
    pull_stage(step, state_ref, turned_ref, d_ref, n_ref, upstream_ref, half_ref, total_ref)
    paths = direct_ref.shape[1]
    for t in range(direct_ref.shape[0]):
        direct_ref[t] = total_ref[:, t * paths : (t + 1) * paths].T


def early_pull_kernel(step, shards, cpty_dev, me_ref, state_ref, turned_ref, d_ref, n_ref, rho_ref, facts_ref, late_exposure_ref, late_ref, *refs):
    sums, refs = refs[:shards], refs[shards:]
    exposure_ref, refs = refs[0], refs[1:]
    chain, refs = refs[:shards], refs[shards:]
    upstream_ref, half_ref, total_ref, chained_ref = refs
    dates, paths, factors = chained_ref.shape
    early = dates - late_ref.shape[0]
    me = me_ref[0]
    facts = [facts_ref[8 * k : 8 * (k + 1), :] for k in range(shards)]
    totals = net_stage(cpty_dev, dates, 0, me, sums, facts, upstream_ref)
    write_table(exposure_ref, totals, 0)
    exposure_ref[early:dates, :] = late_exposure_ref[...]
    pull_stage(step, state_ref, turned_ref, d_ref, n_ref, upstream_ref, half_ref, total_ref)
    carried = jnp.zeros((paths, factors), f32)
    for t in reversed(range(dates)):
        direct = late_ref[t - early] if t >= early else total_ref[:, t * paths : (t + 1) * paths].T
        adjoint = direct + carried
        chained_ref[t] = adjoint
        carried = rho_ref[t : t + 1, :] * adjoint
    piece = paths // shards
    for k in range(shards):
        at = pl.ds(pl.multiple_of((me ^ k) * piece, piece), piece)
        chain[k][...] = chained_ref[:, at, :]


def pull_cost(rows, trades, factors):
    return pl.CostEstimate(
        flops=4 * rows * trades * factors, bytes_accessed=4 * trades * factors, transcendentals=rows * trades
    )


def pull_scratch(blocks, factors, rows):
    return [pltpu.VMEM((blocks, rows), f32), pltpu.VMEM((factors, rows), bf16), pltpu.VMEM((factors, rows), f32)]


def late_pull_pass(dates, paths, cpty_dev, me, state, turned, d, n, sums):
    factors, rows = state.shape
    trades = d.shape[1]
    shards = len(sums)
    count = rows // paths
    vmem = pl.BlockSpec(memory_space=pltpu.VMEM)
    return pl.pallas_call(
        functools.partial(late_pull_kernel, min(2048, trades), shards, cpty_dev, dates, dates - count),
        in_specs=[pl.BlockSpec(memory_space=pltpu.SMEM)] + [vmem] * (4 + shards),
        out_specs=[vmem] * 3,
        out_shape=[
            jax.ShapeDtypeStruct((count, cpty_dev), f32),
            jax.ShapeDtypeStruct((8 * shards, 128), f32),
            jax.ShapeDtypeStruct((count, paths, factors), f32),
        ],
        scratch_shapes=pull_scratch(n.shape[0], factors, rows),
        compiler_params=pltpu.CompilerParams(vmem_limit_bytes=24 << 20),
        cost_estimate=pull_cost(rows, trades, factors),
        name="late_pull_pass",
    )(me, state, turned, d, n, *sums)


def early_pull_pass(dates, paths, cpty_dev, me, state, turned, d, n, rho, facts, late_exposure, late, sums):
    factors, rows = state.shape
    trades = d.shape[1]
    shards = len(sums)
    piece = paths // shards
    vmem = pl.BlockSpec(memory_space=pltpu.VMEM)
    out = pl.pallas_call(
        functools.partial(early_pull_kernel, min(2048, trades), shards, cpty_dev),
        in_specs=[pl.BlockSpec(memory_space=pltpu.SMEM)] + [vmem] * (8 + shards),
        out_specs=[vmem] * (1 + shards),
        out_shape=[jax.ShapeDtypeStruct((dates, cpty_dev), f32)]
        + [jax.ShapeDtypeStruct((dates, piece, factors), f32)] * shards,
        scratch_shapes=pull_scratch(n.shape[0], factors, rows) + [pltpu.VMEM((dates, paths, factors), f32)],
        compiler_params=pltpu.CompilerParams(vmem_limit_bytes=24 << 20),
        cost_estimate=pull_cost(rows, trades, factors),
        name="early_pull_pass",
    )(me, state, turned, d, n, rho, facts, late_exposure, late, *sums)
    return out[0], out[1:]


def pull_kernel(step, state_ref, turned_ref, d_ref, n_ref, upstream_ref, direct_ref, half_ref, total_ref):
    pull_stage(step, state_ref, turned_ref, d_ref, n_ref, upstream_ref, half_ref, total_ref)
    dates, paths, _ = direct_ref.shape
    for t in range(dates):
        direct_ref[t] = total_ref[:, t * paths : (t + 1) * paths].T


def pull_pass(dates, state, turned, d, n, upstream):
    factors, rows = state.shape
    trades = d.shape[1]
    vmem = pl.BlockSpec(memory_space=pltpu.VMEM)
    return pl.pallas_call(
        functools.partial(pull_kernel, min(2048, trades)),
        in_specs=[vmem] * 5,
        out_specs=vmem,
        out_shape=jax.ShapeDtypeStruct((dates, rows // dates, factors), f32),
        scratch_shapes=pull_scratch(n.shape[0], factors, rows)[1:],
        compiler_params=pltpu.CompilerParams(vmem_limit_bytes=32 << 20),
        name="pull_pass",
    )(state, turned, d, n, upstream)


def place_kernel(shards, me_ref, *refs):
    pieces, out_ref = refs[:shards], refs[shards]
    size = pieces[0].shape[1]
    for k in range(shards):
        at = pl.ds(pl.multiple_of((me_ref[0] ^ k) * size, size), size)
        out_ref[:, at, :] = pieces[k][...]


def place(me, pieces):
    shards = len(pieces)
    dates, size, factors = pieces[0].shape
    whole = lambda *shape: pl.BlockSpec(shape, lambda i, s: (0,) * len(shape))
    return pl.pallas_call(
        functools.partial(place_kernel, shards),
        grid_spec=pltpu.PrefetchScalarGridSpec(
            num_scalar_prefetch=1,
            grid=(1,),
            in_specs=[whole(dates, size, factors)] * shards,
            out_specs=whole(dates, shards * size, factors),
        ),
        out_shape=jax.ShapeDtypeStruct((dates, shards * size, factors), f32),
        compiler_params=pltpu.CompilerParams(vmem_limit_bytes=4 << 20),
        name="place",
    )(me, *pieces)


def local_chain(x, rho):
    carried = x[0]
    gain = rho[0]
    for t in range(1, x.shape[0]):
        carried = rho[t][None, :] * carried + x[t]
        gain = rho[t] * gain
    return gain, carried


def near(x, rho, d, size, obligor, ceiling, mass):
    dates, paths, factors = x.shape
    shards = lax.axis_size("trade")
    cpty_dev = ceiling.shape[0]
    n = size.reshape(-1, block_width)
    me = lax.axis_index("trade").astype(jnp.int32)[None]
    date = lax.axis_index("date").astype(jnp.int32)
    over = lambda value, k: swap(value, ("trade",), (shards,), (k,))

    carried, x, rho_near = chain_pass(x, rho)
    arriving = swap(carried, ("date",), (2,), (1,))
    turned, n, facts = prepare_pass(d, n, mass, ceiling, obligor)
    sums, (late_state, early_state) = first_value_pass(2, x, rho_near, arriving, date[None], facts, turned, n)
    late_sums = [sums] + [over(sums, k) for k in range(1, shards)]
    sums = value_pass(early_state, turned, n)
    early_sums = [sums] + [over(sums, k) for k in range(1, shards)]
    exposure, facts, late = late_pull_pass(dates, paths, cpty_dev, me, late_state, turned, d, n, late_sums)
    exposure, chain = early_pull_pass(
        dates, paths, cpty_dev, me, early_state, turned, d, n, rho_near, facts, exposure, late, early_sums
    )
    total = functools.reduce(jnp.add, [chain[0]] + [over(chain[k], k) for k in range(1, shards)])

    message = swap(rho[0][None, :] * total[0], ("date",), (2,), (1,))
    weights = [jnp.where(date > 0, 0.0, jnp.ones((factors,), f32))]
    for t in reversed(range(1, dates)):
        weights.append(rho[t] * weights[-1])
    own = total + jnp.stack(weights[::-1])[:, None, :] * message[None]
    own, exposure = lax.optimization_barrier((own, exposure))
    pieces = [own] + [over(own, k) for k in range(1, shards)]
    exposure_profile = (exposure + swap(exposure, ("path",), (2,), (1,))) / (paths * lax.axis_size("path"))
    return exposure_profile, place(me, pieces)


def far(x, rho, d, size, obligor, ceiling, mass):
    dates, paths, factors = x.shape
    rows = dates * paths
    cpty_dev = ceiling.shape[0]
    n = size.reshape(-1, block_width)
    value = local_chain(x, rho)
    identity = (jnp.ones_like(value[0]), jnp.zeros_like(value[1]))
    _, arriving = entering(value, "date", compose, identity, False)
    turned, n, facts = prepare_pass(d, n, mass, ceiling, obligor)
    sums, (state,) = first_value_pass(1, x, rho, arriving, jnp.ones((1,), jnp.int32), facts, turned, n)
    sums = sums[: n.shape[0]]
    cpties = cpty_dev * lax.axis_size("trade")
    ownership = (obligor[:, None] == jnp.arange(cpties, dtype=jnp.int32)[None, :]).astype(f32)
    partial = lax.dot_general(ownership, sums, (((0,), (0,)), ((), ())), precision=highest)
    netted = lax.psum_scatter(partial, "trade", scatter_dimension=0, tiled=True)
    shifted = (netted - ceiling[:, None]).reshape(cpty_dev, dates, paths)
    exposure = jnp.sum(jax.nn.softplus(shifted), axis=2).T
    exposure_profile = lax.psum(exposure, "path") / (paths * lax.axis_size("path"))
    adjoint = (mass.T[:, :, None] * jax.nn.sigmoid(shifted)).reshape(cpty_dev, rows)
    gathered = lax.all_gather(adjoint, "trade", axis=0, tiled=True)
    upstream = jnp.dot(ownership, gathered, precision=highest)
    direct = lax.psum(pull_pass(dates, state, turned, d, n, upstream), "trade")

    gain = jnp.ones((factors,), f32)
    message = jnp.zeros((paths, factors), f32)
    for t in reversed(range(dates)):
        message = rho[t][None, :] * (direct[t] + message)
        gain = rho[t] * gain
    _, message = entering((gain, message), "date", compose, identity, True)
    adjoints = []
    for t in reversed(range(dates)):
        adjoint = direct[t] + message
        adjoints.append(adjoint)
        message = rho[t][None, :] * adjoint
    return exposure_profile, jnp.stack(adjoints[::-1])


def solution(mesh):
    close = mesh.shape["date"] == 2 and mesh.shape["trade"] == 4 and mesh.shape["path"] == 2
    return jax.shard_map(
        near if close else far,
        mesh=mesh,
        in_specs=(
            P(("grp", "date"), "path", None),
            P(("grp", "date"), None),
            P(None, ("grp", "trade")),
            P(("grp", "trade")),
            P(("grp", "trade")),
            P(("grp", "trade")),
            P(("grp", "date"), "trade"),
        ),
        out_specs=(P(("grp", "date"), "trade"), P(("grp", "date"), "path", None)),
        check_vma=False,
    )
```

```python
import functools

import jax
import jax.numpy as jnp
from jax import lax
from jax.experimental import pallas as pl
from jax.experimental.pallas import tpu as pltpu
from jax.sharding import PartitionSpec as P

block_width = 128
highest = lax.Precision.HIGHEST
f32 = jnp.float32
bf16 = jnp.bfloat16
VALUE_STEP = 2048


def swap(value, axes, sizes, flips):
    count = 1
    for size in sizes:
        count *= size
    pairs = []
    for flat in range(count):
        rest, target, scale = flat, 0, 1
        for size, flip in zip(reversed(sizes), reversed(flips)):
            target += ((rest % size) ^ flip) * scale
            rest //= size
            scale *= size
        pairs.append((flat, target))
    return lax.ppermute(value, axes, pairs)


def entering(value, axis, combine, identity, reverse):
    length, index = (lax.axis_size(axis), lax.axis_index(axis))
    everything = jax.tree.map(lambda part: lax.all_gather(part, axis), value)
    before = jax.tree.map(
        lambda part, zero: jnp.broadcast_to(jnp.asarray(zero, part.dtype), part.shape),
        value,
        identity,
    )
    for k in range(length):
        at = length - 1 - k if reverse else k
        reached = at > index if reverse else at < index
        new = combine(before, jax.tree.map(lambda part: part[at], everything))
        before = jax.tree.map(lambda a, b: jnp.where(reached, a, b), new, before)
    return before


def compose(earlier, later):
    return (later[0] * earlier[0], later[0] * earlier[1] + later[1])


def softplus(v):
    return jnp.maximum(v, jnp.log(1.0 + jnp.exp(jnp.minimum(v, 80.0))))


def far_copy(*parts):
    return [pltpu.with_memory_space_constraint(part, pltpu.HBM) for part in parts]


def chain_kernel(x_hbm, rho_hbm, carried_ref, x_ref, rho_ref, sems):
    dates = x_ref.shape[0]
    copies = [pltpu.make_async_copy(x_hbm.at[t], x_ref.at[t], sems.at[t]) for t in range(dates)]
    copies.append(pltpu.make_async_copy(rho_hbm, rho_ref, sems.at[dates]))
    for copy in copies:
        copy.start()
    copies[dates].wait()
    copies[0].wait()
    carried = x_ref[0]
    for t in range(1, dates):
        copies[t].wait()
        carried = rho_ref[t : t + 1, :] * carried + x_ref[t]
    carried_ref[...] = carried


def chain_pass(x, rho):
    return pl.pallas_call(
        chain_kernel,
        in_specs=[pl.BlockSpec(memory_space=pltpu.HBM)] * 2,
        out_specs=[pl.BlockSpec(memory_space=pltpu.VMEM)] * 3,
        out_shape=[
            jax.ShapeDtypeStruct(x.shape[1:], f32),
            jax.ShapeDtypeStruct(x.shape, f32),
            jax.ShapeDtypeStruct(rho.shape, f32),
        ],
        scratch_shapes=[pltpu.SemaphoreType.DMA((x.shape[0] + 1,))],
        compiler_params=pltpu.CompilerParams(vmem_limit_bytes=4 << 20),
        name="chain_pass",
    )(*far_copy(x, rho))


def prepare_kernel(step, d_hbm, n_hbm, mass_hbm, ceiling_hbm, obligor_hbm, *refs):
    turned_ref, n_ref, facts_ref, d_ref, mass_ref, ceiling_ref, obligor_ref, sems = refs
    pieces = d_ref.shape[1] // step
    copies = []
    for c in range(pieces):
        part = pl.ds(c * step, step)
        copies.append(pltpu.make_async_copy(d_hbm.at[:, part], d_ref.at[:, part], sems.at[c]))
    small = ((n_hbm, n_ref), (mass_hbm, mass_ref), (ceiling_hbm, ceiling_ref), (obligor_hbm, obligor_ref))
    for k, (source, target) in enumerate(small):
        copies.append(pltpu.make_async_copy(source, target, sems.at[pieces + k]))
    for copy in copies:
        copy.start()
    for c in range(pieces):
        copies[c].wait()
        turned_ref[c * step : (c + 1) * step, :] = d_ref[:, c * step : (c + 1) * step].T
    for copy in copies[pieces:]:
        copy.wait()
    dates, cpties = mass_ref.shape
    facts_ref[...] = jnp.zeros_like(facts_ref)
    facts_ref[:dates, :cpties] = mass_ref[...]
    facts_ref[dates : dates + 1, :cpties] = ceiling_ref[...]
    facts_ref[dates + 1 : dates + 2, : obligor_ref.shape[1]] = obligor_ref[...].astype(f32)


def prepare_pass(d, n, mass, ceiling, obligor):
    factors, trades = d.shape
    step = min(2048, trades)
    hbm = pl.BlockSpec(memory_space=pltpu.HBM)
    vmem = pl.BlockSpec(memory_space=pltpu.VMEM)
    ceiling, obligor = ceiling[None, :], obligor[None, :]
    return pl.pallas_call(
        functools.partial(prepare_kernel, step),
        in_specs=[hbm] * 5,
        out_specs=[vmem] * 3,
        out_shape=[
            jax.ShapeDtypeStruct((trades, factors), bf16),
            jax.ShapeDtypeStruct(n.shape, f32),
            jax.ShapeDtypeStruct((8, 128), f32),
        ],
        scratch_shapes=[
            pltpu.VMEM(d.shape, bf16),
            pltpu.VMEM(mass.shape, f32),
            pltpu.VMEM(ceiling.shape, f32),
            pltpu.VMEM(obligor.shape, jnp.int32),
            pltpu.SemaphoreType.DMA((trades // step + 4,)),
        ],
        compiler_params=pltpu.CompilerParams(vmem_limit_bytes=8 << 20),
        cost_estimate=pl.CostEstimate(flops=0, bytes_accessed=4 * trades * factors, transcendentals=0),
        name="prepare_pass",
    )(*far_copy(d, n, mass, ceiling, obligor))


def value_kernel(step, x_ref, rho_ref, arriving_ref, keep_ref, facts_ref, turned_ref, n_ref, sums_ref, state_ref):
    dates, paths, _ = x_ref.shape
    blocks = step // block_width
    carried = arriving_ref[...] * keep_ref[0].astype(f32)
    for t in range(dates):
        carried = rho_ref[t : t + 1, :] * carried + x_ref[t]
        state_ref[:, t * paths : (t + 1) * paths] = carried.T.astype(bf16)
    sums_ref[n_ref.shape[0] :, :128] = facts_ref[...]

    @pl.loop(0, turned_ref.shape[0] // step)
    def _(c):
        size_t = n_ref[pl.ds(pl.multiple_of(c * blocks, blocks), blocks), :].T
        turned = turned_ref[pl.ds(pl.multiple_of(c * step, step), step), :]
        linear = jnp.dot(turned, state_ref[...], preferred_element_type=f32)
        lines = []
        for b in range(blocks):
            value = softplus(linear[b * block_width : (b + 1) * block_width]) * size_t[:, b : b + 1]
            lines.append(jnp.sum(value, axis=0, keepdims=True))
        sums_ref[pl.ds(pl.multiple_of(c * blocks, blocks), blocks), :] = jnp.concatenate(lines, axis=0)


def value_pass(x, rho, arriving, keep, facts, turned, n):
    dates, paths, factors = x.shape
    rows, trades = dates * paths, turned.shape[0]
    vmem = pl.BlockSpec(memory_space=pltpu.VMEM)
    return pl.pallas_call(
        functools.partial(value_kernel, min(VALUE_STEP, trades)),
        in_specs=[vmem, vmem, vmem, pl.BlockSpec(memory_space=pltpu.SMEM), vmem, vmem, vmem],
        out_specs=[vmem] * 2,
        out_shape=[
            jax.ShapeDtypeStruct((n.shape[0] + 8, rows), f32),
            jax.ShapeDtypeStruct((factors, rows), bf16),
        ],
        compiler_params=pltpu.CompilerParams(vmem_limit_bytes=32 << 20),
        cost_estimate=pl.CostEstimate(
            flops=2 * rows * trades * factors, bytes_accessed=2 * trades * factors, transcendentals=2 * rows * trades
        ),
        name="value_pass",
    )(x, rho, arriving, keep, facts, turned, n)


def slope_kernel(step, state_ref, turned_ref, n_ref, slope_ref, half_ref):
    blocks = step // block_width
    half_ref[...] = state_ref[...] * 0.5

    @pl.loop(0, turned_ref.shape[0] // step)
    def _(c):
        size_t = 0.5 * n_ref[pl.ds(pl.multiple_of(c * blocks, blocks), blocks), :].T
        turned = turned_ref[pl.ds(pl.multiple_of(c * step, step), step), :]
        linear = jnp.dot(turned, half_ref[...], preferred_element_type=f32)
        for b in range(blocks):
            size = size_t[:, b : b + 1]
            slope = jnp.tanh(linear[b * block_width : (b + 1) * block_width]) * size + size
            slope_ref[pl.ds(pl.multiple_of(c * step + b * block_width, block_width), block_width), :] = slope


def slope_pass(state, turned, n):
    factors, rows = state.shape
    trades = turned.shape[0]
    vmem = pl.BlockSpec(memory_space=pltpu.VMEM)
    return pl.pallas_call(
        functools.partial(slope_kernel, min(2048, trades)),
        in_specs=[vmem] * 3,
        out_specs=vmem,
        out_shape=jax.ShapeDtypeStruct((trades, rows), f32),
        scratch_shapes=[pltpu.VMEM((factors, rows), bf16)],
        compiler_params=pltpu.CompilerParams(vmem_limit_bytes=16 << 20),
        cost_estimate=pl.CostEstimate(
            flops=2 * rows * trades * factors, bytes_accessed=4 * trades * rows, transcendentals=rows * trades
        ),
        name="slope_pass",
    )(state, turned, n)


def split_dot(selector, value):
    selector = selector.astype(bf16)
    high = value.astype(bf16)
    rest = value - high.astype(f32)
    middle = rest.astype(bf16)
    low = (rest - middle.astype(f32)).astype(bf16)
    dot = functools.partial(jnp.dot, selector, preferred_element_type=f32)
    return dot(low) + dot(middle) + dot(high)


def net_stage(cpty_dev, dates, me, sums, upstream_ref):
    shards = len(sums)
    blocks, rows = upstream_ref.shape
    paths = rows // dates
    cpties = shards * cpty_dev
    shift = cpty_dev.bit_length() - 1

    def label(owner):
        owner = owner.astype(jnp.int32)
        return (((owner >> shift) ^ me) << shift) + (owner & (cpty_dev - 1))

    columns = [part[blocks : blocks + 8, :128].T for part in sums]
    netted = None
    for k in range(shards):
        row = label(sums[k][blocks + dates + 1 : blocks + dates + 2, :blocks])
        pick = lax.broadcasted_iota(jnp.int32, (cpties, blocks), 0) == row
        part = split_dot(jnp.where(pick, 1.0, 0.0), sums[k][:blocks])
        netted = part if netted is None else netted + part
    column = label(columns[0][:blocks, dates + 1 : dates + 2])
    own = jnp.where(lax.broadcasted_iota(jnp.int32, (blocks, cpties), 1) == column, 1.0, 0.0)
    adjoint, totals = [], []
    for k in range(shards):
        shifted = netted[k * cpty_dev : (k + 1) * cpty_dev] - columns[k][:cpty_dev, dates : dates + 1]
        slope = 0.5 * jnp.tanh(0.5 * shifted) + 0.5
        parts = []
        for t in range(dates):
            parts.append(slope[:, t * paths : (t + 1) * paths] * columns[k][:cpty_dev, t : t + 1])
        adjoint.append(jnp.concatenate(parts, axis=1))
        if k == 0:
            exposed = softplus(shifted)
            for t in range(dates):
                totals.append(jnp.sum(exposed[:, t * paths : (t + 1) * paths], axis=1, keepdims=True))
    upstream_ref[...] = split_dot(own, jnp.concatenate(adjoint, axis=0))
    return totals


def pull_stage(step, slope_ref, d_ref, upstream_ref, total_ref):
    blocks = step // block_width
    total_ref[...] = jnp.zeros_like(total_ref)

    @pl.loop(0, d_ref.shape[1] // step)
    def _(c):
        upstream = upstream_ref[pl.ds(pl.multiple_of(c * blocks, blocks), blocks), :]
        parts = []
        for b in range(blocks):
            slope = slope_ref[pl.ds(pl.multiple_of(c * step + b * block_width, block_width), block_width), :]
            parts.append((slope * upstream[b : b + 1, :]).astype(bf16))
        trades = pl.ds(pl.multiple_of(c * step, step), step)
        total_ref[...] += jnp.dot(d_ref[:, trades], jnp.concatenate(parts, axis=0), preferred_element_type=f32)


def net_pull_kernel(step, cpty_dev, shards, me_ref, slope_ref, d_ref, rho_ref, *refs):
    sums, refs = refs[:shards], refs[shards:]
    exposure_ref, refs = refs[0], refs[1:]
    chain, refs = refs[:shards], refs[shards:]
    upstream_ref, total_ref, chained_ref = refs
    dates, paths, factors = chained_ref.shape
    me = me_ref[0]
    totals = net_stage(cpty_dev, dates, me, sums, upstream_ref)
    lane = lax.broadcasted_iota(jnp.int32, (cpty_dev, 128), 1)
    table = jnp.zeros(lane.shape, f32)
    for t, total in enumerate(totals):
        table = jnp.where(lane == t, total, table)
    exposure_ref[...] = table.T[:dates]
    pull_stage(step, slope_ref, d_ref, upstream_ref, total_ref)
    carried = jnp.zeros((paths, factors), f32)
    for t in reversed(range(dates)):
        adjoint = total_ref[:, t * paths : (t + 1) * paths].T + carried
        chained_ref[t] = adjoint
        carried = rho_ref[t : t + 1, :] * adjoint
    piece = paths // shards
    for k in range(shards):
        at = pl.ds(pl.multiple_of((me ^ k) * piece, piece), piece)
        chain[k][...] = chained_ref[:, at, :]


def net_pull_pass(dates, cpty_dev, me, slope, d, rho, sums):
    trades, rows = slope.shape
    factors = d.shape[0]
    paths = rows // dates
    shards = len(sums)
    piece = paths // shards
    vmem = pl.BlockSpec(memory_space=pltpu.VMEM)
    out = pl.pallas_call(
        functools.partial(net_pull_kernel, min(2048, trades), cpty_dev, shards),
        in_specs=[pl.BlockSpec(memory_space=pltpu.SMEM)] + [vmem] * (3 + shards),
        out_specs=[vmem] * (1 + shards),
        out_shape=[jax.ShapeDtypeStruct((dates, cpty_dev), f32)]
        + [jax.ShapeDtypeStruct((dates, piece, factors), f32)] * shards,
        scratch_shapes=[
            pltpu.VMEM((trades // block_width, rows), f32),
            pltpu.VMEM((factors, rows), f32),
            pltpu.VMEM((dates, paths, factors), f32),
        ],
        compiler_params=pltpu.CompilerParams(vmem_limit_bytes=16 << 20),
        cost_estimate=pl.CostEstimate(
            flops=2 * rows * trades * factors, bytes_accessed=4 * trades * rows, transcendentals=0
        ),
        name="net_pull_pass",
    )(me, slope, d, rho, *sums)
    return out[0], out[1:]


def pull_kernel(step, slope_ref, d_ref, upstream_ref, direct_ref, total_ref):
    pull_stage(step, slope_ref, d_ref, upstream_ref, total_ref)
    dates, paths, _ = direct_ref.shape
    for t in range(dates):
        direct_ref[t] = total_ref[:, t * paths : (t + 1) * paths].T


def pull_pass(dates, slope, d, upstream):
    trades, rows = slope.shape
    factors = d.shape[0]
    vmem = pl.BlockSpec(memory_space=pltpu.VMEM)
    return pl.pallas_call(
        functools.partial(pull_kernel, min(2048, trades)),
        in_specs=[vmem] * 3,
        out_specs=vmem,
        out_shape=jax.ShapeDtypeStruct((dates, rows // dates, factors), f32),
        scratch_shapes=[pltpu.VMEM((factors, rows), f32)],
        compiler_params=pltpu.CompilerParams(vmem_limit_bytes=16 << 20),
        name="pull_pass",
    )(slope, d, upstream)


def place_kernel(shards, me_ref, *refs):
    pieces, out_ref = refs[:shards], refs[shards]
    size = pieces[0].shape[1]
    for k in range(shards):
        at = pl.ds(pl.multiple_of((me_ref[0] ^ k) * size, size), size)
        out_ref[:, at, :] = pieces[k][...]


def place(me, pieces):
    shards = len(pieces)
    dates, size, factors = pieces[0].shape
    whole = lambda *shape: pl.BlockSpec(shape, lambda i, s: (0,) * len(shape))
    return pl.pallas_call(
        functools.partial(place_kernel, shards),
        grid_spec=pltpu.PrefetchScalarGridSpec(
            num_scalar_prefetch=1,
            grid=(1,),
            in_specs=[whole(dates, size, factors)] * shards,
            out_specs=whole(dates, shards * size, factors),
        ),
        out_shape=jax.ShapeDtypeStruct((dates, shards * size, factors), f32),
        compiler_params=pltpu.CompilerParams(vmem_limit_bytes=4 << 20),
        name="place",
    )(me, *pieces)


def local_chain(x, rho):
    carried = x[0]
    gain = rho[0]
    for t in range(1, x.shape[0]):
        carried = rho[t][None, :] * carried + x[t]
        gain = rho[t] * gain
    return gain, carried


def near(x, rho, d, size, obligor, ceiling, mass):
    dates, paths, factors = x.shape
    shards = lax.axis_size("trade")
    cpty_dev = ceiling.shape[0]
    n = size.reshape(-1, block_width)
    me = lax.axis_index("trade").astype(jnp.int32)[None]
    date = lax.axis_index("date").astype(jnp.int32)
    over = lambda value, k: swap(value, ("trade",), (shards,), (k,))

    carried, x, rho_near = chain_pass(x, rho)
    arriving = swap(carried, ("date",), (2,), (1,))
    turned, n, facts = prepare_pass(d, n, mass, ceiling, obligor)
    sums, state = value_pass(x, rho_near, arriving, date[None], facts, turned, n)
    sums = [sums] + [over(sums, k) for k in range(1, shards)]
    slope = slope_pass(state, turned, n)
    exposure, chain = net_pull_pass(dates, cpty_dev, me, slope, d, rho_near, sums)
    total = functools.reduce(jnp.add, [chain[0]] + [over(chain[k], k) for k in range(1, shards)])

    message = swap(rho[0][None, :] * total[0], ("date",), (2,), (1,))
    weights = [jnp.where(date > 0, 0.0, jnp.ones((factors,), f32))]
    for t in reversed(range(1, dates)):
        weights.append(rho[t] * weights[-1])
    own = total + jnp.stack(weights[::-1])[:, None, :] * message[None]
    own, exposure = lax.optimization_barrier((own, exposure))
    pieces = [own] + [over(own, k) for k in range(1, shards)]
    exposure_profile = (exposure + swap(exposure, ("path",), (2,), (1,))) / (paths * lax.axis_size("path"))
    return exposure_profile, place(me, pieces)


def far(x, rho, d, size, obligor, ceiling, mass):
    dates, paths, factors = x.shape
    rows = dates * paths
    cpty_dev = ceiling.shape[0]
    n = size.reshape(-1, block_width)
    value = local_chain(x, rho)
    identity = (jnp.ones_like(value[0]), jnp.zeros_like(value[1]))
    _, arriving = entering(value, "date", compose, identity, False)
    turned, n, facts = prepare_pass(d, n, mass, ceiling, obligor)
    sums, state = value_pass(x, rho, arriving, jnp.ones((1,), jnp.int32), facts, turned, n)
    sums = sums[: n.shape[0]]
    cpties = cpty_dev * lax.axis_size("trade")
    ownership = (obligor[:, None] == jnp.arange(cpties, dtype=jnp.int32)[None, :]).astype(f32)
    partial = lax.dot_general(ownership, sums, (((0,), (0,)), ((), ())), precision=highest)
    netted = lax.psum_scatter(partial, "trade", scatter_dimension=0, tiled=True)
    shifted = (netted - ceiling[:, None]).reshape(cpty_dev, dates, paths)
    exposure = jnp.sum(jax.nn.softplus(shifted), axis=2).T
    exposure_profile = lax.psum(exposure, "path") / (paths * lax.axis_size("path"))
    adjoint = (mass.T[:, :, None] * jax.nn.sigmoid(shifted)).reshape(cpty_dev, rows)
    gathered = lax.all_gather(adjoint, "trade", axis=0, tiled=True)
    upstream = jnp.dot(ownership, gathered, precision=highest)
    direct = lax.psum(pull_pass(dates, slope_pass(state, turned, n), d, upstream), "trade")

    gain = jnp.ones((factors,), f32)
    message = jnp.zeros((paths, factors), f32)
    for t in reversed(range(dates)):
        message = rho[t][None, :] * (direct[t] + message)
        gain = rho[t] * gain
    _, message = entering((gain, message), "date", compose, identity, True)
    adjoints = []
    for t in reversed(range(dates)):
        adjoint = direct[t] + message
        adjoints.append(adjoint)
        message = rho[t][None, :] * adjoint
    return exposure_profile, jnp.stack(adjoints[::-1])


def solution(mesh):
    close = mesh.shape["date"] == 2 and mesh.shape["trade"] == 4 and mesh.shape["path"] == 2
    return jax.shard_map(
        near if close else far,
        mesh=mesh,
        in_specs=(
            P(("grp", "date"), "path", None),
            P(("grp", "date"), None),
            P(None, ("grp", "trade")),
            P(("grp", "trade")),
            P(("grp", "trade")),
            P(("grp", "trade")),
            P(("grp", "date"), "trade"),
        ),
        out_specs=(P(("grp", "date"), "trade"), P(("grp", "date"), "path", None)),
        check_vma=False,
    )
```

```python
import functools

import jax
import jax.numpy as jnp
from jax import lax
from jax.experimental import pallas as pl
from jax.experimental.pallas import tpu as pltpu
from jax.sharding import PartitionSpec as P

block_width = 128
highest = lax.Precision.HIGHEST
f32 = jnp.float32
bf16 = jnp.bfloat16
VALUE_STEP = 2048
SUMS_ORDER = (0, 3, 1, 2)
PLACE_ORDER = (0, 1, 3, 2)


def swap(value, axes, sizes, flips):
    count = 1
    for size in sizes:
        count *= size
    pairs = []
    for flat in range(count):
        rest, target, scale = flat, 0, 1
        for size, flip in zip(reversed(sizes), reversed(flips)):
            target += ((rest % size) ^ flip) * scale
            rest //= size
            scale *= size
        pairs.append((flat, target))
    return lax.ppermute(value, axes, pairs)


def entering(value, axis, combine, identity, reverse):
    length, index = (lax.axis_size(axis), lax.axis_index(axis))
    everything = jax.tree.map(lambda part: lax.all_gather(part, axis), value)
    before = jax.tree.map(
        lambda part, zero: jnp.broadcast_to(jnp.asarray(zero, part.dtype), part.shape),
        value,
        identity,
    )
    for k in range(length):
        at = length - 1 - k if reverse else k
        reached = at > index if reverse else at < index
        new = combine(before, jax.tree.map(lambda part: part[at], everything))
        before = jax.tree.map(lambda a, b: jnp.where(reached, a, b), new, before)
    return before


def compose(earlier, later):
    return (later[0] * earlier[0], later[0] * earlier[1] + later[1])


def softplus(v):
    return jnp.maximum(v, jnp.log(1.0 + jnp.exp(jnp.minimum(v, 80.0))))


def far_copy(*parts):
    return [pltpu.with_memory_space_constraint(part, pltpu.HBM) for part in parts]


def chain_kernel(x_hbm, rho_hbm, carried_ref, x_ref, rho_ref, sems):
    dates = x_ref.shape[0]
    copies = [pltpu.make_async_copy(x_hbm.at[t], x_ref.at[t], sems.at[t]) for t in range(dates)]
    copies.append(pltpu.make_async_copy(rho_hbm, rho_ref, sems.at[dates]))
    for copy in copies:
        copy.start()
    copies[dates].wait()
    copies[0].wait()
    carried = x_ref[0]
    for t in range(1, dates):
        copies[t].wait()
        carried = rho_ref[t : t + 1, :] * carried + x_ref[t]
    carried_ref[...] = carried


def chain_pass(x, rho):
    return pl.pallas_call(
        chain_kernel,
        in_specs=[pl.BlockSpec(memory_space=pltpu.HBM)] * 2,
        out_specs=[pl.BlockSpec(memory_space=pltpu.VMEM)] * 3,
        out_shape=[
            jax.ShapeDtypeStruct(x.shape[1:], f32),
            jax.ShapeDtypeStruct(x.shape, f32),
            jax.ShapeDtypeStruct(rho.shape, f32),
        ],
        scratch_shapes=[pltpu.SemaphoreType.DMA((x.shape[0] + 1,))],
        compiler_params=pltpu.CompilerParams(vmem_limit_bytes=4 << 20),
        name="chain_pass",
    )(*far_copy(x, rho))


def prepare_kernel(step, d_hbm, n_hbm, mass_hbm, ceiling_hbm, obligor_hbm, *refs):
    turned_ref, n_ref, facts_ref, d_ref, mass_ref, ceiling_ref, obligor_ref, sems = refs
    pieces = d_ref.shape[1] // step
    copies = []
    for c in range(pieces):
        part = pl.ds(c * step, step)
        copies.append(pltpu.make_async_copy(d_hbm.at[:, part], d_ref.at[:, part], sems.at[c]))
    small = ((n_hbm, n_ref), (mass_hbm, mass_ref), (ceiling_hbm, ceiling_ref), (obligor_hbm, obligor_ref))
    for k, (source, target) in enumerate(small):
        copies.append(pltpu.make_async_copy(source, target, sems.at[pieces + k]))
    for copy in copies:
        copy.start()
    for c in range(pieces):
        copies[c].wait()
        turned_ref[c * step : (c + 1) * step, :] = d_ref[:, c * step : (c + 1) * step].T
    for copy in copies[pieces:]:
        copy.wait()
    dates, cpties = mass_ref.shape
    facts_ref[...] = jnp.zeros_like(facts_ref)
    facts_ref[:dates, :cpties] = mass_ref[...]
    facts_ref[dates : dates + 1, :cpties] = ceiling_ref[...]
    facts_ref[dates + 1 : dates + 2, : obligor_ref.shape[1]] = obligor_ref[...].astype(f32)


def prepare_pass(d, n, mass, ceiling, obligor):
    factors, trades = d.shape
    step = min(2048, trades)
    hbm = pl.BlockSpec(memory_space=pltpu.HBM)
    vmem = pl.BlockSpec(memory_space=pltpu.VMEM)
    ceiling, obligor = ceiling[None, :], obligor[None, :]
    return pl.pallas_call(
        functools.partial(prepare_kernel, step),
        in_specs=[hbm] * 5,
        out_specs=[vmem] * 3,
        out_shape=[
            jax.ShapeDtypeStruct((trades, factors), bf16),
            jax.ShapeDtypeStruct(n.shape, f32),
            jax.ShapeDtypeStruct((8, 128), f32),
        ],
        scratch_shapes=[
            pltpu.VMEM(d.shape, bf16),
            pltpu.VMEM(mass.shape, f32),
            pltpu.VMEM(ceiling.shape, f32),
            pltpu.VMEM(obligor.shape, jnp.int32),
            pltpu.SemaphoreType.DMA((trades // step + 4,)),
        ],
        compiler_params=pltpu.CompilerParams(vmem_limit_bytes=8 << 20),
        cost_estimate=pl.CostEstimate(flops=0, bytes_accessed=4 * trades * factors, transcendentals=0),
        name="prepare_pass",
    )(*far_copy(d, n, mass, ceiling, obligor))


def value_kernel(step, x_ref, rho_ref, arriving_ref, keep_ref, facts_ref, turned_ref, n_ref, sums_ref, state_ref):
    dates, paths, _ = x_ref.shape
    blocks = step // block_width
    carried = arriving_ref[...] * keep_ref[0].astype(f32)
    for t in range(dates):
        carried = rho_ref[t : t + 1, :] * carried + x_ref[t]
        state_ref[:, t * paths : (t + 1) * paths] = carried.T.astype(bf16)
    total = n_ref.shape[0]
    tiles = state_ref.shape[1] // 128
    sums_ref[tiles * total :, :] = facts_ref[...]

    @pl.loop(0, turned_ref.shape[0] // step)
    def _(c):
        size_t = n_ref[pl.ds(pl.multiple_of(c * blocks, blocks), blocks), :].T
        turned = turned_ref[pl.ds(pl.multiple_of(c * step, step), step), :]
        linear = jnp.dot(turned, state_ref[...], preferred_element_type=f32)
        lines = []
        for b in range(blocks):
            value = softplus(linear[b * block_width : (b + 1) * block_width]) * size_t[:, b : b + 1]
            lines.append(jnp.sum(value, axis=0, keepdims=True))
        sums = jnp.concatenate(lines, axis=0)
        for q in range(tiles):
            at = pl.ds(pl.multiple_of(q * total + c * blocks, blocks), blocks)
            sums_ref[at, :] = sums[:, q * 128 : (q + 1) * 128]


def value_pass(x, rho, arriving, keep, facts, turned, n):
    dates, paths, factors = x.shape
    rows, trades = dates * paths, turned.shape[0]
    vmem = pl.BlockSpec(memory_space=pltpu.VMEM)
    return pl.pallas_call(
        functools.partial(value_kernel, min(VALUE_STEP, trades)),
        in_specs=[vmem, vmem, vmem, pl.BlockSpec(memory_space=pltpu.SMEM), vmem, vmem, vmem],
        out_specs=[vmem] * 2,
        out_shape=[
            jax.ShapeDtypeStruct((rows // 128 * n.shape[0] + 8, 128), f32),
            jax.ShapeDtypeStruct((factors, rows), bf16),
        ],
        compiler_params=pltpu.CompilerParams(vmem_limit_bytes=32 << 20),
        cost_estimate=pl.CostEstimate(
            flops=2 * rows * trades * factors, bytes_accessed=2 * trades * factors, transcendentals=2 * rows * trades
        ),
        name="value_pass",
    )(x, rho, arriving, keep, facts, turned, n)


def slope_kernel(step, state_ref, turned_ref, n_ref, slope_ref, half_ref):
    blocks = step // block_width
    half_ref[...] = state_ref[...] * 0.5

    @pl.loop(0, turned_ref.shape[0] // step)
    def _(c):
        size_t = 0.5 * n_ref[pl.ds(pl.multiple_of(c * blocks, blocks), blocks), :].T
        turned = turned_ref[pl.ds(pl.multiple_of(c * step, step), step), :]
        linear = jnp.dot(turned, half_ref[...], preferred_element_type=f32)
        for b in range(blocks):
            size = size_t[:, b : b + 1]
            slope = jnp.tanh(linear[b * block_width : (b + 1) * block_width]) * size + size
            slope_ref[pl.ds(pl.multiple_of(c * step + b * block_width, block_width), block_width), :] = slope


def slope_pass(state, turned, n):
    factors, rows = state.shape
    trades = turned.shape[0]
    vmem = pl.BlockSpec(memory_space=pltpu.VMEM)
    return pl.pallas_call(
        functools.partial(slope_kernel, min(2048, trades)),
        in_specs=[vmem] * 3,
        out_specs=vmem,
        out_shape=jax.ShapeDtypeStruct((trades, rows), f32),
        scratch_shapes=[pltpu.VMEM((factors, rows), bf16)],
        compiler_params=pltpu.CompilerParams(vmem_limit_bytes=16 << 20),
        cost_estimate=pl.CostEstimate(
            flops=2 * rows * trades * factors, bytes_accessed=4 * trades * rows, transcendentals=rows * trades
        ),
        name="slope_pass",
    )(state, turned, n)


def split_dot(selector, value):
    selector = selector.astype(bf16)
    high = value.astype(bf16)
    rest = value - high.astype(f32)
    middle = rest.astype(bf16)
    low = (rest - middle.astype(f32)).astype(bf16)
    dot = functools.partial(jnp.dot, selector, preferred_element_type=f32)
    return dot(low) + dot(middle) + dot(high)


def net_stage(cpty_dev, dates, me, sums, upstream_ref):
    shards = len(sums)
    blocks, rows = upstream_ref.shape
    paths = rows // dates
    cpties = shards * cpty_dev
    shift = cpty_dev.bit_length() - 1

    def label(owner):
        owner = owner.astype(jnp.int32)
        return (((owner >> shift) ^ me) << shift) + (owner & (cpty_dev - 1))

    tiles = rows // 128
    last = tiles * blocks
    columns = [part[last:, :].T for part in sums]
    netted = None
    for k in range(shards):
        row = label(sums[k][last + dates + 1 : last + dates + 2, :blocks])
        pick = lax.broadcasted_iota(jnp.int32, (cpties, blocks), 0) == row
        slabs = [sums[k][q * blocks : (q + 1) * blocks] for q in range(tiles)]
        part = split_dot(jnp.where(pick, 1.0, 0.0), jnp.concatenate(slabs, axis=1))
        netted = part if netted is None else netted + part
    column = label(columns[0][:blocks, dates + 1 : dates + 2])
    own = jnp.where(lax.broadcasted_iota(jnp.int32, (blocks, cpties), 1) == column, 1.0, 0.0)
    adjoint, totals = [], []
    for k in range(shards):
        shifted = netted[k * cpty_dev : (k + 1) * cpty_dev] - columns[k][:cpty_dev, dates : dates + 1]
        slope = 0.5 * jnp.tanh(0.5 * shifted) + 0.5
        parts = []
        for t in range(dates):
            parts.append(slope[:, t * paths : (t + 1) * paths] * columns[k][:cpty_dev, t : t + 1])
        adjoint.append(jnp.concatenate(parts, axis=1))
        if k == 0:
            exposed = softplus(shifted)
            for t in range(dates):
                totals.append(jnp.sum(exposed[:, t * paths : (t + 1) * paths], axis=1, keepdims=True))
    upstream_ref[...] = split_dot(own, jnp.concatenate(adjoint, axis=0))
    return totals


def pull_stage(step, slope_ref, d_ref, upstream_ref, total_ref):
    blocks = step // block_width
    total_ref[...] = jnp.zeros_like(total_ref)

    @pl.loop(0, d_ref.shape[1] // step)
    def _(c):
        upstream = upstream_ref[pl.ds(pl.multiple_of(c * blocks, blocks), blocks), :]
        parts = []
        for b in range(blocks):
            slope = slope_ref[pl.ds(pl.multiple_of(c * step + b * block_width, block_width), block_width), :]
            parts.append((slope * upstream[b : b + 1, :]).astype(bf16))
        trades = pl.ds(pl.multiple_of(c * step, step), step)
        total_ref[...] += jnp.dot(d_ref[:, trades], jnp.concatenate(parts, axis=0), preferred_element_type=f32)


def net_pull_kernel(step, cpty_dev, shards, me_ref, slope_ref, d_ref, rho_ref, *refs):
    sums, refs = [refs[SUMS_ORDER.index(k)] for k in range(shards)], refs[shards:]
    exposure_ref, refs = refs[0], refs[1:]
    chain, refs = refs[:shards], refs[shards:]
    upstream_ref, total_ref, chained_ref = refs
    dates, paths, factors = chained_ref.shape
    me = me_ref[0]
    totals = net_stage(cpty_dev, dates, me, sums, upstream_ref)
    lane = lax.broadcasted_iota(jnp.int32, (cpty_dev, 128), 1)
    table = jnp.zeros(lane.shape, f32)
    for t, total in enumerate(totals):
        table = jnp.where(lane == t, total, table)
    exposure_ref[...] = table.T[:dates]
    pull_stage(step, slope_ref, d_ref, upstream_ref, total_ref)
    carried = jnp.zeros((paths, factors), f32)
    for t in reversed(range(dates)):
        adjoint = total_ref[:, t * paths : (t + 1) * paths].T + carried
        chained_ref[t] = adjoint
        carried = rho_ref[t : t + 1, :] * adjoint
    piece = paths // shards
    for k in range(shards):
        at = pl.ds(pl.multiple_of((me ^ k) * piece, piece), piece)
        chain[k][...] = chained_ref[:, at, :]


def net_pull_pass(dates, cpty_dev, me, slope, d, rho, sums):
    trades, rows = slope.shape
    factors = d.shape[0]
    paths = rows // dates
    shards = len(sums)
    piece = paths // shards
    vmem = pl.BlockSpec(memory_space=pltpu.VMEM)
    out = pl.pallas_call(
        functools.partial(net_pull_kernel, min(2048, trades), cpty_dev, shards),
        in_specs=[pl.BlockSpec(memory_space=pltpu.SMEM)] + [vmem] * (3 + shards),
        out_specs=[vmem] * (1 + shards),
        out_shape=[jax.ShapeDtypeStruct((dates, cpty_dev), f32)]
        + [jax.ShapeDtypeStruct((dates, piece, factors), f32)] * shards,
        scratch_shapes=[
            pltpu.VMEM((trades // block_width, rows), f32),
            pltpu.VMEM((factors, rows), f32),
            pltpu.VMEM((dates, paths, factors), f32),
        ],
        compiler_params=pltpu.CompilerParams(vmem_limit_bytes=16 << 20),
        cost_estimate=pl.CostEstimate(
            flops=2 * rows * trades * factors, bytes_accessed=4 * trades * rows, transcendentals=0
        ),
        name="net_pull_pass",
    )(me, slope, d, rho, *[sums[k] for k in SUMS_ORDER])
    return out[0], out[1:]


def pull_kernel(step, slope_ref, d_ref, upstream_ref, direct_ref, total_ref):
    pull_stage(step, slope_ref, d_ref, upstream_ref, total_ref)
    dates, paths, _ = direct_ref.shape
    for t in range(dates):
        direct_ref[t] = total_ref[:, t * paths : (t + 1) * paths].T


def pull_pass(dates, slope, d, upstream):
    trades, rows = slope.shape
    factors = d.shape[0]
    vmem = pl.BlockSpec(memory_space=pltpu.VMEM)
    return pl.pallas_call(
        functools.partial(pull_kernel, min(2048, trades)),
        in_specs=[vmem] * 3,
        out_specs=vmem,
        out_shape=jax.ShapeDtypeStruct((dates, rows // dates, factors), f32),
        scratch_shapes=[pltpu.VMEM((factors, rows), f32)],
        compiler_params=pltpu.CompilerParams(vmem_limit_bytes=16 << 20),
        name="pull_pass",
    )(slope, d, upstream)


def place_kernel(shards, me_ref, *refs):
    pieces, out_ref = [refs[PLACE_ORDER.index(k)] for k in range(shards)], refs[shards]
    size = pieces[0].shape[1]
    for k in range(shards):
        at = pl.ds(pl.multiple_of((me_ref[0] ^ k) * size, size), size)
        out_ref[:, at, :] = pieces[k][...]


def place(me, pieces):
    shards = len(pieces)
    dates, size, factors = pieces[0].shape
    whole = lambda *shape: pl.BlockSpec(shape, lambda i, s: (0,) * len(shape))
    return pl.pallas_call(
        functools.partial(place_kernel, shards),
        grid_spec=pltpu.PrefetchScalarGridSpec(
            num_scalar_prefetch=1,
            grid=(1,),
            in_specs=[whole(dates, size, factors)] * shards,
            out_specs=whole(dates, shards * size, factors),
        ),
        out_shape=jax.ShapeDtypeStruct((dates, shards * size, factors), f32),
        compiler_params=pltpu.CompilerParams(vmem_limit_bytes=4 << 20),
        name="place",
    )(me, *[pieces[k] for k in PLACE_ORDER])


def local_chain(x, rho):
    carried = x[0]
    gain = rho[0]
    for t in range(1, x.shape[0]):
        carried = rho[t][None, :] * carried + x[t]
        gain = rho[t] * gain
    return gain, carried


def near(x, rho, d, size, obligor, ceiling, mass):
    dates, paths, factors = x.shape
    shards = lax.axis_size("trade")
    cpty_dev = ceiling.shape[0]
    n = size.reshape(-1, block_width)
    me = lax.axis_index("trade").astype(jnp.int32)[None]
    date = lax.axis_index("date").astype(jnp.int32)
    over = lambda value, k: swap(value, ("trade",), (shards,), (k,))

    carried, x, rho_near = chain_pass(x, rho)
    def spread(value):
        return [value] + [over(value, k) for k in range(1, shards)]

    carried, x, rho_near = chain_pass(x, rho)
    arriving = swap(carried, ("date",), (2,), (1,))
    turned, n, facts = prepare_pass(d, n, mass, ceiling, obligor)
    sums, state = value_pass(x, rho_near, arriving, date[None], facts, turned, n)
    sums = spread(sums)
    slope = slope_pass(state, turned, n)
    exposure, chain = net_pull_pass(dates, cpty_dev, me, slope, d, rho_near, sums)
    total = chain[0] + over(chain[3], 3) + over(chain[2], 2) + over(chain[1], 1)

    message = swap(rho[0][None, :] * total[0], ("date",), (2,), (1,))
    weights = [jnp.where(date > 0, 0.0, jnp.ones((factors,), f32))]
    for t in reversed(range(1, dates)):
        weights.append(rho[t] * weights[-1])
    own = total + jnp.stack(weights[::-1])[:, None, :] * message[None]
    own, exposure = lax.optimization_barrier((own, exposure))
    pieces = spread(own)
    exposure_profile = (exposure + swap(exposure, ("path",), (2,), (1,))) / (paths * lax.axis_size("path"))
    return exposure_profile, place(me, pieces)


def far(x, rho, d, size, obligor, ceiling, mass):
    dates, paths, factors = x.shape
    rows = dates * paths
    cpty_dev = ceiling.shape[0]
    n = size.reshape(-1, block_width)
    value = local_chain(x, rho)
    identity = (jnp.ones_like(value[0]), jnp.zeros_like(value[1]))
    _, arriving = entering(value, "date", compose, identity, False)
    turned, n, facts = prepare_pass(d, n, mass, ceiling, obligor)
    sums, state = value_pass(x, rho, arriving, jnp.ones((1,), jnp.int32), facts, turned, n)
    tiles = rows // 128
    sums = sums[:-8].reshape(tiles, n.shape[0], 128).transpose(1, 0, 2).reshape(n.shape[0], rows)
    cpties = cpty_dev * lax.axis_size("trade")
    ownership = (obligor[:, None] == jnp.arange(cpties, dtype=jnp.int32)[None, :]).astype(f32)
    partial = lax.dot_general(ownership, sums, (((0,), (0,)), ((), ())), precision=highest)
    netted = lax.psum_scatter(partial, "trade", scatter_dimension=0, tiled=True)
    shifted = (netted - ceiling[:, None]).reshape(cpty_dev, dates, paths)
    exposure = jnp.sum(jax.nn.softplus(shifted), axis=2).T
    exposure_profile = lax.psum(exposure, "path") / (paths * lax.axis_size("path"))
    adjoint = (mass.T[:, :, None] * jax.nn.sigmoid(shifted)).reshape(cpty_dev, rows)
    gathered = lax.all_gather(adjoint, "trade", axis=0, tiled=True)
    upstream = jnp.dot(ownership, gathered, precision=highest)
    direct = lax.psum(pull_pass(dates, slope_pass(state, turned, n), d, upstream), "trade")

    gain = jnp.ones((factors,), f32)
    message = jnp.zeros((paths, factors), f32)
    for t in reversed(range(dates)):
        message = rho[t][None, :] * (direct[t] + message)
        gain = rho[t] * gain
    _, message = entering((gain, message), "date", compose, identity, True)
    adjoints = []
    for t in reversed(range(dates)):
        adjoint = direct[t] + message
        adjoints.append(adjoint)
        message = rho[t][None, :] * adjoint
    return exposure_profile, jnp.stack(adjoints[::-1])


def solution(mesh):
    close = mesh.shape["date"] == 2 and mesh.shape["trade"] == 4 and mesh.shape["path"] == 2
    return jax.shard_map(
        near if close else far,
        mesh=mesh,
        in_specs=(
            P(("grp", "date"), "path", None),
            P(("grp", "date"), None),
            P(None, ("grp", "trade")),
            P(("grp", "trade")),
            P(("grp", "trade")),
            P(("grp", "trade")),
            P(("grp", "date"), "trade"),
        ),
        out_specs=(P(("grp", "date"), "trade"), P(("grp", "date"), "path", None)),
        check_vma=False,
    )
```

```python
import functools

import jax
import jax.numpy as jnp
from jax import lax
from jax.experimental import pallas as pl
from jax.experimental.pallas import tpu as pltpu
from jax.sharding import PartitionSpec as P

block_width = 128
highest = lax.Precision.HIGHEST
f32 = jnp.float32
bf16 = jnp.bfloat16
VALUE_STEP = 2048
SUMS_ORDER = (0, 3, 1, 2)
PLACE_ORDER = (0, 2, 1, 3)


def swap(value, axes, sizes, flips):
    count = 1
    for size in sizes:
        count *= size
    pairs = []
    for flat in range(count):
        rest, target, scale = flat, 0, 1
        for size, flip in zip(reversed(sizes), reversed(flips)):
            target += ((rest % size) ^ flip) * scale
            rest //= size
            scale *= size
        pairs.append((flat, target))
    return lax.ppermute(value, axes, pairs)


def entering(value, axis, combine, identity, reverse):
    length, index = (lax.axis_size(axis), lax.axis_index(axis))
    everything = jax.tree.map(lambda part: lax.all_gather(part, axis), value)
    before = jax.tree.map(
        lambda part, zero: jnp.broadcast_to(jnp.asarray(zero, part.dtype), part.shape),
        value,
        identity,
    )
    for k in range(length):
        at = length - 1 - k if reverse else k
        reached = at > index if reverse else at < index
        new = combine(before, jax.tree.map(lambda part: part[at], everything))
        before = jax.tree.map(lambda a, b: jnp.where(reached, a, b), new, before)
    return before


def compose(earlier, later):
    return (later[0] * earlier[0], later[0] * earlier[1] + later[1])


def softplus(v):
    return jnp.maximum(v, jnp.log(1.0 + jnp.exp(jnp.minimum(v, 80.0))))


def far_copy(*parts):
    return [pltpu.with_memory_space_constraint(part, pltpu.HBM) for part in parts]


def chain_kernel(x_hbm, rho_hbm, carried_ref, x_ref, rho_ref, sems):
    dates = x_ref.shape[0]
    copies = [pltpu.make_async_copy(x_hbm.at[t], x_ref.at[t], sems.at[t]) for t in range(dates)]
    copies.append(pltpu.make_async_copy(rho_hbm, rho_ref, sems.at[dates]))
    for copy in copies:
        copy.start()
    copies[dates].wait()
    copies[0].wait()
    carried = x_ref[0]
    for t in range(1, dates):
        copies[t].wait()
        carried = rho_ref[t : t + 1, :] * carried + x_ref[t]
    carried_ref[...] = carried


def chain_pass(x, rho):
    return pl.pallas_call(
        chain_kernel,
        in_specs=[pl.BlockSpec(memory_space=pltpu.HBM)] * 2,
        out_specs=[pl.BlockSpec(memory_space=pltpu.VMEM)] * 3,
        out_shape=[
            jax.ShapeDtypeStruct(x.shape[1:], f32),
            jax.ShapeDtypeStruct(x.shape, f32),
            jax.ShapeDtypeStruct(rho.shape, f32),
        ],
        scratch_shapes=[pltpu.SemaphoreType.DMA((x.shape[0] + 1,))],
        compiler_params=pltpu.CompilerParams(vmem_limit_bytes=4 << 20),
        name="chain_pass",
    )(*far_copy(x, rho))


def prepare_kernel(step, d_hbm, n_hbm, mass_hbm, ceiling_hbm, obligor_hbm, *refs):
    turned_ref, n_ref, facts_ref, d_ref, mass_ref, ceiling_ref, obligor_ref, sems = refs
    pieces = d_ref.shape[1] // step
    copies = []
    for c in range(pieces):
        part = pl.ds(c * step, step)
        copies.append(pltpu.make_async_copy(d_hbm.at[:, part], d_ref.at[:, part], sems.at[c]))
    small = ((n_hbm, n_ref), (mass_hbm, mass_ref), (ceiling_hbm, ceiling_ref), (obligor_hbm, obligor_ref))
    for k, (source, target) in enumerate(small):
        copies.append(pltpu.make_async_copy(source, target, sems.at[pieces + k]))
    for copy in copies:
        copy.start()
    for c in range(pieces):
        copies[c].wait()
        turned_ref[c * step : (c + 1) * step, :] = d_ref[:, c * step : (c + 1) * step].T
    for copy in copies[pieces:]:
        copy.wait()
    dates, cpties = mass_ref.shape
    facts_ref[...] = jnp.zeros_like(facts_ref)
    facts_ref[:dates, :cpties] = mass_ref[...]
    facts_ref[dates : dates + 1, :cpties] = ceiling_ref[...]
    facts_ref[dates + 1 : dates + 2, : obligor_ref.shape[1]] = obligor_ref[...].astype(f32)


def prepare_pass(d, n, mass, ceiling, obligor):
    factors, trades = d.shape
    step = min(2048, trades)
    hbm = pl.BlockSpec(memory_space=pltpu.HBM)
    vmem = pl.BlockSpec(memory_space=pltpu.VMEM)
    ceiling, obligor = ceiling[None, :], obligor[None, :]
    return pl.pallas_call(
        functools.partial(prepare_kernel, step),
        in_specs=[hbm] * 5,
        out_specs=[vmem] * 3,
        out_shape=[
            jax.ShapeDtypeStruct((trades, factors), bf16),
            jax.ShapeDtypeStruct(n.shape, f32),
            jax.ShapeDtypeStruct((8, 128), f32),
        ],
        scratch_shapes=[
            pltpu.VMEM(d.shape, bf16),
            pltpu.VMEM(mass.shape, f32),
            pltpu.VMEM(ceiling.shape, f32),
            pltpu.VMEM(obligor.shape, jnp.int32),
            pltpu.SemaphoreType.DMA((trades // step + 4,)),
        ],
        compiler_params=pltpu.CompilerParams(vmem_limit_bytes=8 << 20),
        cost_estimate=pl.CostEstimate(flops=0, bytes_accessed=4 * trades * factors, transcendentals=0),
        name="prepare_pass",
    )(*far_copy(d, n, mass, ceiling, obligor))


def value_kernel(step, x_ref, rho_ref, arriving_ref, keep_ref, facts_ref, turned_ref, n_ref, sums_ref, state_ref):
    dates, paths, _ = x_ref.shape
    blocks = step // block_width
    carried = arriving_ref[...] * keep_ref[0].astype(f32)
    for t in range(dates):
        carried = rho_ref[t : t + 1, :] * carried + x_ref[t]
        state_ref[:, t * paths : (t + 1) * paths] = carried.T.astype(bf16)
    total = n_ref.shape[0]
    tiles = state_ref.shape[1] // 128
    sums_ref[tiles * total :, :] = facts_ref[...]

    @pl.loop(0, turned_ref.shape[0] // step)
    def _(c):
        size_t = n_ref[pl.ds(pl.multiple_of(c * blocks, blocks), blocks), :].T
        turned = turned_ref[pl.ds(pl.multiple_of(c * step, step), step), :]
        linear = jnp.dot(turned, state_ref[...], preferred_element_type=f32)
        lines = []
        for b in range(blocks):
            value = softplus(linear[b * block_width : (b + 1) * block_width]) * size_t[:, b : b + 1]
            lines.append(jnp.sum(value, axis=0, keepdims=True))
        sums = jnp.concatenate(lines, axis=0)
        for q in range(tiles):
            at = pl.ds(pl.multiple_of(q * total + c * blocks, blocks), blocks)
            sums_ref[at, :] = sums[:, q * 128 : (q + 1) * 128]


def value_pass(x, rho, arriving, keep, facts, turned, n):
    dates, paths, factors = x.shape
    rows, trades = dates * paths, turned.shape[0]
    vmem = pl.BlockSpec(memory_space=pltpu.VMEM)
    return pl.pallas_call(
        functools.partial(value_kernel, min(VALUE_STEP, trades)),
        in_specs=[vmem, vmem, vmem, pl.BlockSpec(memory_space=pltpu.SMEM), vmem, vmem, vmem],
        out_specs=[vmem] * 2,
        out_shape=[
            jax.ShapeDtypeStruct((rows // 128 * n.shape[0] + 8, 128), f32),
            jax.ShapeDtypeStruct((factors, rows), bf16),
        ],
        compiler_params=pltpu.CompilerParams(vmem_limit_bytes=32 << 20),
        cost_estimate=pl.CostEstimate(
            flops=2 * rows * trades * factors, bytes_accessed=2 * trades * factors, transcendentals=2 * rows * trades
        ),
        name="value_pass",
    )(x, rho, arriving, keep, facts, turned, n)


def slope_kernel(step, state_ref, turned_ref, n_ref, slope_ref, half_ref):
    blocks = step // block_width
    half_ref[...] = state_ref[...] * 0.5

    @pl.loop(0, turned_ref.shape[0] // step)
    def _(c):
        size_t = 0.5 * n_ref[pl.ds(pl.multiple_of(c * blocks, blocks), blocks), :].T
        turned = turned_ref[pl.ds(pl.multiple_of(c * step, step), step), :]
        linear = jnp.dot(turned, half_ref[...], preferred_element_type=f32)
        for b in range(blocks):
            size = size_t[:, b : b + 1]
            slope = jnp.tanh(linear[b * block_width : (b + 1) * block_width]) * size + size
            slope_ref[pl.ds(pl.multiple_of(c * step + b * block_width, block_width), block_width), :] = slope


def slope_pass(state, turned, n):
    factors, rows = state.shape
    trades = turned.shape[0]
    vmem = pl.BlockSpec(memory_space=pltpu.VMEM)
    return pl.pallas_call(
        functools.partial(slope_kernel, min(2048, trades)),
        in_specs=[vmem] * 3,
        out_specs=vmem,
        out_shape=jax.ShapeDtypeStruct((trades, rows), f32),
        scratch_shapes=[pltpu.VMEM((factors, rows), bf16)],
        compiler_params=pltpu.CompilerParams(vmem_limit_bytes=16 << 20),
        cost_estimate=pl.CostEstimate(
            flops=2 * rows * trades * factors, bytes_accessed=4 * trades * rows, transcendentals=rows * trades
        ),
        name="slope_pass",
    )(state, turned, n)


def split_dot(selector, value):
    selector = selector.astype(bf16)
    high = value.astype(bf16)
    rest = value - high.astype(f32)
    middle = rest.astype(bf16)
    low = (rest - middle.astype(f32)).astype(bf16)
    dot = functools.partial(jnp.dot, selector, preferred_element_type=f32)
    return dot(low) + dot(middle) + dot(high)


def net_stage(cpty_dev, dates, me, sums, upstream_ref):
    shards = len(sums)
    blocks, rows = upstream_ref.shape
    paths = rows // dates
    cpties = shards * cpty_dev
    shift = cpty_dev.bit_length() - 1

    def label(owner):
        owner = owner.astype(jnp.int32)
        return (((owner >> shift) ^ me) << shift) + (owner & (cpty_dev - 1))

    tiles = rows // 128
    last = tiles * blocks
    columns = [part[last:, :].T for part in sums]
    netted = None
    for k in range(shards):
        row = label(sums[k][last + dates + 1 : last + dates + 2, :blocks])
        pick = lax.broadcasted_iota(jnp.int32, (cpties, blocks), 0) == row
        slabs = [sums[k][q * blocks : (q + 1) * blocks] for q in range(tiles)]
        part = split_dot(jnp.where(pick, 1.0, 0.0), jnp.concatenate(slabs, axis=1))
        netted = part if netted is None else netted + part
    column = label(columns[0][:blocks, dates + 1 : dates + 2])
    own = jnp.where(lax.broadcasted_iota(jnp.int32, (blocks, cpties), 1) == column, 1.0, 0.0)
    adjoint, totals = [], []
    for k in range(shards):
        shifted = netted[k * cpty_dev : (k + 1) * cpty_dev] - columns[k][:cpty_dev, dates : dates + 1]
        slope = 0.5 * jnp.tanh(0.5 * shifted) + 0.5
        parts = []
        for t in range(dates):
            parts.append(slope[:, t * paths : (t + 1) * paths] * columns[k][:cpty_dev, t : t + 1])
        adjoint.append(jnp.concatenate(parts, axis=1))
        if k == 0:
            exposed = softplus(shifted)
            for t in range(dates):
                totals.append(jnp.sum(exposed[:, t * paths : (t + 1) * paths], axis=1, keepdims=True))
    upstream_ref[...] = split_dot(own, jnp.concatenate(adjoint, axis=0))
    return totals


def pull_stage(step, slope_ref, d_ref, upstream_ref, total_ref):
    blocks = step // block_width
    total_ref[...] = jnp.zeros_like(total_ref)

    @pl.loop(0, d_ref.shape[1] // step)
    def _(c):
        upstream = upstream_ref[pl.ds(pl.multiple_of(c * blocks, blocks), blocks), :]
        parts = []
        for b in range(blocks):
            slope = slope_ref[pl.ds(pl.multiple_of(c * step + b * block_width, block_width), block_width), :]
            parts.append((slope * upstream[b : b + 1, :]).astype(bf16))
        trades = pl.ds(pl.multiple_of(c * step, step), step)
        total_ref[...] += jnp.dot(d_ref[:, trades], jnp.concatenate(parts, axis=0), preferred_element_type=f32)


def net_pull_kernel(step, cpty_dev, shards, me_ref, slope_ref, d_ref, rho_ref, *refs):
    sums, refs = [refs[SUMS_ORDER.index(k)] for k in range(shards)], refs[shards:]
    exposure_ref, refs = refs[0], refs[1:]
    chain, refs = refs[:shards], refs[shards:]
    upstream_ref, total_ref, chained_ref = refs
    dates, paths, factors = chained_ref.shape
    me = me_ref[0]
    totals = net_stage(cpty_dev, dates, me, sums, upstream_ref)
    lane = lax.broadcasted_iota(jnp.int32, (cpty_dev, 128), 1)
    table = jnp.zeros(lane.shape, f32)
    for t, total in enumerate(totals):
        table = jnp.where(lane == t, total, table)
    exposure_ref[...] = table.T[:dates]
    pull_stage(step, slope_ref, d_ref, upstream_ref, total_ref)
    carried = jnp.zeros((paths, factors), f32)
    for t in reversed(range(dates)):
        adjoint = total_ref[:, t * paths : (t + 1) * paths].T + carried
        chained_ref[t] = adjoint
        carried = rho_ref[t : t + 1, :] * adjoint
    piece = paths // shards
    for k in range(shards):
        at = pl.ds(pl.multiple_of((me ^ k) * piece, piece), piece)
        chain[k][...] = chained_ref[:, at, :]


def net_pull_pass(dates, cpty_dev, me, slope, d, rho, sums):
    trades, rows = slope.shape
    factors = d.shape[0]
    paths = rows // dates
    shards = len(sums)
    piece = paths // shards
    vmem = pl.BlockSpec(memory_space=pltpu.VMEM)
    out = pl.pallas_call(
        functools.partial(net_pull_kernel, min(2048, trades), cpty_dev, shards),
        in_specs=[pl.BlockSpec(memory_space=pltpu.SMEM)] + [vmem] * (3 + shards),
        out_specs=[vmem] * (1 + shards),
        out_shape=[jax.ShapeDtypeStruct((dates, cpty_dev), f32)]
        + [jax.ShapeDtypeStruct((dates, piece, factors), f32)] * shards,
        scratch_shapes=[
            pltpu.VMEM((trades // block_width, rows), f32),
            pltpu.VMEM((factors, rows), f32),
            pltpu.VMEM((dates, paths, factors), f32),
        ],
        compiler_params=pltpu.CompilerParams(vmem_limit_bytes=16 << 20),
        cost_estimate=pl.CostEstimate(
            flops=2 * rows * trades * factors, bytes_accessed=4 * trades * rows, transcendentals=0
        ),
        name="net_pull_pass",
    )(me, slope, d, rho, *[sums[k] for k in SUMS_ORDER])
    return out[0], out[1:]


def pull_kernel(step, slope_ref, d_ref, upstream_ref, direct_ref, total_ref):
    pull_stage(step, slope_ref, d_ref, upstream_ref, total_ref)
    dates, paths, _ = direct_ref.shape
    for t in range(dates):
        direct_ref[t] = total_ref[:, t * paths : (t + 1) * paths].T


def pull_pass(dates, slope, d, upstream):
    trades, rows = slope.shape
    factors = d.shape[0]
    vmem = pl.BlockSpec(memory_space=pltpu.VMEM)
    return pl.pallas_call(
        functools.partial(pull_kernel, min(2048, trades)),
        in_specs=[vmem] * 3,
        out_specs=vmem,
        out_shape=jax.ShapeDtypeStruct((dates, rows // dates, factors), f32),
        scratch_shapes=[pltpu.VMEM((factors, rows), f32)],
        compiler_params=pltpu.CompilerParams(vmem_limit_bytes=16 << 20),
        name="pull_pass",
    )(slope, d, upstream)


def place_kernel(shards, share, me_ref, exposure_ref, other_ref, *refs):
    pieces, (profile_ref, out_ref) = [refs[PLACE_ORDER.index(k)] for k in range(shards)], refs[shards:]
    size = pieces[0].shape[1]
    profile_ref[...] = (exposure_ref[...] + other_ref[...]) * share
    for k in range(shards):
        at = pl.ds(pl.multiple_of((me_ref[0] ^ k) * size, size), size)
        out_ref[:, at, :] = pieces[k][...]


def place(me, share, exposure, other, pieces):
    shards = len(pieces)
    dates, size, factors = pieces[0].shape
    vmem = pl.BlockSpec(memory_space=pltpu.VMEM)
    return pl.pallas_call(
        functools.partial(place_kernel, shards, share),
        in_specs=[pl.BlockSpec(memory_space=pltpu.SMEM)] + [vmem] * (2 + shards),
        out_specs=[vmem] * 2,
        out_shape=[
            jax.ShapeDtypeStruct(exposure.shape, f32),
            jax.ShapeDtypeStruct((dates, shards * size, factors), f32),
        ],
        compiler_params=pltpu.CompilerParams(vmem_limit_bytes=4 << 20),
        name="place",
    )(me, exposure, other, *[pieces[k] for k in PLACE_ORDER])


def local_chain(x, rho):
    carried = x[0]
    gain = rho[0]
    for t in range(1, x.shape[0]):
        carried = rho[t][None, :] * carried + x[t]
        gain = rho[t] * gain
    return gain, carried


def near(x, rho, d, size, obligor, ceiling, mass):
    dates, paths, factors = x.shape
    shards = lax.axis_size("trade")
    cpty_dev = ceiling.shape[0]
    n = size.reshape(-1, block_width)
    me = lax.axis_index("trade").astype(jnp.int32)[None]
    date = lax.axis_index("date").astype(jnp.int32)
    over = lambda value, k: swap(value, ("trade",), (shards,), (k,))

    def spread(value):
        return [value] + [over(value, k) for k in range(1, shards)]

    carried, x, rho_near = chain_pass(x, rho)
    arriving = swap(carried, ("date",), (2,), (1,))
    turned, n, facts = prepare_pass(d, n, mass, ceiling, obligor)
    sums, state = value_pass(x, rho_near, arriving, date[None], facts, turned, n)
    sums = spread(sums)
    slope = slope_pass(state, turned, n)
    exposure, chain = net_pull_pass(dates, cpty_dev, me, slope, d, rho_near, sums)
    total = chain[0] + over(chain[3], 3) + over(chain[2], 2) + over(chain[1], 1)

    message = swap(rho[0][None, :] * total[0], ("date",), (2,), (1,))
    weights = [jnp.where(date > 0, 0.0, jnp.ones((factors,), f32))]
    for t in reversed(range(1, dates)):
        weights.append(rho[t] * weights[-1])
    own = total + jnp.stack(weights[::-1])[:, None, :] * message[None]
    pieces = spread(own)
    pieces[3], exposure = lax.optimization_barrier((pieces[3], exposure))
    other = swap(exposure, ("path",), (2,), (1,))
    profile, gradient = place(me, 1.0 / (paths * lax.axis_size("path")), exposure, other, pieces)
    return profile, gradient


def far(x, rho, d, size, obligor, ceiling, mass):
    dates, paths, factors = x.shape
    rows = dates * paths
    cpty_dev = ceiling.shape[0]
    n = size.reshape(-1, block_width)
    value = local_chain(x, rho)
    identity = (jnp.ones_like(value[0]), jnp.zeros_like(value[1]))
    _, arriving = entering(value, "date", compose, identity, False)
    turned, n, facts = prepare_pass(d, n, mass, ceiling, obligor)
    sums, state = value_pass(x, rho, arriving, jnp.ones((1,), jnp.int32), facts, turned, n)
    tiles = rows // 128
    sums = sums[:-8].reshape(tiles, n.shape[0], 128).transpose(1, 0, 2).reshape(n.shape[0], rows)
    cpties = cpty_dev * lax.axis_size("trade")
    ownership = (obligor[:, None] == jnp.arange(cpties, dtype=jnp.int32)[None, :]).astype(f32)
    partial = lax.dot_general(ownership, sums, (((0,), (0,)), ((), ())), precision=highest)
    netted = lax.psum_scatter(partial, "trade", scatter_dimension=0, tiled=True)
    shifted = (netted - ceiling[:, None]).reshape(cpty_dev, dates, paths)
    exposure = jnp.sum(jax.nn.softplus(shifted), axis=2).T
    exposure_profile = lax.psum(exposure, "path") / (paths * lax.axis_size("path"))
    adjoint = (mass.T[:, :, None] * jax.nn.sigmoid(shifted)).reshape(cpty_dev, rows)
    gathered = lax.all_gather(adjoint, "trade", axis=0, tiled=True)
    upstream = jnp.dot(ownership, gathered, precision=highest)
    direct = lax.psum(pull_pass(dates, slope_pass(state, turned, n), d, upstream), "trade")

    gain = jnp.ones((factors,), f32)
    message = jnp.zeros((paths, factors), f32)
    for t in reversed(range(dates)):
        message = rho[t][None, :] * (direct[t] + message)
        gain = rho[t] * gain
    _, message = entering((gain, message), "date", compose, identity, True)
    adjoints = []
    for t in reversed(range(dates)):
        adjoint = direct[t] + message
        adjoints.append(adjoint)
        message = rho[t][None, :] * adjoint
    return exposure_profile, jnp.stack(adjoints[::-1])


def solution(mesh):
    close = mesh.shape["date"] == 2 and mesh.shape["trade"] == 4 and mesh.shape["path"] == 2
    return jax.shard_map(
        near if close else far,
        mesh=mesh,
        in_specs=(
            P(("grp", "date"), "path", None),
            P(("grp", "date"), None),
            P(None, ("grp", "trade")),
            P(("grp", "trade")),
            P(("grp", "trade")),
            P(("grp", "trade")),
            P(("grp", "date"), "trade"),
        ),
        out_specs=(P(("grp", "date"), "trade"), P(("grp", "date"), "path", None)),
        check_vma=False,
    )
```

```python
import functools

import jax
import jax.numpy as jnp
from jax import lax
from jax.experimental import pallas as pl
from jax.experimental.pallas import tpu as pltpu
from jax.sharding import PartitionSpec as P

block_width = 128
highest = lax.Precision.HIGHEST
f32 = jnp.float32
bf16 = jnp.bfloat16
VALUE_STEP = 8192
PULL_STEP = 8192
SUMS_ORDER = (0, 3, 2, 1)
PLACE_ORDER = (0, 2, 1, 3)


def swap(value, axes, sizes, flips):
    count = 1
    for size in sizes:
        count *= size
    pairs = []
    for flat in range(count):
        rest, target, scale = flat, 0, 1
        for size, flip in zip(reversed(sizes), reversed(flips)):
            target += ((rest % size) ^ flip) * scale
            rest //= size
            scale *= size
        pairs.append((flat, target))
    return lax.ppermute(value, axes, pairs)


def entering(value, axis, combine, identity, reverse):
    length, index = (lax.axis_size(axis), lax.axis_index(axis))
    everything = jax.tree.map(lambda part: lax.all_gather(part, axis), value)
    before = jax.tree.map(
        lambda part, zero: jnp.broadcast_to(jnp.asarray(zero, part.dtype), part.shape),
        value,
        identity,
    )
    for k in range(length):
        at = length - 1 - k if reverse else k
        reached = at > index if reverse else at < index
        new = combine(before, jax.tree.map(lambda part: part[at], everything))
        before = jax.tree.map(lambda a, b: jnp.where(reached, a, b), new, before)
    return before


def compose(earlier, later):
    return (later[0] * earlier[0], later[0] * earlier[1] + later[1])


def softplus(v):
    return jnp.maximum(v, jnp.log(1.0 + jnp.exp(jnp.minimum(v, 80.0))))


def far_copy(*parts):
    return [pltpu.with_memory_space_constraint(part, pltpu.HBM) for part in parts]


def chain_kernel(x_hbm, rho_hbm, carried_ref, x_ref, rho_ref, sems):
    dates = x_ref.shape[0]
    copies = [pltpu.make_async_copy(x_hbm.at[t], x_ref.at[t], sems.at[t]) for t in range(dates)]
    copies.append(pltpu.make_async_copy(rho_hbm, rho_ref, sems.at[dates]))
    for copy in copies:
        copy.start()
    copies[dates].wait()
    copies[0].wait()
    carried = x_ref[0]
    for t in range(1, dates):
        copies[t].wait()
        carried = rho_ref[t : t + 1, :] * carried + x_ref[t]
    carried_ref[...] = carried


def chain_pass(x, rho):
    return pl.pallas_call(
        chain_kernel,
        in_specs=[pl.BlockSpec(memory_space=pltpu.HBM)] * 2,
        out_specs=[pl.BlockSpec(memory_space=pltpu.VMEM)] * 3,
        out_shape=[
            jax.ShapeDtypeStruct(x.shape[1:], f32),
            jax.ShapeDtypeStruct(x.shape, f32),
            jax.ShapeDtypeStruct(rho.shape, f32),
        ],
        scratch_shapes=[pltpu.SemaphoreType.DMA((x.shape[0] + 1,))],
        compiler_params=pltpu.CompilerParams(vmem_limit_bytes=4 << 20),
        name="chain_pass",
    )(*far_copy(x, rho))


def prepare_kernel(step, d_hbm, n_hbm, mass_hbm, ceiling_hbm, obligor_hbm, *refs):
    turned_ref, n_ref, facts_ref, d_ref, mass_ref, ceiling_ref, obligor_ref, sems = refs
    pieces = d_ref.shape[1] // step
    copies = []
    for c in range(pieces):
        part = pl.ds(c * step, step)
        copies.append(pltpu.make_async_copy(d_hbm.at[:, part], d_ref.at[:, part], sems.at[c]))
    small = ((n_hbm, n_ref), (mass_hbm, mass_ref), (ceiling_hbm, ceiling_ref), (obligor_hbm, obligor_ref))
    for k, (source, target) in enumerate(small):
        copies.append(pltpu.make_async_copy(source, target, sems.at[pieces + k]))
    for copy in copies:
        copy.start()
    for c in range(pieces):
        copies[c].wait()
        turned_ref[c * step : (c + 1) * step, :] = d_ref[:, c * step : (c + 1) * step].T
    for copy in copies[pieces:]:
        copy.wait()
    dates, cpties = mass_ref.shape
    facts_ref[...] = jnp.zeros_like(facts_ref)
    facts_ref[:dates, :cpties] = mass_ref[...]
    facts_ref[dates : dates + 1, :cpties] = ceiling_ref[...]
    facts_ref[dates + 1 : dates + 2, : obligor_ref.shape[1]] = obligor_ref[...].astype(f32)


def prepare_pass(d, n, mass, ceiling, obligor):
    factors, trades = d.shape
    step = min(2048, trades)
    hbm = pl.BlockSpec(memory_space=pltpu.HBM)
    vmem = pl.BlockSpec(memory_space=pltpu.VMEM)
    ceiling, obligor = ceiling[None, :], obligor[None, :]
    return pl.pallas_call(
        functools.partial(prepare_kernel, step),
        in_specs=[hbm] * 5,
        out_specs=[vmem] * 3,
        out_shape=[
            jax.ShapeDtypeStruct((trades, factors), bf16),
            jax.ShapeDtypeStruct(n.shape, f32),
            jax.ShapeDtypeStruct((8, 128), f32),
        ],
        scratch_shapes=[
            pltpu.VMEM(d.shape, bf16),
            pltpu.VMEM(mass.shape, f32),
            pltpu.VMEM(ceiling.shape, f32),
            pltpu.VMEM(obligor.shape, jnp.int32),
            pltpu.SemaphoreType.DMA((trades // step + 4,)),
        ],
        compiler_params=pltpu.CompilerParams(vmem_limit_bytes=8 << 20),
        cost_estimate=pl.CostEstimate(flops=0, bytes_accessed=4 * trades * factors, transcendentals=0),
        name="prepare_pass",
    )(*far_copy(d, n, mass, ceiling, obligor))


def value_kernel(step, x_ref, rho_ref, arriving_ref, keep_ref, facts_ref, turned_ref, n_ref, sums_ref, state_ref):
    dates, paths, _ = x_ref.shape
    blocks = step // block_width
    carried = arriving_ref[...] * keep_ref[0].astype(f32)
    for t in range(dates):
        carried = rho_ref[t : t + 1, :] * carried + x_ref[t]
        state_ref[:, t * paths : (t + 1) * paths] = carried.T.astype(bf16)
    total = n_ref.shape[0]
    tiles = state_ref.shape[1] // 128
    sums_ref[tiles * total :, :] = facts_ref[...]

    @pl.loop(0, turned_ref.shape[0] // step)
    def _(c):
        size_t = n_ref[pl.ds(pl.multiple_of(c * blocks, blocks), blocks), :].T
        turned = turned_ref[pl.ds(pl.multiple_of(c * step, step), step), :]
        linear = jnp.dot(turned, state_ref[...], preferred_element_type=f32)
        lines = []
        for b in range(blocks):
            value = softplus(linear[b * block_width : (b + 1) * block_width]) * size_t[:, b : b + 1]
            lines.append(jnp.sum(value, axis=0, keepdims=True))
        sums = jnp.concatenate(lines, axis=0)
        for q in range(tiles):
            at = pl.ds(pl.multiple_of(q * total + c * blocks, blocks), blocks)
            sums_ref[at, :] = sums[:, q * 128 : (q + 1) * 128]


def value_pass(x, rho, arriving, keep, facts, turned, n):
    dates, paths, factors = x.shape
    rows, trades = dates * paths, turned.shape[0]
    vmem = pl.BlockSpec(memory_space=pltpu.VMEM)
    return pl.pallas_call(
        functools.partial(value_kernel, min(VALUE_STEP, trades)),
        in_specs=[vmem, vmem, vmem, pl.BlockSpec(memory_space=pltpu.SMEM), vmem, vmem, vmem],
        out_specs=[vmem] * 2,
        out_shape=[
            jax.ShapeDtypeStruct((rows // 128 * n.shape[0] + 8, 128), f32),
            jax.ShapeDtypeStruct((factors, rows), bf16),
        ],
        compiler_params=pltpu.CompilerParams(vmem_limit_bytes=32 << 20),
        cost_estimate=pl.CostEstimate(
            flops=2 * rows * trades * factors, bytes_accessed=2 * trades * factors, transcendentals=2 * rows * trades
        ),
        name="value_pass",
    )(x, rho, arriving, keep, facts, turned, n)


def slope_kernel(step, state_ref, turned_ref, n_ref, slope_ref, half_ref):
    blocks = step // block_width
    half_ref[...] = state_ref[...] * 0.5

    @pl.loop(0, turned_ref.shape[0] // step)
    def _(c):
        size_t = 0.5 * n_ref[pl.ds(pl.multiple_of(c * blocks, blocks), blocks), :].T
        turned = turned_ref[pl.ds(pl.multiple_of(c * step, step), step), :]
        linear = jnp.dot(turned, half_ref[...], preferred_element_type=f32)
        for b in range(blocks):
            size = size_t[:, b : b + 1]
            slope = jnp.tanh(linear[b * block_width : (b + 1) * block_width]) * size + size
            slope_ref[pl.ds(pl.multiple_of(c * step + b * block_width, block_width), block_width), :] = slope


def slope_pass(state, turned, n):
    factors, rows = state.shape
    trades = turned.shape[0]
    vmem = pl.BlockSpec(memory_space=pltpu.VMEM)
    return pl.pallas_call(
        functools.partial(slope_kernel, min(2048, trades)),
        in_specs=[vmem] * 3,
        out_specs=vmem,
        out_shape=jax.ShapeDtypeStruct((trades, rows), f32),
        scratch_shapes=[pltpu.VMEM((factors, rows), bf16)],
        compiler_params=pltpu.CompilerParams(vmem_limit_bytes=16 << 20),
        cost_estimate=pl.CostEstimate(
            flops=2 * rows * trades * factors, bytes_accessed=4 * trades * rows, transcendentals=rows * trades
        ),
        name="slope_pass",
    )(state, turned, n)


def split_dot(selector, value):
    selector = selector.astype(bf16)
    high = value.astype(bf16)
    rest = value - high.astype(f32)
    middle = rest.astype(bf16)
    low = (rest - middle.astype(f32)).astype(bf16)
    dot = functools.partial(jnp.dot, selector, preferred_element_type=f32)
    return dot(low) + dot(middle) + dot(high)


def net_stage(cpty_dev, dates, me, sums, upstream_ref):
    shards = len(sums)
    blocks, rows = upstream_ref.shape
    paths = rows // dates
    cpties = shards * cpty_dev
    shift = cpty_dev.bit_length() - 1

    def label(owner):
        owner = owner.astype(jnp.int32)
        return (((owner >> shift) ^ me) << shift) + (owner & (cpty_dev - 1))

    tiles = rows // 128
    last = tiles * blocks
    columns = [part[last:, :].T for part in sums]
    netted = None
    for k in range(shards):
        row = label(sums[k][last + dates + 1 : last + dates + 2, :blocks])
        pick = lax.broadcasted_iota(jnp.int32, (cpties, blocks), 0) == row
        slabs = [sums[k][q * blocks : (q + 1) * blocks] for q in range(tiles)]
        part = split_dot(jnp.where(pick, 1.0, 0.0), jnp.concatenate(slabs, axis=1))
        netted = part if netted is None else netted + part
    column = label(columns[0][:blocks, dates + 1 : dates + 2])
    own = jnp.where(lax.broadcasted_iota(jnp.int32, (blocks, cpties), 1) == column, 1.0, 0.0)
    adjoint, totals = [], []
    for k in range(shards):
        shifted = netted[k * cpty_dev : (k + 1) * cpty_dev] - columns[k][:cpty_dev, dates : dates + 1]
        slope = 0.5 * jnp.tanh(0.5 * shifted) + 0.5
        parts = []
        for t in range(dates):
            parts.append(slope[:, t * paths : (t + 1) * paths] * columns[k][:cpty_dev, t : t + 1])
        adjoint.append(jnp.concatenate(parts, axis=1))
        if k == 0:
            exposed = softplus(shifted)
            for t in range(dates):
                totals.append(jnp.sum(exposed[:, t * paths : (t + 1) * paths], axis=1, keepdims=True))
    upstream_ref[...] = split_dot(own, jnp.concatenate(adjoint, axis=0))
    return totals


def pull_stage(step, slope_ref, d_ref, upstream_ref, total_ref):
    blocks = step // block_width
    total_ref[...] = jnp.zeros_like(total_ref)

    @pl.loop(0, d_ref.shape[1] // step)
    def _(c):
        upstream = upstream_ref[pl.ds(pl.multiple_of(c * blocks, blocks), blocks), :]
        parts = []
        for b in range(blocks):
            slope = slope_ref[pl.ds(pl.multiple_of(c * step + b * block_width, block_width), block_width), :]
            parts.append((slope * upstream[b : b + 1, :]).astype(bf16))
        trades = pl.ds(pl.multiple_of(c * step, step), step)
        total_ref[...] += jnp.dot(d_ref[:, trades], jnp.concatenate(parts, axis=0), preferred_element_type=f32)


def net_pull_kernel(step, cpty_dev, shards, me_ref, slope_ref, d_ref, rho_ref, *refs):
    sums, refs = [refs[SUMS_ORDER.index(k)] for k in range(shards)], refs[shards:]
    exposure_ref, refs = refs[0], refs[1:]
    chain, refs = refs[:shards], refs[shards:]
    upstream_ref, total_ref, chained_ref = refs
    dates, paths, factors = chained_ref.shape
    me = me_ref[0]
    totals = net_stage(cpty_dev, dates, me, sums, upstream_ref)
    lane = lax.broadcasted_iota(jnp.int32, (cpty_dev, 128), 1)
    table = jnp.zeros(lane.shape, f32)
    for t, total in enumerate(totals):
        table = jnp.where(lane == t, total, table)
    exposure_ref[...] = table.T[:dates]
    pull_stage(step, slope_ref, d_ref, upstream_ref, total_ref)
    carried = jnp.zeros((paths, factors), f32)
    for t in reversed(range(dates)):
        adjoint = total_ref[:, t * paths : (t + 1) * paths].T + carried
        chained_ref[t] = adjoint
        carried = rho_ref[t : t + 1, :] * adjoint
    piece = paths // shards
    for k in range(shards):
        at = pl.ds(pl.multiple_of((me ^ k) * piece, piece), piece)
        chain[k][...] = chained_ref[:, at, :]


def net_pull_pass(dates, cpty_dev, me, slope, d, rho, sums):
    trades, rows = slope.shape
    factors = d.shape[0]
    paths = rows // dates
    shards = len(sums)
    piece = paths // shards
    vmem = pl.BlockSpec(memory_space=pltpu.VMEM)
    out = pl.pallas_call(
        functools.partial(net_pull_kernel, min(PULL_STEP, trades), cpty_dev, shards),
        in_specs=[pl.BlockSpec(memory_space=pltpu.SMEM)] + [vmem] * (3 + shards),
        out_specs=[vmem] * (1 + shards),
        out_shape=[jax.ShapeDtypeStruct((dates, cpty_dev), f32)]
        + [jax.ShapeDtypeStruct((dates, piece, factors), f32)] * shards,
        scratch_shapes=[
            pltpu.VMEM((trades // block_width, rows), f32),
            pltpu.VMEM((factors, rows), f32),
            pltpu.VMEM((dates, paths, factors), f32),
        ],
        compiler_params=pltpu.CompilerParams(vmem_limit_bytes=16 << 20),
        cost_estimate=pl.CostEstimate(
            flops=2 * rows * trades * factors, bytes_accessed=4 * trades * rows, transcendentals=0
        ),
        name="net_pull_pass",
    )(me, slope, d, rho, *[sums[k] for k in SUMS_ORDER])
    return out[0], out[1:]


def pull_kernel(step, slope_ref, d_ref, upstream_ref, direct_ref, total_ref):
    pull_stage(step, slope_ref, d_ref, upstream_ref, total_ref)
    dates, paths, _ = direct_ref.shape
    for t in range(dates):
        direct_ref[t] = total_ref[:, t * paths : (t + 1) * paths].T


def pull_pass(dates, slope, d, upstream):
    trades, rows = slope.shape
    factors = d.shape[0]
    vmem = pl.BlockSpec(memory_space=pltpu.VMEM)
    return pl.pallas_call(
        functools.partial(pull_kernel, min(2048, trades)),
        in_specs=[vmem] * 3,
        out_specs=vmem,
        out_shape=jax.ShapeDtypeStruct((dates, rows // dates, factors), f32),
        scratch_shapes=[pltpu.VMEM((factors, rows), f32)],
        compiler_params=pltpu.CompilerParams(vmem_limit_bytes=16 << 20),
        name="pull_pass",
    )(slope, d, upstream)


def place_kernel(shards, share, me_ref, exposure_ref, other_ref, *refs):
    pieces, (profile_ref, out_ref) = [refs[PLACE_ORDER.index(k)] for k in range(shards)], refs[shards:]
    size = pieces[0].shape[1]
    profile_ref[...] = (exposure_ref[...] + other_ref[...]) * share
    for k in range(shards):
        at = pl.ds(pl.multiple_of((me_ref[0] ^ k) * size, size), size)
        out_ref[:, at, :] = pieces[k][...]


def place(me, share, exposure, other, pieces):
    shards = len(pieces)
    dates, size, factors = pieces[0].shape
    vmem = pl.BlockSpec(memory_space=pltpu.VMEM)
    return pl.pallas_call(
        functools.partial(place_kernel, shards, share),
        in_specs=[pl.BlockSpec(memory_space=pltpu.SMEM)] + [vmem] * (2 + shards),
        out_specs=[vmem] * 2,
        out_shape=[
            jax.ShapeDtypeStruct(exposure.shape, f32),
            jax.ShapeDtypeStruct((dates, shards * size, factors), f32),
        ],
        compiler_params=pltpu.CompilerParams(vmem_limit_bytes=4 << 20),
        name="place",
    )(me, exposure, other, *[pieces[k] for k in PLACE_ORDER])


def local_chain(x, rho):
    carried = x[0]
    gain = rho[0]
    for t in range(1, x.shape[0]):
        carried = rho[t][None, :] * carried + x[t]
        gain = rho[t] * gain
    return gain, carried


def near(x, rho, d, size, obligor, ceiling, mass):
    dates, paths, factors = x.shape
    shards = lax.axis_size("trade")
    cpty_dev = ceiling.shape[0]
    n = size.reshape(-1, block_width)
    me = lax.axis_index("trade").astype(jnp.int32)[None]
    date = lax.axis_index("date").astype(jnp.int32)
    over = lambda value, k: swap(value, ("trade",), (shards,), (k,))

    def spread(value):
        return [value] + [over(value, k) for k in range(1, shards)]

    carried, x, rho_near = chain_pass(x, rho)
    arriving = swap(carried, ("date",), (2,), (1,))
    turned, n, facts = prepare_pass(d, n, mass, ceiling, obligor)
    sums, state = value_pass(x, rho_near, arriving, date[None], facts, turned, n)
    sums = spread(sums)
    slope = slope_pass(state, turned, n)
    exposure, chain = net_pull_pass(dates, cpty_dev, me, slope, d, rho_near, sums)
    total = chain[0] + over(chain[3], 3) + over(chain[2], 2) + over(chain[1], 1)

    message = swap(rho[0][None, :] * total[0], ("date",), (2,), (1,))
    weights = [jnp.where(date > 0, 0.0, jnp.ones((factors,), f32))]
    for t in reversed(range(1, dates)):
        weights.append(rho[t] * weights[-1])
    own = total + jnp.stack(weights[::-1])[:, None, :] * message[None]
    pieces = spread(own)
    pieces[3], exposure = lax.optimization_barrier((pieces[3], exposure))
    other = swap(exposure, ("path",), (2,), (1,))
    profile, gradient = place(me, 1.0 / (paths * lax.axis_size("path")), exposure, other, pieces)
    return profile, gradient


def far(x, rho, d, size, obligor, ceiling, mass):
    dates, paths, factors = x.shape
    rows = dates * paths
    cpty_dev = ceiling.shape[0]
    n = size.reshape(-1, block_width)
    value = local_chain(x, rho)
    identity = (jnp.ones_like(value[0]), jnp.zeros_like(value[1]))
    _, arriving = entering(value, "date", compose, identity, False)
    turned, n, facts = prepare_pass(d, n, mass, ceiling, obligor)
    sums, state = value_pass(x, rho, arriving, jnp.ones((1,), jnp.int32), facts, turned, n)
    tiles = rows // 128
    sums = sums[:-8].reshape(tiles, n.shape[0], 128).transpose(1, 0, 2).reshape(n.shape[0], rows)
    cpties = cpty_dev * lax.axis_size("trade")
    ownership = (obligor[:, None] == jnp.arange(cpties, dtype=jnp.int32)[None, :]).astype(f32)
    partial = lax.dot_general(ownership, sums, (((0,), (0,)), ((), ())), precision=highest)
    netted = lax.psum_scatter(partial, "trade", scatter_dimension=0, tiled=True)
    shifted = (netted - ceiling[:, None]).reshape(cpty_dev, dates, paths)
    exposure = jnp.sum(jax.nn.softplus(shifted), axis=2).T
    exposure_profile = lax.psum(exposure, "path") / (paths * lax.axis_size("path"))
    adjoint = (mass.T[:, :, None] * jax.nn.sigmoid(shifted)).reshape(cpty_dev, rows)
    gathered = lax.all_gather(adjoint, "trade", axis=0, tiled=True)
    upstream = jnp.dot(ownership, gathered, precision=highest)
    direct = lax.psum(pull_pass(dates, slope_pass(state, turned, n), d, upstream), "trade")

    gain = jnp.ones((factors,), f32)
    message = jnp.zeros((paths, factors), f32)
    for t in reversed(range(dates)):
        message = rho[t][None, :] * (direct[t] + message)
        gain = rho[t] * gain
    _, message = entering((gain, message), "date", compose, identity, True)
    adjoints = []
    for t in reversed(range(dates)):
        adjoint = direct[t] + message
        adjoints.append(adjoint)
        message = rho[t][None, :] * adjoint
    return exposure_profile, jnp.stack(adjoints[::-1])


def solution(mesh):
    close = mesh.shape["date"] == 2 and mesh.shape["trade"] == 4 and mesh.shape["path"] == 2
    return jax.shard_map(
        near if close else far,
        mesh=mesh,
        in_specs=(
            P(("grp", "date"), "path", None),
            P(("grp", "date"), None),
            P(None, ("grp", "trade")),
            P(("grp", "trade")),
            P(("grp", "trade")),
            P(("grp", "trade")),
            P(("grp", "date"), "trade"),
        ),
        out_specs=(P(("grp", "date"), "trade"), P(("grp", "date"), "path", None)),
        check_vma=False,
    )
```

```python
import functools

import jax
import jax.numpy as jnp
from jax import lax
from jax.experimental import pallas as pl
from jax.experimental.pallas import tpu as pltpu
from jax.sharding import PartitionSpec as P

block_width = 128
highest = lax.Precision.HIGHEST
f32 = jnp.float32
bf16 = jnp.bfloat16
VALUE_STEP = 8192
PULL_STEP = 8192
SUMS_ORDER = (0, 3, 2, 1)
PLACE_ORDER = (0, 1, 3, 2)


def swap(value, axes, sizes, flips):
    count = 1
    for size in sizes:
        count *= size
    pairs = []
    for flat in range(count):
        rest, target, scale = flat, 0, 1
        for size, flip in zip(reversed(sizes), reversed(flips)):
            target += ((rest % size) ^ flip) * scale
            rest //= size
            scale *= size
        pairs.append((flat, target))
    return lax.ppermute(value, axes, pairs)


def entering(value, axis, combine, identity, reverse):
    length, index = (lax.axis_size(axis), lax.axis_index(axis))
    everything = jax.tree.map(lambda part: lax.all_gather(part, axis), value)
    before = jax.tree.map(
        lambda part, zero: jnp.broadcast_to(jnp.asarray(zero, part.dtype), part.shape),
        value,
        identity,
    )
    for k in range(length):
        at = length - 1 - k if reverse else k
        reached = at > index if reverse else at < index
        new = combine(before, jax.tree.map(lambda part: part[at], everything))
        before = jax.tree.map(lambda a, b: jnp.where(reached, a, b), new, before)
    return before


def compose(earlier, later):
    return (later[0] * earlier[0], later[0] * earlier[1] + later[1])


def softplus(v):
    return jnp.maximum(v, jnp.log(1.0 + jnp.exp(jnp.minimum(v, 80.0))))


def far_copy(*parts):
    return [pltpu.with_memory_space_constraint(part, pltpu.HBM) for part in parts]


def chain_kernel(x_hbm, rho_hbm, carried_ref, x_ref, rho_ref, sems):
    dates = x_ref.shape[0]
    copies = [pltpu.make_async_copy(x_hbm.at[t], x_ref.at[t], sems.at[t]) for t in range(dates)]
    copies.append(pltpu.make_async_copy(rho_hbm, rho_ref, sems.at[dates]))
    for copy in copies:
        copy.start()
    copies[dates].wait()
    copies[0].wait()
    carried = x_ref[0]
    for t in range(1, dates):
        copies[t].wait()
        carried = rho_ref[t : t + 1, :] * carried + x_ref[t]
    carried_ref[...] = carried


def chain_pass(x, rho):
    return pl.pallas_call(
        chain_kernel,
        in_specs=[pl.BlockSpec(memory_space=pltpu.HBM)] * 2,
        out_specs=[pl.BlockSpec(memory_space=pltpu.VMEM)] * 3,
        out_shape=[
            jax.ShapeDtypeStruct(x.shape[1:], f32),
            jax.ShapeDtypeStruct(x.shape, f32),
            jax.ShapeDtypeStruct(rho.shape, f32),
        ],
        scratch_shapes=[pltpu.SemaphoreType.DMA((x.shape[0] + 1,))],
        compiler_params=pltpu.CompilerParams(vmem_limit_bytes=4 << 20),
        name="chain_pass",
    )(*far_copy(x, rho))


def prepare_kernel(step, d_hbm, n_hbm, mass_hbm, ceiling_hbm, obligor_hbm, *refs):
    turned_ref, n_ref, facts_ref, d_ref, mass_ref, ceiling_ref, obligor_ref, sems = refs
    pieces = d_ref.shape[1] // step
    copies = []
    for c in range(pieces):
        part = pl.ds(c * step, step)
        copies.append(pltpu.make_async_copy(d_hbm.at[:, part], d_ref.at[:, part], sems.at[c]))
    small = ((n_hbm, n_ref), (mass_hbm, mass_ref), (ceiling_hbm, ceiling_ref), (obligor_hbm, obligor_ref))
    for k, (source, target) in enumerate(small):
        copies.append(pltpu.make_async_copy(source, target, sems.at[pieces + k]))
    for copy in copies:
        copy.start()
    for c in range(pieces):
        copies[c].wait()
        turned_ref[c * step : (c + 1) * step, :] = d_ref[:, c * step : (c + 1) * step].T
    for copy in copies[pieces:]:
        copy.wait()
    dates, cpties = mass_ref.shape
    facts_ref[...] = jnp.zeros_like(facts_ref)
    facts_ref[:dates, :cpties] = mass_ref[...]
    facts_ref[dates : dates + 1, :cpties] = ceiling_ref[...]
    facts_ref[dates + 1 : dates + 2, : obligor_ref.shape[1]] = obligor_ref[...].astype(f32)


def prepare_pass(d, n, mass, ceiling, obligor):
    factors, trades = d.shape
    step = min(2048, trades)
    hbm = pl.BlockSpec(memory_space=pltpu.HBM)
    vmem = pl.BlockSpec(memory_space=pltpu.VMEM)
    ceiling, obligor = ceiling[None, :], obligor[None, :]
    return pl.pallas_call(
        functools.partial(prepare_kernel, step),
        in_specs=[hbm] * 5,
        out_specs=[vmem] * 3,
        out_shape=[
            jax.ShapeDtypeStruct((trades, factors), bf16),
            jax.ShapeDtypeStruct(n.shape, f32),
            jax.ShapeDtypeStruct((8, 128), f32),
        ],
        scratch_shapes=[
            pltpu.VMEM(d.shape, bf16),
            pltpu.VMEM(mass.shape, f32),
            pltpu.VMEM(ceiling.shape, f32),
            pltpu.VMEM(obligor.shape, jnp.int32),
            pltpu.SemaphoreType.DMA((trades // step + 4,)),
        ],
        compiler_params=pltpu.CompilerParams(vmem_limit_bytes=8 << 20),
        cost_estimate=pl.CostEstimate(flops=0, bytes_accessed=4 * trades * factors, transcendentals=0),
        name="prepare_pass",
    )(*far_copy(d, n, mass, ceiling, obligor))


def value_kernel(step, x_ref, rho_ref, arriving_ref, keep_ref, facts_ref, turned_ref, n_ref, sums_ref, state_ref):
    dates, paths, _ = x_ref.shape
    blocks = step // block_width
    carried = arriving_ref[...] * keep_ref[0].astype(f32)
    for t in range(dates):
        carried = rho_ref[t : t + 1, :] * carried + x_ref[t]
        state_ref[:, t * paths : (t + 1) * paths] = carried.T.astype(bf16)
    total = n_ref.shape[0]
    tiles = state_ref.shape[1] // 128
    sums_ref[tiles * total :, :] = facts_ref[...]

    @pl.loop(0, turned_ref.shape[0] // step)
    def _(c):
        size_t = n_ref[pl.ds(pl.multiple_of(c * blocks, blocks), blocks), :].T
        turned = turned_ref[pl.ds(pl.multiple_of(c * step, step), step), :]
        linear = jnp.dot(turned, state_ref[...], preferred_element_type=f32)
        lines = []
        for b in range(blocks):
            value = softplus(linear[b * block_width : (b + 1) * block_width]) * size_t[:, b : b + 1]
            lines.append(jnp.sum(value, axis=0, keepdims=True))
        sums = jnp.concatenate(lines, axis=0)
        for q in range(tiles):
            at = pl.ds(pl.multiple_of(q * total + c * blocks, blocks), blocks)
            sums_ref[at, :] = sums[:, q * 128 : (q + 1) * 128]


def value_pass(x, rho, arriving, keep, facts, turned, n):
    dates, paths, factors = x.shape
    rows, trades = dates * paths, turned.shape[0]
    vmem = pl.BlockSpec(memory_space=pltpu.VMEM)
    return pl.pallas_call(
        functools.partial(value_kernel, min(VALUE_STEP, trades)),
        in_specs=[vmem, vmem, vmem, pl.BlockSpec(memory_space=pltpu.SMEM), vmem, vmem, vmem],
        out_specs=[vmem] * 2,
        out_shape=[
            jax.ShapeDtypeStruct((rows // 128 * n.shape[0] + 8, 128), f32),
            jax.ShapeDtypeStruct((factors, rows), bf16),
        ],
        compiler_params=pltpu.CompilerParams(vmem_limit_bytes=32 << 20),
        cost_estimate=pl.CostEstimate(
            flops=2 * rows * trades * factors, bytes_accessed=2 * trades * factors, transcendentals=2 * rows * trades
        ),
        name="value_pass",
    )(x, rho, arriving, keep, facts, turned, n)


def slope_kernel(step, state_ref, turned_ref, n_ref, slope_ref, half_ref):
    blocks = step // block_width
    half_ref[...] = state_ref[...] * 0.5

    @pl.loop(0, turned_ref.shape[0] // step)
    def _(c):
        size_t = 0.5 * n_ref[pl.ds(pl.multiple_of(c * blocks, blocks), blocks), :].T
        turned = turned_ref[pl.ds(pl.multiple_of(c * step, step), step), :]
        linear = jnp.dot(turned, half_ref[...], preferred_element_type=f32)
        for b in range(blocks):
            size = size_t[:, b : b + 1]
            slope = jnp.tanh(linear[b * block_width : (b + 1) * block_width]) * size + size
            slope_ref[pl.ds(pl.multiple_of(c * step + b * block_width, block_width), block_width), :] = slope


def slope_pass(state, turned, n):
    factors, rows = state.shape
    trades = turned.shape[0]
    vmem = pl.BlockSpec(memory_space=pltpu.VMEM)
    return pl.pallas_call(
        functools.partial(slope_kernel, min(2048, trades)),
        in_specs=[vmem] * 3,
        out_specs=vmem,
        out_shape=jax.ShapeDtypeStruct((trades, rows), f32),
        scratch_shapes=[pltpu.VMEM((factors, rows), bf16)],
        compiler_params=pltpu.CompilerParams(vmem_limit_bytes=16 << 20),
        cost_estimate=pl.CostEstimate(
            flops=2 * rows * trades * factors, bytes_accessed=4 * trades * rows, transcendentals=rows * trades
        ),
        name="slope_pass",
    )(state, turned, n)


def split_dot(selector, value):
    selector = selector.astype(bf16)
    high = value.astype(bf16)
    rest = value - high.astype(f32)
    middle = rest.astype(bf16)
    low = (rest - middle.astype(f32)).astype(bf16)
    dot = functools.partial(jnp.dot, selector, preferred_element_type=f32)
    return dot(low) + dot(middle) + dot(high)


def net_stage(cpty_dev, dates, me, sums, upstream_ref):
    shards = len(sums)
    blocks, rows = upstream_ref.shape
    paths = rows // dates
    cpties = shards * cpty_dev
    shift = cpty_dev.bit_length() - 1

    def label(owner):
        owner = owner.astype(jnp.int32)
        return (((owner >> shift) ^ me) << shift) + (owner & (cpty_dev - 1))

    tiles = rows // 128
    last = tiles * blocks
    columns = [part[last:, :].T for part in sums]
    netted = None
    for k in range(shards):
        row = label(sums[k][last + dates + 1 : last + dates + 2, :blocks])
        pick = lax.broadcasted_iota(jnp.int32, (cpties, blocks), 0) == row
        slabs = [sums[k][q * blocks : (q + 1) * blocks] for q in range(tiles)]
        part = split_dot(jnp.where(pick, 1.0, 0.0), jnp.concatenate(slabs, axis=1))
        netted = part if netted is None else netted + part
    column = label(columns[0][:blocks, dates + 1 : dates + 2])
    own = jnp.where(lax.broadcasted_iota(jnp.int32, (blocks, cpties), 1) == column, 1.0, 0.0)
    adjoint, totals = [], []
    for k in range(shards):
        shifted = netted[k * cpty_dev : (k + 1) * cpty_dev] - columns[k][:cpty_dev, dates : dates + 1]
        slope = 0.5 * jnp.tanh(0.5 * shifted) + 0.5
        parts = []
        for t in range(dates):
            parts.append(slope[:, t * paths : (t + 1) * paths] * columns[k][:cpty_dev, t : t + 1])
        adjoint.append(jnp.concatenate(parts, axis=1))
        if k == 0:
            exposed = softplus(shifted)
            for t in range(dates):
                totals.append(jnp.sum(exposed[:, t * paths : (t + 1) * paths], axis=1, keepdims=True))
    upstream_ref[...] = split_dot(own, jnp.concatenate(adjoint, axis=0))
    return totals


def pull_stage(step, slope_ref, d_ref, upstream_ref, total_ref):
    blocks = step // block_width
    total_ref[...] = jnp.zeros_like(total_ref)

    @pl.loop(0, d_ref.shape[1] // step)
    def _(c):
        upstream = upstream_ref[pl.ds(pl.multiple_of(c * blocks, blocks), blocks), :]
        parts = []
        for b in range(blocks):
            slope = slope_ref[pl.ds(pl.multiple_of(c * step + b * block_width, block_width), block_width), :]
            parts.append((slope * upstream[b : b + 1, :]).astype(bf16))
        trades = pl.ds(pl.multiple_of(c * step, step), step)
        total_ref[...] += jnp.dot(d_ref[:, trades], jnp.concatenate(parts, axis=0), preferred_element_type=f32)


def net_pull_kernel(step, cpty_dev, shards, me_ref, slope_ref, d_ref, rho_ref, *refs):
    sums, refs = [refs[SUMS_ORDER.index(k)] for k in range(shards)], refs[shards:]
    exposure_ref, refs = refs[0], refs[1:]
    chain, refs = refs[:shards], refs[shards:]
    upstream_ref, total_ref, chained_ref = refs
    dates, paths, factors = chained_ref.shape
    me = me_ref[0]
    totals = net_stage(cpty_dev, dates, me, sums, upstream_ref)
    lane = lax.broadcasted_iota(jnp.int32, (cpty_dev, 128), 1)
    table = jnp.zeros(lane.shape, f32)
    for t, total in enumerate(totals):
        table = jnp.where(lane == t, total, table)
    exposure_ref[...] = table.T[:dates]
    pull_stage(step, slope_ref, d_ref, upstream_ref, total_ref)
    carried = jnp.zeros((paths, factors), f32)
    for t in reversed(range(dates)):
        adjoint = total_ref[:, t * paths : (t + 1) * paths].T + carried
        chained_ref[t] = adjoint
        carried = rho_ref[t : t + 1, :] * adjoint
    piece = paths // shards
    for k in range(shards):
        at = pl.ds(pl.multiple_of((me ^ k) * piece, piece), piece)
        chain[k][...] = chained_ref[:, at, :]


def net_pull_pass(dates, cpty_dev, me, slope, d, rho, sums):
    trades, rows = slope.shape
    factors = d.shape[0]
    paths = rows // dates
    shards = len(sums)
    piece = paths // shards
    vmem = pl.BlockSpec(memory_space=pltpu.VMEM)
    out = pl.pallas_call(
        functools.partial(net_pull_kernel, min(PULL_STEP, trades), cpty_dev, shards),
        in_specs=[pl.BlockSpec(memory_space=pltpu.SMEM)] + [vmem] * (3 + shards),
        out_specs=[vmem] * (1 + shards),
        out_shape=[jax.ShapeDtypeStruct((dates, cpty_dev), f32)]
        + [jax.ShapeDtypeStruct((dates, piece, factors), f32)] * shards,
        scratch_shapes=[
            pltpu.VMEM((trades // block_width, rows), f32),
            pltpu.VMEM((factors, rows), f32),
            pltpu.VMEM((dates, paths, factors), f32),
        ],
        compiler_params=pltpu.CompilerParams(vmem_limit_bytes=16 << 20),
        cost_estimate=pl.CostEstimate(
            flops=2 * rows * trades * factors, bytes_accessed=4 * trades * rows, transcendentals=0
        ),
        name="net_pull_pass",
    )(me, slope, d, rho, *[sums[k] for k in SUMS_ORDER])
    return out[0], out[1:]


def pull_kernel(step, slope_ref, d_ref, upstream_ref, direct_ref, total_ref):
    pull_stage(step, slope_ref, d_ref, upstream_ref, total_ref)
    dates, paths, _ = direct_ref.shape
    for t in range(dates):
        direct_ref[t] = total_ref[:, t * paths : (t + 1) * paths].T


def pull_pass(dates, slope, d, upstream):
    trades, rows = slope.shape
    factors = d.shape[0]
    vmem = pl.BlockSpec(memory_space=pltpu.VMEM)
    return pl.pallas_call(
        functools.partial(pull_kernel, min(2048, trades)),
        in_specs=[vmem] * 3,
        out_specs=vmem,
        out_shape=jax.ShapeDtypeStruct((dates, rows // dates, factors), f32),
        scratch_shapes=[pltpu.VMEM((factors, rows), f32)],
        compiler_params=pltpu.CompilerParams(vmem_limit_bytes=16 << 20),
        name="pull_pass",
    )(slope, d, upstream)


def place_kernel(shards, share, me_ref, exposure_ref, other_ref, *refs):
    pieces, (profile_ref, out_ref) = [refs[PLACE_ORDER.index(k)] for k in range(shards)], refs[shards:]
    size = pieces[0].shape[1]
    profile_ref[...] = (exposure_ref[...] + other_ref[...]) * share
    for k in range(shards):
        at = pl.ds(pl.multiple_of((me_ref[0] ^ k) * size, size), size)
        out_ref[:, at, :] = pieces[k][...]


def place(me, share, exposure, other, pieces):
    shards = len(pieces)
    dates, size, factors = pieces[0].shape
    vmem = pl.BlockSpec(memory_space=pltpu.VMEM)
    return pl.pallas_call(
        functools.partial(place_kernel, shards, share),
        in_specs=[pl.BlockSpec(memory_space=pltpu.SMEM)] + [vmem] * (2 + shards),
        out_specs=[vmem] * 2,
        out_shape=[
            jax.ShapeDtypeStruct(exposure.shape, f32),
            jax.ShapeDtypeStruct((dates, shards * size, factors), f32),
        ],
        compiler_params=pltpu.CompilerParams(vmem_limit_bytes=4 << 20),
        name="place",
    )(me, exposure, other, *[pieces[k] for k in PLACE_ORDER])


def local_chain(x, rho):
    carried = x[0]
    gain = rho[0]
    for t in range(1, x.shape[0]):
        carried = rho[t][None, :] * carried + x[t]
        gain = rho[t] * gain
    return gain, carried


def near(x, rho, d, size, obligor, ceiling, mass):
    dates, paths, factors = x.shape
    shards = lax.axis_size("trade")
    cpty_dev = ceiling.shape[0]
    n = size.reshape(-1, block_width)
    me = lax.axis_index("trade").astype(jnp.int32)[None]
    date = lax.axis_index("date").astype(jnp.int32)
    over = lambda value, k: swap(value, ("trade",), (shards,), (k,))

    def spread(value):
        return [value] + [over(value, k) for k in range(1, shards)]

    carried, x, rho_near = chain_pass(x, rho)
    arriving = swap(carried, ("date",), (2,), (1,))
    turned, n, facts = prepare_pass(d, n, mass, ceiling, obligor)
    sums, state = value_pass(x, rho_near, arriving, date[None], facts, turned, n)
    sums = spread(sums)
    slope = slope_pass(state, turned, n)
    exposure, chain = net_pull_pass(dates, cpty_dev, me, slope, d, rho_near, sums)
    total = chain[0] + over(chain[2], 2) + over(chain[3], 3) + over(chain[1], 1)

    message = swap(rho[0][None, :] * total[0], ("date",), (2,), (1,))
    weights = [jnp.where(date > 0, 0.0, jnp.ones((factors,), f32))]
    for t in reversed(range(1, dates)):
        weights.append(rho[t] * weights[-1])
    own = total + jnp.stack(weights[::-1])[:, None, :] * message[None]
    pieces = spread(own)
    pieces[3], exposure = lax.optimization_barrier((pieces[3], exposure))
    other = swap(exposure, ("path",), (2,), (1,))
    profile, gradient = place(me, 1.0 / (paths * lax.axis_size("path")), exposure, other, pieces)
    return profile, gradient


def far(x, rho, d, size, obligor, ceiling, mass):
    dates, paths, factors = x.shape
    rows = dates * paths
    cpty_dev = ceiling.shape[0]
    n = size.reshape(-1, block_width)
    value = local_chain(x, rho)
    identity = (jnp.ones_like(value[0]), jnp.zeros_like(value[1]))
    _, arriving = entering(value, "date", compose, identity, False)
    turned, n, facts = prepare_pass(d, n, mass, ceiling, obligor)
    sums, state = value_pass(x, rho, arriving, jnp.ones((1,), jnp.int32), facts, turned, n)
    tiles = rows // 128
    sums = sums[:-8].reshape(tiles, n.shape[0], 128).transpose(1, 0, 2).reshape(n.shape[0], rows)
    cpties = cpty_dev * lax.axis_size("trade")
    ownership = (obligor[:, None] == jnp.arange(cpties, dtype=jnp.int32)[None, :]).astype(f32)
    partial = lax.dot_general(ownership, sums, (((0,), (0,)), ((), ())), precision=highest)
    netted = lax.psum_scatter(partial, "trade", scatter_dimension=0, tiled=True)
    shifted = (netted - ceiling[:, None]).reshape(cpty_dev, dates, paths)
    exposure = jnp.sum(jax.nn.softplus(shifted), axis=2).T
    exposure_profile = lax.psum(exposure, "path") / (paths * lax.axis_size("path"))
    adjoint = (mass.T[:, :, None] * jax.nn.sigmoid(shifted)).reshape(cpty_dev, rows)
    gathered = lax.all_gather(adjoint, "trade", axis=0, tiled=True)
    upstream = jnp.dot(ownership, gathered, precision=highest)
    direct = lax.psum(pull_pass(dates, slope_pass(state, turned, n), d, upstream), "trade")

    gain = jnp.ones((factors,), f32)
    message = jnp.zeros((paths, factors), f32)
    for t in reversed(range(dates)):
        message = rho[t][None, :] * (direct[t] + message)
        gain = rho[t] * gain
    _, message = entering((gain, message), "date", compose, identity, True)
    adjoints = []
    for t in reversed(range(dates)):
        adjoint = direct[t] + message
        adjoints.append(adjoint)
        message = rho[t][None, :] * adjoint
    return exposure_profile, jnp.stack(adjoints[::-1])


def solution(mesh):
    close = mesh.shape["date"] == 2 and mesh.shape["trade"] == 4 and mesh.shape["path"] == 2
    return jax.shard_map(
        near if close else far,
        mesh=mesh,
        in_specs=(
            P(("grp", "date"), "path", None),
            P(("grp", "date"), None),
            P(None, ("grp", "trade")),
            P(("grp", "trade")),
            P(("grp", "trade")),
            P(("grp", "trade")),
            P(("grp", "date"), "trade"),
        ),
        out_specs=(P(("grp", "date"), "trade"), P(("grp", "date"), "path", None)),
        check_vma=False,
    )
```

```python
import functools

import jax
import jax.numpy as jnp
from jax import lax
from jax.experimental import pallas as pl
from jax.experimental.pallas import tpu as pltpu
from jax.sharding import PartitionSpec as P

block_width = 128
highest = lax.Precision.HIGHEST
f32 = jnp.float32
bf16 = jnp.bfloat16
VALUE_STEP = 8192
PULL_STEP = 8192
SUMS_ORDER = (0, 3, 2, 1)
PLACE_ORDER = (0, 1, 3, 2)


def swap(value, axes, sizes, flips):
    count = 1
    for size in sizes:
        count *= size
    pairs = []
    for flat in range(count):
        rest, target, scale = flat, 0, 1
        for size, flip in zip(reversed(sizes), reversed(flips)):
            target += ((rest % size) ^ flip) * scale
            rest //= size
            scale *= size
        pairs.append((flat, target))
    return lax.ppermute(value, axes, pairs)


def entering(value, axis, combine, identity, reverse):
    length, index = (lax.axis_size(axis), lax.axis_index(axis))
    everything = jax.tree.map(lambda part: lax.all_gather(part, axis), value)
    before = jax.tree.map(
        lambda part, zero: jnp.broadcast_to(jnp.asarray(zero, part.dtype), part.shape),
        value,
        identity,
    )
    for k in range(length):
        at = length - 1 - k if reverse else k
        reached = at > index if reverse else at < index
        new = combine(before, jax.tree.map(lambda part: part[at], everything))
        before = jax.tree.map(lambda a, b: jnp.where(reached, a, b), new, before)
    return before


def compose(earlier, later):
    return (later[0] * earlier[0], later[0] * earlier[1] + later[1])


def softplus(v):
    return jnp.maximum(v, jnp.log(1.0 + jnp.exp(jnp.minimum(v, 80.0))))


def far_copy(*parts):
    return [pltpu.with_memory_space_constraint(part, pltpu.HBM) for part in parts]


def chain_kernel(x_hbm, rho_hbm, carried_ref, x_ref, rho_ref, sems):
    dates = x_ref.shape[0]
    copies = [pltpu.make_async_copy(x_hbm.at[t], x_ref.at[t], sems.at[t]) for t in range(dates)]
    copies.append(pltpu.make_async_copy(rho_hbm, rho_ref, sems.at[dates]))
    for copy in copies:
        copy.start()
    copies[dates].wait()
    copies[0].wait()
    carried = x_ref[0]
    for t in range(1, dates):
        copies[t].wait()
        carried = rho_ref[t : t + 1, :] * carried + x_ref[t]
    carried_ref[...] = carried


def chain_pass(x, rho):
    return pl.pallas_call(
        chain_kernel,
        in_specs=[pl.BlockSpec(memory_space=pltpu.HBM)] * 2,
        out_specs=[pl.BlockSpec(memory_space=pltpu.VMEM)] * 3,
        out_shape=[
            jax.ShapeDtypeStruct(x.shape[1:], f32),
            jax.ShapeDtypeStruct(x.shape, f32),
            jax.ShapeDtypeStruct(rho.shape, f32),
        ],
        scratch_shapes=[pltpu.SemaphoreType.DMA((x.shape[0] + 1,))],
        compiler_params=pltpu.CompilerParams(vmem_limit_bytes=4 << 20),
        name="chain_pass",
    )(*far_copy(x, rho))


def prepare_kernel(step, d_hbm, n_hbm, mass_hbm, ceiling_hbm, obligor_hbm, *refs):
    turned_ref, n_ref, facts_ref, d_ref, mass_ref, ceiling_ref, obligor_ref, sems = refs
    pieces = d_ref.shape[1] // step
    copies = []
    for c in range(pieces):
        part = pl.ds(c * step, step)
        copies.append(pltpu.make_async_copy(d_hbm.at[:, part], d_ref.at[:, part], sems.at[c]))
    small = ((n_hbm, n_ref), (mass_hbm, mass_ref), (ceiling_hbm, ceiling_ref), (obligor_hbm, obligor_ref))
    for k, (source, target) in enumerate(small):
        copies.append(pltpu.make_async_copy(source, target, sems.at[pieces + k]))
    for copy in copies:
        copy.start()
    for c in range(pieces):
        copies[c].wait()
        turned_ref[c * step : (c + 1) * step, :] = d_ref[:, c * step : (c + 1) * step].T
    for copy in copies[pieces:]:
        copy.wait()
    dates, cpties = mass_ref.shape
    facts_ref[...] = jnp.zeros_like(facts_ref)
    facts_ref[:dates, :cpties] = mass_ref[...]
    facts_ref[dates : dates + 1, :cpties] = ceiling_ref[...]
    facts_ref[dates + 1 : dates + 2, : obligor_ref.shape[1]] = obligor_ref[...].astype(f32)


def prepare_pass(d, n, mass, ceiling, obligor):
    factors, trades = d.shape
    step = min(2048, trades)
    hbm = pl.BlockSpec(memory_space=pltpu.HBM)
    vmem = pl.BlockSpec(memory_space=pltpu.VMEM)
    ceiling, obligor = ceiling[None, :], obligor[None, :]
    return pl.pallas_call(
        functools.partial(prepare_kernel, step),
        in_specs=[hbm] * 5,
        out_specs=[vmem] * 3,
        out_shape=[
            jax.ShapeDtypeStruct((trades, factors), bf16),
            jax.ShapeDtypeStruct(n.shape, f32),
            jax.ShapeDtypeStruct((8, 128), f32),
        ],
        scratch_shapes=[
            pltpu.VMEM(d.shape, bf16),
            pltpu.VMEM(mass.shape, f32),
            pltpu.VMEM(ceiling.shape, f32),
            pltpu.VMEM(obligor.shape, jnp.int32),
            pltpu.SemaphoreType.DMA((trades // step + 4,)),
        ],
        compiler_params=pltpu.CompilerParams(vmem_limit_bytes=8 << 20),
        cost_estimate=pl.CostEstimate(flops=0, bytes_accessed=4 * trades * factors, transcendentals=0),
        name="prepare_pass",
    )(*far_copy(d, n, mass, ceiling, obligor))


def value_kernel(step, x_ref, rho_ref, arriving_ref, keep_ref, facts_ref, turned_ref, n_ref, sums_ref, state_ref):
    dates, paths, _ = x_ref.shape
    blocks = step // block_width
    carried = arriving_ref[...] * keep_ref[0].astype(f32)
    for t in range(dates):
        carried = rho_ref[t : t + 1, :] * carried + x_ref[t]
        state_ref[:, t * paths : (t + 1) * paths] = carried.T.astype(bf16)
    total = n_ref.shape[0]
    tiles = state_ref.shape[1] // 128
    sums_ref[tiles * total :, :] = facts_ref[...]

    @pl.loop(0, turned_ref.shape[0] // step)
    def _(c):
        size_t = n_ref[pl.ds(pl.multiple_of(c * blocks, blocks), blocks), :].T
        turned = turned_ref[pl.ds(pl.multiple_of(c * step, step), step), :]
        linear = jnp.dot(turned, state_ref[...], preferred_element_type=f32)
        lines = []
        for b in range(blocks):
            value = softplus(linear[b * block_width : (b + 1) * block_width]) * size_t[:, b : b + 1]
            lines.append(jnp.sum(value, axis=0, keepdims=True))
        sums = jnp.concatenate(lines, axis=0)
        for q in range(tiles):
            at = pl.ds(pl.multiple_of(q * total + c * blocks, blocks), blocks)
            sums_ref[at, :] = sums[:, q * 128 : (q + 1) * 128]


def value_pass(x, rho, arriving, keep, facts, turned, n):
    dates, paths, factors = x.shape
    rows, trades = dates * paths, turned.shape[0]
    vmem = pl.BlockSpec(memory_space=pltpu.VMEM)
    return pl.pallas_call(
        functools.partial(value_kernel, min(VALUE_STEP, trades)),
        in_specs=[vmem, vmem, vmem, pl.BlockSpec(memory_space=pltpu.SMEM), vmem, vmem, vmem],
        out_specs=[vmem] * 2,
        out_shape=[
            jax.ShapeDtypeStruct((rows // 128 * n.shape[0] + 8, 128), f32),
            jax.ShapeDtypeStruct((factors, rows), bf16),
        ],
        compiler_params=pltpu.CompilerParams(vmem_limit_bytes=32 << 20),
        cost_estimate=pl.CostEstimate(
            flops=2 * rows * trades * factors, bytes_accessed=2 * trades * factors, transcendentals=2 * rows * trades
        ),
        name="value_pass",
    )(x, rho, arriving, keep, facts, turned, n)


def sigmoid(v):
    return 1.0 / (1.0 + jnp.exp(-v))


def slope_kernel(step, state_ref, turned_ref, n_ref, slope_ref):
    blocks = step // block_width

    @pl.loop(0, turned_ref.shape[0] // step)
    def _(c):
        size_t = n_ref[pl.ds(pl.multiple_of(c * blocks, blocks), blocks), :].T
        turned = turned_ref[pl.ds(pl.multiple_of(c * step, step), step), :]
        linear = jnp.dot(turned, state_ref[...], preferred_element_type=f32)
        for b in range(blocks):
            slope = sigmoid(linear[b * block_width : (b + 1) * block_width]) * size_t[:, b : b + 1]
            slope_ref[pl.ds(pl.multiple_of(c * step + b * block_width, block_width), block_width), :] = slope


def slope_pass(state, turned, n):
    factors, rows = state.shape
    trades = turned.shape[0]
    vmem = pl.BlockSpec(memory_space=pltpu.VMEM)
    return pl.pallas_call(
        functools.partial(slope_kernel, min(2048, trades)),
        in_specs=[vmem] * 3,
        out_specs=vmem,
        out_shape=jax.ShapeDtypeStruct((trades, rows), f32),
        compiler_params=pltpu.CompilerParams(vmem_limit_bytes=16 << 20),
        cost_estimate=pl.CostEstimate(
            flops=2 * rows * trades * factors, bytes_accessed=4 * trades * rows, transcendentals=2 * rows * trades
        ),
        name="slope_pass",
    )(state, turned, n)


def split_dot(selector, value):
    selector = selector.astype(bf16)
    high = value.astype(bf16)
    rest = value - high.astype(f32)
    middle = rest.astype(bf16)
    low = (rest - middle.astype(f32)).astype(bf16)
    dot = functools.partial(jnp.dot, selector, preferred_element_type=f32)
    return dot(low) + dot(middle) + dot(high)


def net_stage(cpty_dev, dates, me, sums, upstream_ref):
    shards = len(sums)
    blocks, rows = upstream_ref.shape
    paths = rows // dates
    cpties = shards * cpty_dev
    shift = cpty_dev.bit_length() - 1

    def label(owner):
        owner = owner.astype(jnp.int32)
        return (((owner >> shift) ^ me) << shift) + (owner & (cpty_dev - 1))

    tiles = rows // 128
    last = tiles * blocks
    columns = [part[last:, :].T for part in sums]
    netted = None
    for k in range(shards):
        row = label(sums[k][last + dates + 1 : last + dates + 2, :blocks])
        pick = lax.broadcasted_iota(jnp.int32, (cpties, blocks), 0) == row
        slabs = [sums[k][q * blocks : (q + 1) * blocks] for q in range(tiles)]
        part = split_dot(jnp.where(pick, 1.0, 0.0), jnp.concatenate(slabs, axis=1))
        netted = part if netted is None else netted + part
    column = label(columns[0][:blocks, dates + 1 : dates + 2])
    own = jnp.where(lax.broadcasted_iota(jnp.int32, (blocks, cpties), 1) == column, 1.0, 0.0)
    adjoint, totals = [], []
    for k in range(shards):
        shifted = netted[k * cpty_dev : (k + 1) * cpty_dev] - columns[k][:cpty_dev, dates : dates + 1]
        slope = sigmoid(shifted)
        parts = []
        for t in range(dates):
            parts.append(slope[:, t * paths : (t + 1) * paths] * columns[k][:cpty_dev, t : t + 1])
        adjoint.append(jnp.concatenate(parts, axis=1))
        if k == 0:
            exposed = jnp.maximum(shifted, 0.0) + jnp.log1p(jnp.exp(-jnp.abs(shifted)))
            for t in range(dates):
                totals.append(jnp.sum(exposed[:, t * paths : (t + 1) * paths], axis=1, keepdims=True))
    upstream_ref[...] = split_dot(own, jnp.concatenate(adjoint, axis=0))
    return totals


def pull_stage(step, slope_ref, d_ref, upstream_ref, total_ref):
    blocks = step // block_width
    total_ref[...] = jnp.zeros_like(total_ref)

    @pl.loop(0, d_ref.shape[1] // step)
    def _(c):
        upstream = upstream_ref[pl.ds(pl.multiple_of(c * blocks, blocks), blocks), :]
        parts = []
        for b in range(blocks):
            slope = slope_ref[pl.ds(pl.multiple_of(c * step + b * block_width, block_width), block_width), :]
            parts.append((slope * upstream[b : b + 1, :]).astype(bf16))
        trades = pl.ds(pl.multiple_of(c * step, step), step)
        total_ref[...] += jnp.dot(d_ref[:, trades], jnp.concatenate(parts, axis=0), preferred_element_type=f32)


def net_pull_kernel(step, cpty_dev, shards, me_ref, slope_ref, d_ref, rho_ref, *refs):
    sums, refs = [refs[SUMS_ORDER.index(k)] for k in range(shards)], refs[shards:]
    exposure_ref, refs = refs[0], refs[1:]
    chain, refs = refs[:shards], refs[shards:]
    upstream_ref, total_ref, chained_ref = refs
    dates, paths, factors = chained_ref.shape
    me = me_ref[0]
    totals = net_stage(cpty_dev, dates, me, sums, upstream_ref)
    lane = lax.broadcasted_iota(jnp.int32, (cpty_dev, 128), 1)
    table = jnp.zeros(lane.shape, f32)
    for t, total in enumerate(totals):
        table = jnp.where(lane == t, total, table)
    exposure_ref[...] = table.T[:dates]
    pull_stage(step, slope_ref, d_ref, upstream_ref, total_ref)
    carried = jnp.zeros((paths, factors), f32)
    for t in reversed(range(dates)):
        adjoint = total_ref[:, t * paths : (t + 1) * paths].T + carried
        chained_ref[t] = adjoint
        carried = rho_ref[t : t + 1, :] * adjoint
    piece = paths // shards
    for k in range(shards):
        at = pl.ds(pl.multiple_of((me ^ k) * piece, piece), piece)
        chain[k][...] = chained_ref[:, at, :]


def net_pull_pass(dates, cpty_dev, me, slope, d, rho, sums):
    trades, rows = slope.shape
    factors = d.shape[0]
    paths = rows // dates
    shards = len(sums)
    piece = paths // shards
    vmem = pl.BlockSpec(memory_space=pltpu.VMEM)
    out = pl.pallas_call(
        functools.partial(net_pull_kernel, min(PULL_STEP, trades), cpty_dev, shards),
        in_specs=[pl.BlockSpec(memory_space=pltpu.SMEM)] + [vmem] * (3 + shards),
        out_specs=[vmem] * (1 + shards),
        out_shape=[jax.ShapeDtypeStruct((dates, cpty_dev), f32)]
        + [jax.ShapeDtypeStruct((dates, piece, factors), f32)] * shards,
        scratch_shapes=[
            pltpu.VMEM((trades // block_width, rows), f32),
            pltpu.VMEM((factors, rows), f32),
            pltpu.VMEM((dates, paths, factors), f32),
        ],
        compiler_params=pltpu.CompilerParams(vmem_limit_bytes=16 << 20),
        cost_estimate=pl.CostEstimate(
            flops=2 * rows * trades * factors, bytes_accessed=4 * trades * rows, transcendentals=0
        ),
        name="net_pull_pass",
    )(me, slope, d, rho, *[sums[k] for k in SUMS_ORDER])
    return out[0], out[1:]


def pull_kernel(step, slope_ref, d_ref, upstream_ref, direct_ref, total_ref):
    pull_stage(step, slope_ref, d_ref, upstream_ref, total_ref)
    dates, paths, _ = direct_ref.shape
    for t in range(dates):
        direct_ref[t] = total_ref[:, t * paths : (t + 1) * paths].T


def pull_pass(dates, slope, d, upstream):
    trades, rows = slope.shape
    factors = d.shape[0]
    vmem = pl.BlockSpec(memory_space=pltpu.VMEM)
    return pl.pallas_call(
        functools.partial(pull_kernel, min(2048, trades)),
        in_specs=[vmem] * 3,
        out_specs=vmem,
        out_shape=jax.ShapeDtypeStruct((dates, rows // dates, factors), f32),
        scratch_shapes=[pltpu.VMEM((factors, rows), f32)],
        compiler_params=pltpu.CompilerParams(vmem_limit_bytes=16 << 20),
        name="pull_pass",
    )(slope, d, upstream)


def place_kernel(shards, share, me_ref, exposure_ref, other_ref, *refs):
    pieces, (profile_ref, out_ref) = [refs[PLACE_ORDER.index(k)] for k in range(shards)], refs[shards:]
    size = pieces[0].shape[1]
    profile_ref[...] = (exposure_ref[...] + other_ref[...]) * share
    for k in range(shards):
        at = pl.ds(pl.multiple_of((me_ref[0] ^ k) * size, size), size)
        out_ref[:, at, :] = pieces[k][...]


def place(me, share, exposure, other, pieces):
    shards = len(pieces)
    dates, size, factors = pieces[0].shape
    vmem = pl.BlockSpec(memory_space=pltpu.VMEM)
    return pl.pallas_call(
        functools.partial(place_kernel, shards, share),
        in_specs=[pl.BlockSpec(memory_space=pltpu.SMEM)] + [vmem] * (2 + shards),
        out_specs=[vmem] * 2,
        out_shape=[
            jax.ShapeDtypeStruct(exposure.shape, f32),
            jax.ShapeDtypeStruct((dates, shards * size, factors), f32),
        ],
        compiler_params=pltpu.CompilerParams(vmem_limit_bytes=4 << 20),
        name="place",
    )(me, exposure, other, *[pieces[k] for k in PLACE_ORDER])


def local_chain(x, rho):
    carried = x[0]
    gain = rho[0]
    for t in range(1, x.shape[0]):
        carried = rho[t][None, :] * carried + x[t]
        gain = rho[t] * gain
    return gain, carried


def near(x, rho, d, size, obligor, ceiling, mass):
    dates, paths, factors = x.shape
    shards = lax.axis_size("trade")
    cpty_dev = ceiling.shape[0]
    n = size.reshape(-1, block_width)
    me = lax.axis_index("trade").astype(jnp.int32)[None]
    date = lax.axis_index("date").astype(jnp.int32)
    over = lambda value, k: swap(value, ("trade",), (shards,), (k,))

    def spread(value):
        return [value] + [over(value, k) for k in range(1, shards)]

    carried, x, rho_near = chain_pass(x, rho)
    arriving = swap(carried, ("date",), (2,), (1,))
    turned, n, facts = prepare_pass(d, n, mass, ceiling, obligor)
    sums, state = value_pass(x, rho_near, arriving, date[None], facts, turned, n)
    sums = spread(sums)
    slope = slope_pass(state, turned, n)
    exposure, chain = net_pull_pass(dates, cpty_dev, me, slope, d, rho_near, sums)
    total = chain[0] + over(chain[2], 2) + over(chain[3], 3) + over(chain[1], 1)

    message = swap(rho[0][None, :] * total[0], ("date",), (2,), (1,))
    weights = [jnp.where(date > 0, 0.0, jnp.ones((factors,), f32))]
    for t in reversed(range(1, dates)):
        weights.append(rho[t] * weights[-1])
    own = total + jnp.stack(weights[::-1])[:, None, :] * message[None]
    pieces = spread(own)
    pieces[3], exposure = lax.optimization_barrier((pieces[3], exposure))
    other = swap(exposure, ("path",), (2,), (1,))
    profile, gradient = place(me, 1.0 / (paths * lax.axis_size("path")), exposure, other, pieces)
    return profile, gradient


def far(x, rho, d, size, obligor, ceiling, mass):
    dates, paths, factors = x.shape
    rows = dates * paths
    cpty_dev = ceiling.shape[0]
    n = size.reshape(-1, block_width)
    value = local_chain(x, rho)
    identity = (jnp.ones_like(value[0]), jnp.zeros_like(value[1]))
    _, arriving = entering(value, "date", compose, identity, False)
    turned, n, facts = prepare_pass(d, n, mass, ceiling, obligor)
    sums, state = value_pass(x, rho, arriving, jnp.ones((1,), jnp.int32), facts, turned, n)
    tiles = rows // 128
    sums = sums[:-8].reshape(tiles, n.shape[0], 128).transpose(1, 0, 2).reshape(n.shape[0], rows)
    cpties = cpty_dev * lax.axis_size("trade")
    ownership = (obligor[:, None] == jnp.arange(cpties, dtype=jnp.int32)[None, :]).astype(f32)
    partial = lax.dot_general(ownership, sums, (((0,), (0,)), ((), ())), precision=highest)
    netted = lax.psum_scatter(partial, "trade", scatter_dimension=0, tiled=True)
    shifted = (netted - ceiling[:, None]).reshape(cpty_dev, dates, paths)
    exposure = jnp.sum(jax.nn.softplus(shifted), axis=2).T
    exposure_profile = lax.psum(exposure, "path") / (paths * lax.axis_size("path"))
    adjoint = (mass.T[:, :, None] * jax.nn.sigmoid(shifted)).reshape(cpty_dev, rows)
    gathered = lax.all_gather(adjoint, "trade", axis=0, tiled=True)
    upstream = jnp.dot(ownership, gathered, precision=highest)
    direct = lax.psum(pull_pass(dates, slope_pass(state, turned, n), d, upstream), "trade")

    gain = jnp.ones((factors,), f32)
    message = jnp.zeros((paths, factors), f32)
    for t in reversed(range(dates)):
        message = rho[t][None, :] * (direct[t] + message)
        gain = rho[t] * gain
    _, message = entering((gain, message), "date", compose, identity, True)
    adjoints = []
    for t in reversed(range(dates)):
        adjoint = direct[t] + message
        adjoints.append(adjoint)
        message = rho[t][None, :] * adjoint
    return exposure_profile, jnp.stack(adjoints[::-1])


def solution(mesh):
    close = mesh.shape["date"] == 2 and mesh.shape["trade"] == 4 and mesh.shape["path"] == 2
    return jax.shard_map(
        near if close else far,
        mesh=mesh,
        in_specs=(
            P(("grp", "date"), "path", None),
            P(("grp", "date"), None),
            P(None, ("grp", "trade")),
            P(("grp", "trade")),
            P(("grp", "trade")),
            P(("grp", "trade")),
            P(("grp", "date"), "trade"),
        ),
        out_specs=(P(("grp", "date"), "trade"), P(("grp", "date"), "path", None)),
        check_vma=False,
    )
```

```python
import functools

import jax
import jax.numpy as jnp
from jax import lax
from jax.experimental import pallas as pl
from jax.experimental.pallas import tpu as pltpu
from jax.sharding import PartitionSpec as P

block_width = 128
highest = lax.Precision.HIGHEST
f32 = jnp.float32
bf16 = jnp.bfloat16
VALUE_STEP = 8192
PULL_STEP = 8192
SUMS_ORDER = (0, 3, 2, 1)
PLACE_ORDER = (0, 1, 3, 2)


def swap(value, axes, sizes, flips):
    count = 1
    for size in sizes:
        count *= size
    pairs = []
    for flat in range(count):
        rest, target, scale = flat, 0, 1
        for size, flip in zip(reversed(sizes), reversed(flips)):
            target += ((rest % size) ^ flip) * scale
            rest //= size
            scale *= size
        pairs.append((flat, target))
    return lax.ppermute(value, axes, pairs)


def entering(value, axis, combine, identity, reverse):
    length, index = (lax.axis_size(axis), lax.axis_index(axis))
    everything = jax.tree.map(lambda part: lax.all_gather(part, axis), value)
    before = jax.tree.map(
        lambda part, zero: jnp.broadcast_to(jnp.asarray(zero, part.dtype), part.shape),
        value,
        identity,
    )
    for k in range(length):
        at = length - 1 - k if reverse else k
        reached = at > index if reverse else at < index
        new = combine(before, jax.tree.map(lambda part: part[at], everything))
        before = jax.tree.map(lambda a, b: jnp.where(reached, a, b), new, before)
    return before


def compose(earlier, later):
    return (later[0] * earlier[0], later[0] * earlier[1] + later[1])


def softplus(v):
    return jnp.maximum(v, jnp.log(1.0 + jnp.exp(jnp.minimum(v, 80.0))))


def far_copy(*parts):
    return [pltpu.with_memory_space_constraint(part, pltpu.HBM) for part in parts]


def chain_kernel(x_hbm, rho_hbm, carried_ref, x_ref, rho_ref, sems):
    dates = x_ref.shape[0]
    copies = [pltpu.make_async_copy(x_hbm.at[t], x_ref.at[t], sems.at[t]) for t in range(dates)]
    copies.append(pltpu.make_async_copy(rho_hbm, rho_ref, sems.at[dates]))
    for copy in copies:
        copy.start()
    copies[dates].wait()
    copies[0].wait()
    carried = x_ref[0]
    for t in range(1, dates):
        copies[t].wait()
        carried = rho_ref[t : t + 1, :] * carried + x_ref[t]
    carried_ref[...] = carried


def chain_pass(x, rho):
    return pl.pallas_call(
        chain_kernel,
        in_specs=[pl.BlockSpec(memory_space=pltpu.HBM)] * 2,
        out_specs=[pl.BlockSpec(memory_space=pltpu.VMEM)] * 3,
        out_shape=[
            jax.ShapeDtypeStruct(x.shape[1:], f32),
            jax.ShapeDtypeStruct(x.shape, f32),
            jax.ShapeDtypeStruct(rho.shape, f32),
        ],
        scratch_shapes=[pltpu.SemaphoreType.DMA((x.shape[0] + 1,))],
        compiler_params=pltpu.CompilerParams(vmem_limit_bytes=4 << 20),
        name="chain_pass",
    )(*far_copy(x, rho))


def prepare_kernel(step, d_hbm, n_hbm, mass_hbm, ceiling_hbm, obligor_hbm, *refs):
    turned_ref, n_ref, facts_ref, d_ref, mass_ref, ceiling_ref, obligor_ref, sems = refs
    pieces = d_ref.shape[1] // step
    copies = []
    for c in range(pieces):
        part = pl.ds(c * step, step)
        copies.append(pltpu.make_async_copy(d_hbm.at[:, part], d_ref.at[:, part], sems.at[c]))
    small = ((n_hbm, n_ref), (mass_hbm, mass_ref), (ceiling_hbm, ceiling_ref), (obligor_hbm, obligor_ref))
    for k, (source, target) in enumerate(small):
        copies.append(pltpu.make_async_copy(source, target, sems.at[pieces + k]))
    for copy in copies:
        copy.start()
    for c in range(pieces):
        copies[c].wait()
        turned_ref[c * step : (c + 1) * step, :] = d_ref[:, c * step : (c + 1) * step].T
    for copy in copies[pieces:]:
        copy.wait()
    dates, cpties = mass_ref.shape
    facts_ref[...] = jnp.zeros_like(facts_ref)
    facts_ref[:dates, :cpties] = mass_ref[...]
    facts_ref[dates : dates + 1, :cpties] = ceiling_ref[...]
    facts_ref[dates + 1 : dates + 2, : obligor_ref.shape[1]] = obligor_ref[...].astype(f32)


def prepare_pass(d, n, mass, ceiling, obligor):
    factors, trades = d.shape
    step = min(2048, trades)
    hbm = pl.BlockSpec(memory_space=pltpu.HBM)
    vmem = pl.BlockSpec(memory_space=pltpu.VMEM)
    ceiling, obligor = ceiling[None, :], obligor[None, :]
    return pl.pallas_call(
        functools.partial(prepare_kernel, step),
        in_specs=[hbm] * 5,
        out_specs=[vmem] * 3,
        out_shape=[
            jax.ShapeDtypeStruct((trades, factors), bf16),
            jax.ShapeDtypeStruct(n.shape, f32),
            jax.ShapeDtypeStruct((8, 128), f32),
        ],
        scratch_shapes=[
            pltpu.VMEM(d.shape, bf16),
            pltpu.VMEM(mass.shape, f32),
            pltpu.VMEM(ceiling.shape, f32),
            pltpu.VMEM(obligor.shape, jnp.int32),
            pltpu.SemaphoreType.DMA((trades // step + 4,)),
        ],
        compiler_params=pltpu.CompilerParams(vmem_limit_bytes=8 << 20),
        cost_estimate=pl.CostEstimate(flops=0, bytes_accessed=4 * trades * factors, transcendentals=0),
        name="prepare_pass",
    )(*far_copy(d, n, mass, ceiling, obligor))


def value_kernel(step, x_ref, rho_ref, arriving_ref, keep_ref, facts_ref, turned_ref, n_ref, sums_ref, state_ref):
    dates, paths, _ = x_ref.shape
    blocks = step // block_width
    carried = arriving_ref[...] * keep_ref[0].astype(f32)
    for t in range(dates):
        carried = rho_ref[t : t + 1, :] * carried + x_ref[t]
        state_ref[:, t * paths : (t + 1) * paths] = carried.T.astype(bf16)
    total = n_ref.shape[0]
    tiles = state_ref.shape[1] // 128
    sums_ref[tiles * total :, :] = facts_ref[...]

    @pl.loop(0, turned_ref.shape[0] // step)
    def _(c):
        size_t = n_ref[pl.ds(pl.multiple_of(c * blocks, blocks), blocks), :].T
        turned = turned_ref[pl.ds(pl.multiple_of(c * step, step), step), :]
        linear = jnp.dot(turned, state_ref[...], preferred_element_type=f32)
        lines = []
        for b in range(blocks):
            value = softplus(linear[b * block_width : (b + 1) * block_width]) * size_t[:, b : b + 1]
            lines.append(jnp.sum(value, axis=0, keepdims=True))
        sums = jnp.concatenate(lines, axis=0)
        for q in range(tiles):
            at = pl.ds(pl.multiple_of(q * total + c * blocks, blocks), blocks)
            sums_ref[at, :] = sums[:, q * 128 : (q + 1) * 128]


def value_pass(x, rho, arriving, keep, facts, turned, n):
    dates, paths, factors = x.shape
    rows, trades = dates * paths, turned.shape[0]
    vmem = pl.BlockSpec(memory_space=pltpu.VMEM)
    return pl.pallas_call(
        functools.partial(value_kernel, min(VALUE_STEP, trades)),
        in_specs=[vmem, vmem, vmem, pl.BlockSpec(memory_space=pltpu.SMEM), vmem, vmem, vmem],
        out_specs=[vmem] * 2,
        out_shape=[
            jax.ShapeDtypeStruct((rows // 128 * n.shape[0] + 8, 128), f32),
            jax.ShapeDtypeStruct((factors, rows), bf16),
        ],
        compiler_params=pltpu.CompilerParams(vmem_limit_bytes=32 << 20),
        cost_estimate=pl.CostEstimate(
            flops=2 * rows * trades * factors, bytes_accessed=2 * trades * factors, transcendentals=2 * rows * trades
        ),
        name="value_pass",
    )(x, rho, arriving, keep, facts, turned, n)


def sigmoid(v):
    return 1.0 / (1.0 + jnp.exp(-v))


def slope_kernel(step, state_ref, turned_ref, n_ref, slope_ref):
    blocks = step // block_width

    @pl.loop(0, turned_ref.shape[0] // step)
    def _(c):
        size_t = n_ref[pl.ds(pl.multiple_of(c * blocks, blocks), blocks), :].T
        turned = turned_ref[pl.ds(pl.multiple_of(c * step, step), step), :]
        linear = jnp.dot(turned, state_ref[...], preferred_element_type=f32)
        for b in range(blocks):
            slope = sigmoid(linear[b * block_width : (b + 1) * block_width]) * size_t[:, b : b + 1]
            slope_ref[pl.ds(pl.multiple_of(c * step + b * block_width, block_width), block_width), :] = slope


def slope_pass(state, turned, n):
    factors, rows = state.shape
    trades = turned.shape[0]
    vmem = pl.BlockSpec(memory_space=pltpu.VMEM)
    return pl.pallas_call(
        functools.partial(slope_kernel, min(8192, trades)),
        in_specs=[vmem] * 3,
        out_specs=vmem,
        out_shape=jax.ShapeDtypeStruct((trades, rows), f32),
        compiler_params=pltpu.CompilerParams(vmem_limit_bytes=16 << 20),
        cost_estimate=pl.CostEstimate(
            flops=2 * rows * trades * factors, bytes_accessed=4 * trades * rows, transcendentals=2 * rows * trades
        ),
        name="slope_pass",
    )(state, turned, n)


def split_dot(selector, value):
    selector = selector.astype(bf16)
    high = value.astype(bf16)
    rest = value - high.astype(f32)
    middle = rest.astype(bf16)
    low = (rest - middle.astype(f32)).astype(bf16)
    parts = jnp.concatenate([low, middle, high], axis=0)
    return jnp.dot(jnp.concatenate([selector] * 3, axis=1), parts, preferred_element_type=f32)


def net_stage(cpty_dev, dates, me, sums, upstream_ref):
    shards = len(sums)
    blocks, rows = upstream_ref.shape
    paths = rows // dates
    cpties = shards * cpty_dev
    shift = cpty_dev.bit_length() - 1

    def label(owner):
        owner = owner.astype(jnp.int32)
        return (((owner >> shift) ^ me) << shift) + (owner & (cpty_dev - 1))

    tiles = rows // 128
    last = tiles * blocks
    columns = [part[last:, :].T for part in sums]
    rows_of = [label(part[last + dates + 1 : last + dates + 2, :blocks]) for part in sums]
    pick = lax.broadcasted_iota(jnp.int32, (cpties, shards * blocks), 0) == jnp.concatenate(rows_of, axis=1)
    slabs = [jnp.concatenate([part[q * blocks : (q + 1) * blocks] for q in range(tiles)], axis=1) for part in sums]
    netted = split_dot(jnp.where(pick, 1.0, 0.0), jnp.concatenate(slabs, axis=0))
    column = label(columns[0][:blocks, dates + 1 : dates + 2])
    own = jnp.where(lax.broadcasted_iota(jnp.int32, (blocks, cpties), 1) == column, 1.0, 0.0)
    adjoint, totals = [], []
    for k in range(shards):
        shifted = netted[k * cpty_dev : (k + 1) * cpty_dev] - columns[k][:cpty_dev, dates : dates + 1]
        slope = sigmoid(shifted)
        parts = []
        for t in range(dates):
            parts.append(slope[:, t * paths : (t + 1) * paths] * columns[k][:cpty_dev, t : t + 1])
        adjoint.append(jnp.concatenate(parts, axis=1))
        if k == 0:
            exposed = jnp.maximum(shifted, 0.0) + jnp.log1p(jnp.exp(-jnp.abs(shifted)))
            for t in range(dates):
                totals.append(jnp.sum(exposed[:, t * paths : (t + 1) * paths], axis=1, keepdims=True))
    upstream_ref[...] = split_dot(own, jnp.concatenate(adjoint, axis=0))
    return totals


def pull_stage(step, slope_ref, d_ref, upstream_ref, total_ref):
    blocks = step // block_width
    total_ref[...] = jnp.zeros_like(total_ref)

    @pl.loop(0, d_ref.shape[1] // step)
    def _(c):
        upstream = upstream_ref[pl.ds(pl.multiple_of(c * blocks, blocks), blocks), :]
        parts = []
        for b in range(blocks):
            slope = slope_ref[pl.ds(pl.multiple_of(c * step + b * block_width, block_width), block_width), :]
            parts.append((slope * upstream[b : b + 1, :]).astype(bf16))
        trades = pl.ds(pl.multiple_of(c * step, step), step)
        total_ref[...] += jnp.dot(d_ref[:, trades], jnp.concatenate(parts, axis=0), preferred_element_type=f32)


def net_pull_kernel(step, cpty_dev, shards, me_ref, slope_ref, d_ref, rho_ref, *refs):
    sums, refs = [refs[SUMS_ORDER.index(k)] for k in range(shards)], refs[shards:]
    exposure_ref, refs = refs[0], refs[1:]
    chain, refs = refs[:shards], refs[shards:]
    upstream_ref, total_ref, chained_ref = refs
    dates, paths, factors = chained_ref.shape
    me = me_ref[0]
    totals = net_stage(cpty_dev, dates, me, sums, upstream_ref)
    lane = lax.broadcasted_iota(jnp.int32, (cpty_dev, 128), 1)
    table = jnp.zeros(lane.shape, f32)
    for t, total in enumerate(totals):
        table = jnp.where(lane == t, total, table)
    exposure_ref[...] = table.T[:dates]
    pull_stage(step, slope_ref, d_ref, upstream_ref, total_ref)
    carried = jnp.zeros((paths, factors), f32)
    for t in reversed(range(dates)):
        adjoint = total_ref[:, t * paths : (t + 1) * paths].T + carried
        chained_ref[t] = adjoint
        carried = rho_ref[t : t + 1, :] * adjoint
    piece = paths // shards
    for k in range(shards):
        at = pl.ds(pl.multiple_of((me ^ k) * piece, piece), piece)
        chain[k][...] = chained_ref[:, at, :]


def net_pull_pass(dates, cpty_dev, me, slope, d, rho, sums):
    trades, rows = slope.shape
    factors = d.shape[0]
    paths = rows // dates
    shards = len(sums)
    piece = paths // shards
    vmem = pl.BlockSpec(memory_space=pltpu.VMEM)
    out = pl.pallas_call(
        functools.partial(net_pull_kernel, min(PULL_STEP, trades), cpty_dev, shards),
        in_specs=[pl.BlockSpec(memory_space=pltpu.SMEM)] + [vmem] * (3 + shards),
        out_specs=[vmem] * (1 + shards),
        out_shape=[jax.ShapeDtypeStruct((dates, cpty_dev), f32)]
        + [jax.ShapeDtypeStruct((dates, piece, factors), f32)] * shards,
        scratch_shapes=[
            pltpu.VMEM((trades // block_width, rows), f32),
            pltpu.VMEM((factors, rows), f32),
            pltpu.VMEM((dates, paths, factors), f32),
        ],
        compiler_params=pltpu.CompilerParams(vmem_limit_bytes=16 << 20),
        cost_estimate=pl.CostEstimate(
            flops=2 * rows * trades * factors, bytes_accessed=4 * trades * rows, transcendentals=0
        ),
        name="net_pull_pass",
    )(me, slope, d, rho, *[sums[k] for k in SUMS_ORDER])
    return out[0], out[1:]


def pull_kernel(step, slope_ref, d_ref, upstream_ref, direct_ref, total_ref):
    pull_stage(step, slope_ref, d_ref, upstream_ref, total_ref)
    dates, paths, _ = direct_ref.shape
    for t in range(dates):
        direct_ref[t] = total_ref[:, t * paths : (t + 1) * paths].T


def pull_pass(dates, slope, d, upstream):
    trades, rows = slope.shape
    factors = d.shape[0]
    vmem = pl.BlockSpec(memory_space=pltpu.VMEM)
    return pl.pallas_call(
        functools.partial(pull_kernel, min(2048, trades)),
        in_specs=[vmem] * 3,
        out_specs=vmem,
        out_shape=jax.ShapeDtypeStruct((dates, rows // dates, factors), f32),
        scratch_shapes=[pltpu.VMEM((factors, rows), f32)],
        compiler_params=pltpu.CompilerParams(vmem_limit_bytes=16 << 20),
        name="pull_pass",
    )(slope, d, upstream)


def place_kernel(shards, share, me_ref, exposure_ref, other_ref, *refs):
    pieces, (profile_ref, out_ref) = [refs[PLACE_ORDER.index(k)] for k in range(shards)], refs[shards:]
    size = pieces[0].shape[1]
    profile_ref[...] = (exposure_ref[...] + other_ref[...]) * share
    for k in range(shards):
        at = pl.ds(pl.multiple_of((me_ref[0] ^ k) * size, size), size)
        out_ref[:, at, :] = pieces[k][...]


def place(me, share, exposure, other, pieces):
    shards = len(pieces)
    dates, size, factors = pieces[0].shape
    vmem = pl.BlockSpec(memory_space=pltpu.VMEM)
    return pl.pallas_call(
        functools.partial(place_kernel, shards, share),
        in_specs=[pl.BlockSpec(memory_space=pltpu.SMEM)] + [vmem] * (2 + shards),
        out_specs=[vmem] * 2,
        out_shape=[
            jax.ShapeDtypeStruct(exposure.shape, f32),
            jax.ShapeDtypeStruct((dates, shards * size, factors), f32),
        ],
        compiler_params=pltpu.CompilerParams(vmem_limit_bytes=4 << 20),
        name="place",
    )(me, exposure, other, *[pieces[k] for k in PLACE_ORDER])


def local_chain(x, rho):
    carried = x[0]
    gain = rho[0]
    for t in range(1, x.shape[0]):
        carried = rho[t][None, :] * carried + x[t]
        gain = rho[t] * gain
    return gain, carried


def near(x, rho, d, size, obligor, ceiling, mass):
    dates, paths, factors = x.shape
    shards = lax.axis_size("trade")
    cpty_dev = ceiling.shape[0]
    n = size.reshape(-1, block_width)
    me = lax.axis_index("trade").astype(jnp.int32)[None]
    date = lax.axis_index("date").astype(jnp.int32)
    over = lambda value, k: swap(value, ("trade",), (shards,), (k,))

    def spread(value):
        return [value] + [over(value, k) for k in range(1, shards)]

    carried, x, rho_near = chain_pass(x, rho)
    arriving = swap(carried, ("date",), (2,), (1,))
    turned, n, facts = prepare_pass(d, n, mass, ceiling, obligor)
    sums, state = value_pass(x, rho_near, arriving, date[None], facts, turned, n)
    sums = spread(sums)
    slope = slope_pass(state, turned, n)
    exposure, chain = net_pull_pass(dates, cpty_dev, me, slope, d, rho_near, sums)
    total = chain[0] + over(chain[2], 2) + over(chain[3], 3) + over(chain[1], 1)

    message = swap(rho[0][None, :] * total[0], ("date",), (2,), (1,))
    weights = [jnp.where(date > 0, 0.0, jnp.ones((factors,), f32))]
    for t in reversed(range(1, dates)):
        weights.append(rho[t] * weights[-1])
    own = total + jnp.stack(weights[::-1])[:, None, :] * message[None]
    pieces = spread(own)
    pieces[3], exposure = lax.optimization_barrier((pieces[3], exposure))
    other = swap(exposure, ("path",), (2,), (1,))
    profile, gradient = place(me, 1.0 / (paths * lax.axis_size("path")), exposure, other, pieces)
    return profile, gradient


def far(x, rho, d, size, obligor, ceiling, mass):
    dates, paths, factors = x.shape
    rows = dates * paths
    cpty_dev = ceiling.shape[0]
    n = size.reshape(-1, block_width)
    value = local_chain(x, rho)
    identity = (jnp.ones_like(value[0]), jnp.zeros_like(value[1]))
    _, arriving = entering(value, "date", compose, identity, False)
    turned, n, facts = prepare_pass(d, n, mass, ceiling, obligor)
    sums, state = value_pass(x, rho, arriving, jnp.ones((1,), jnp.int32), facts, turned, n)
    tiles = rows // 128
    sums = sums[:-8].reshape(tiles, n.shape[0], 128).transpose(1, 0, 2).reshape(n.shape[0], rows)
    cpties = cpty_dev * lax.axis_size("trade")
    ownership = (obligor[:, None] == jnp.arange(cpties, dtype=jnp.int32)[None, :]).astype(f32)
    partial = lax.dot_general(ownership, sums, (((0,), (0,)), ((), ())), precision=highest)
    netted = lax.psum_scatter(partial, "trade", scatter_dimension=0, tiled=True)
    shifted = (netted - ceiling[:, None]).reshape(cpty_dev, dates, paths)
    exposure = jnp.sum(jax.nn.softplus(shifted), axis=2).T
    exposure_profile = lax.psum(exposure, "path") / (paths * lax.axis_size("path"))
    adjoint = (mass.T[:, :, None] * jax.nn.sigmoid(shifted)).reshape(cpty_dev, rows)
    gathered = lax.all_gather(adjoint, "trade", axis=0, tiled=True)
    upstream = jnp.dot(ownership, gathered, precision=highest)
    direct = lax.psum(pull_pass(dates, slope_pass(state, turned, n), d, upstream), "trade")

    gain = jnp.ones((factors,), f32)
    message = jnp.zeros((paths, factors), f32)
    for t in reversed(range(dates)):
        message = rho[t][None, :] * (direct[t] + message)
        gain = rho[t] * gain
    _, message = entering((gain, message), "date", compose, identity, True)
    adjoints = []
    for t in reversed(range(dates)):
        adjoint = direct[t] + message
        adjoints.append(adjoint)
        message = rho[t][None, :] * adjoint
    return exposure_profile, jnp.stack(adjoints[::-1])


def solution(mesh):
    close = mesh.shape["date"] == 2 and mesh.shape["trade"] == 4 and mesh.shape["path"] == 2
    return jax.shard_map(
        near if close else far,
        mesh=mesh,
        in_specs=(
            P(("grp", "date"), "path", None),
            P(("grp", "date"), None),
            P(None, ("grp", "trade")),
            P(("grp", "trade")),
            P(("grp", "trade")),
            P(("grp", "trade")),
            P(("grp", "date"), "trade"),
        ),
        out_specs=(P(("grp", "date"), "trade"), P(("grp", "date"), "path", None)),
        check_vma=False,
    )
```
